256 devices in a mesh: sample: 64 (over z_lo, x, y), depth: 4 (over z_hi, core).
Axes of the slice: x: 4, y: 4, z: 8 (z_hi: 2, z_lo: 4; z = z_hi * 4 + z_lo), core: 2. Of those that a mesh axis runs over, the one named last changes fastest.
Arguments:
- volume: bfloat16 [64, 16, 8, 2048], P('sample', 'depth'), may hold values from -6 to 6
- kernels: bfloat16 [3, 27, 1024], replicated, may hold values from -0.21875 to 0.21875
- partner: int32 [64], replicated, may hold values from 0 to 63, each once
- cotangent: bfloat16 [64, 16, 8, 2048], P('sample', 'depth'), may hold values from -6 to 6
Outputs:
- grad_volume: bfloat16 [64, 16, 8, 2048], P('sample', 'depth')
- kernel_grads: float32 [64, 3, 27, 1024], P('sample')
The draws below stay inside these ranges and needn't reach their ends.
Inputs may be any that keep to these rules, and one draw needn't show every extreme that they name: partner is a permutation of the 64 crops: every crop is the partner of exactly one crop, and a crop may be its own partner.
All inputs are finite; a program needn't handle non-finite values.
Results may differ from the reference program's by a relative error of at most 0.014.
Values may be sent and summed in bfloat16 or wider, within the bound.
A program may use at most 64 MiB of HBM per device.

```python
import jax
import jax.numpy as jnp
from jax import lax

CH = 32
HEIGHT = 8
WIDTH = 64
LAYERS = 3
TAPS = 27
CROPS = 64
DEPTH = 16


def steps_of(key, dims, split, least, largest):
    factor_of, own = 1.0, jax.random.fold_in(key, 6)
    for dim, shards_of in split:
        draws = jnp.exp(jax.random.uniform(jax.random.fold_in(own, dim), (shards_of,), jnp.float32, least / len(split), largest / len(split)))
        factor_of = factor_of * jnp.repeat(draws, dims[dim] // shards_of).reshape([-1 if axis == dim else 1 for axis in range(len(dims))])
    return factor_of


def bell_draw(key, extent, spread, reach, cuts=(), held_as=jnp.bfloat16):
    entries = spread * jax.random.normal(key, extent, jnp.float32)
    if cuts:
        entries = entries * steps_of(key, extent, cuts, -0.22, 0.18)
    return jnp.clip(entries, -reach, reach).astype(held_as)


def setup_inputs(seed: int = 0) -> dict:
    keys = jax.random.split(jax.random.key(seed), 5)
    return {
        "volume": bell_draw(keys[0], (CROPS, DEPTH, HEIGHT, WIDTH * CH), 1.0, 6.0, ((0, 64), (1, 4))),
        "kernels": bell_draw(keys[1], (LAYERS, TAPS, CH * CH), (TAPS * CH) ** -0.5, 0.21875),
        "partner": jax.random.permutation(keys[2], CROPS).astype(jnp.int32),
        "cotangent": bell_draw(keys[3], (CROPS, DEPTH, HEIGHT, WIDTH * CH), 1.0, 6.0, ((0, 64), (1, 4))),
    }


OWN_SHARE = 0.6
PARTNER_SHARE = 0.4

def swish_value(values):
    return values * jax.nn.sigmoid(values)

def swish_slope(values):
    logistic = jax.nn.sigmoid(values)
    return logistic * (1.0 + values * (1.0 - logistic))

def rounded(values):
    return lax.optimization_barrier(values.astype(jnp.bfloat16)).astype(jnp.float32)

def conv_grid(values, kernel):
    weights = kernel.reshape(3, 3, 3, CH, CH)
    result = lax.conv_general_dilated(values[None], weights, (1, 1, 1), [(1, 1), (1, 1), (1, 1)], dimension_numbers=('NDHWC', 'DHWIO', 'NDHWC'), precision=lax.Precision.HIGHEST)
    return result[0]

def reference(volume, kernels, partner, cotangent):
    grid_shape = (DEPTH, HEIGHT, WIDTH, CH)
    weights = kernels.astype(jnp.float32)

    def first_layer(crop_cells):
        return swish_value(conv_grid(crop_cells.reshape(grid_shape).astype(jnp.float32), weights[0])).astype(jnp.bfloat16)
    hidden = lax.map(first_layer, volume)
    blended = (OWN_SHARE * hidden.astype(jnp.float32) + PARTNER_SHARE * hidden[partner].astype(jnp.float32)).astype(jnp.bfloat16)

    def middle_layers(crop_pair):
        blended_crop, cot_crop = crop_pair
        pre_two, pull_two = jax.vjp(conv_grid, blended_crop.astype(jnp.float32), weights[1])
        second = rounded(swish_value(pre_two))
        pre_three, pull_three = jax.vjp(conv_grid, second, weights[2])
        grad_three = rounded(cot_crop.reshape(grid_shape).astype(jnp.float32) * swish_slope(pre_three))
        grad_second, kernel_three = pull_three(grad_three)
        grad_two = rounded(grad_second * swish_slope(pre_two))
        grad_blended, kernel_two = pull_two(grad_two)
        return (grad_blended.astype(jnp.bfloat16), kernel_two, kernel_three)
    grad_blended, kernel_two, kernel_three = lax.map(middle_layers, (blended, cotangent))
    grad_partner = grad_blended[jnp.argsort(partner)]

    def first_backward(triple):
        crop_cells, own_grad, other_grad = triple
        pre_one, pull_one = jax.vjp(conv_grid, crop_cells.reshape(grid_shape).astype(jnp.float32), weights[0])
        grad_hidden = OWN_SHARE * own_grad.astype(jnp.float32) + PARTNER_SHARE * other_grad.astype(jnp.float32)
        grad_one = rounded(grad_hidden * swish_slope(pre_one))
        grad_crop, kernel_one = pull_one(grad_one)
        return (grad_crop.astype(jnp.bfloat16).reshape(DEPTH, HEIGHT, WIDTH * CH), kernel_one)
    grad_volume, kernel_one = lax.map(first_backward, (volume, grad_blended, grad_partner))
    kernel_grads = jnp.stack([kernel_one, kernel_two, kernel_three], axis=1)
    return (grad_volume, kernel_grads)
```

```python
import functools

import jax
import jax.numpy as jnp
from jax import lax
from jax.experimental import pallas as pl
from jax.experimental.pallas import tpu as pltpu
from jax.sharding import PartitionSpec as P

CH = 32
OWN_SHARE = 0.6
PARTNER_SHARE = 0.4
MESH = pl.DeviceIdType.MESH
F32 = jnp.float32
BF16 = jnp.bfloat16
ROWS = 256
LANES = 256
LAYER = 64
NT = (((1,), (1,)), ((), ()))
TN = (((0,), (0,)), ((), ()))


def logistic(v):
    return 0.5 * jnp.tanh(0.5 * v) + 0.5


def block_transpose(y):
    sub = lax.broadcasted_iota(jnp.int32, y.shape, 1) % 4
    blk = lax.broadcasted_iota(jnp.int32, y.shape, 2) // 32
    delta = sub - blk
    turned = [y] + [pltpu.roll(y, 128 - 32 * m, 2) for m in (1, 2, 3)]
    out = y
    for m in (1, 2, 3):
        out = jnp.where(delta == m, pltpu.roll(turned[m], m, 1), out)
        out = jnp.where(delta == m - 4, pltpu.roll(turned[m], m + 4, 1), out)
    return out


def to_rows(v):
    even = jnp.stack([v[:, 256 * t : 256 * t + 128] for t in range(8)])
    odd = jnp.stack([v[:, 256 * t + 128 : 256 * t + 256] for t in range(8)])
    first = lax.broadcasted_iota(jnp.int32, even.shape, 1) < 4
    y0 = jnp.where(first, even, pltpu.roll(odd, 4, 1))
    y1 = jnp.where(first, pltpu.roll(even, 4, 1), odd)
    return jnp.concatenate(
        [block_transpose(y0).reshape(64, 128), block_transpose(y1).reshape(64, 128)], axis=1
    )


def from_rows(r):
    y0 = block_transpose(r[:, :128].reshape(8, 8, 128))
    y1 = block_transpose(r[:, 128:].reshape(8, 8, 128))
    first = lax.broadcasted_iota(jnp.int32, y0.shape, 1) < 4
    even = jnp.where(first, y0, pltpu.roll(y1, 4, 1))
    odd = jnp.where(first, pltpu.roll(y0, 4, 1), y1)
    return jnp.concatenate([part[t] for t in range(8) for part in (even, odd)], axis=1)


def width_index(shape):
    return lax.broadcasted_iota(jnp.int32, shape, 0) % LAYER


def from_left(x):
    return jnp.where(width_index(x.shape) == 0, 0.0, pltpu.roll(x, 1, 0))


def from_right(x):
    return jnp.where(width_index(x.shape) == LAYER - 1, 0.0, pltpu.roll(x, x.shape[0] - 1, 0))


def kernel(
    crops,
    partner,
    inverse,
    vol,
    cot,
    kern,
    gvol,
    kg,
    kf,
    fwd_w,
    bwd_w,
    ext,
    cotr,
    slope1,
    slope2,
    part,
    pieces_out,
    pieces_in,
    mixed_out,
    mixed_in,
    kg_send,
    kg_recv,
    kg_pair,
    kg_all,
    halo_send,
    halo_recv,
    a2a_send,
    a2a_recv,
    pair_sems,
    all_send,
    all_recv,
):
    me = lax.axis_index("sample")
    d = lax.axis_index("depth")
    core = lax.rem(d, 2)
    mate = d + 1 - 2 * core
    far = lax.rem(d + 2, 4)
    far_mate = lax.rem(mate + 2, 4)

    barrier = pltpu.get_barrier_semaphore()

    @pl.loop(1, crops)
    def _(k):
        peer = lax.rem(me + k, crops)
        pl.semaphore_signal(barrier, inc=1, device_id=(peer, d), device_id_type=MESH)

    for k in (1, 2, 3):
        pl.semaphore_signal(
            barrier, inc=1, device_id=(me, lax.rem(d + k, 4)), device_id_type=MESH
        )

    for layer in range(4):
        ext[0, LAYER * (layer + 1) : LAYER * (layer + 2), :] = to_rows(
            vol[0, layer].astype(F32)
        ).astype(BF16)

    @pl.when(d == 0)
    def _():
        for k in range(6):
            ext[k, 0:LAYER, :] = jnp.zeros((LAYER, LANES), BF16)

    @pl.when(d == 3)
    def _():
        for k in range(6):
            ext[k, 5 * LAYER : 6 * LAYER, :] = jnp.zeros((LAYER, LANES), BF16)

    for l in range(3):
        kf[l] = kern[l].astype(F32)

    sub = lax.broadcasted_iota(jnp.int32, (8, 128), 0)
    blk8 = lax.broadcasted_iota(jnp.int32, (8, 128), 1) // 32
    blk32 = lax.broadcasted_iota(jnp.int32, (32, 128), 1) // 32

    def build(l):
        @pl.loop(0, 9)
        def _(ac):
            a = ac // 3
            c = lax.rem(ac, 3)
            taps = []
            for b in range(3):
                row = kf[l, pl.ds(9 * a + 3 * b + c, 1), :]
                tiles = []
                for r in range(4):
                    low = jnp.broadcast_to(row[:, 256 * r : 256 * r + 128], (8, 128))
                    high = jnp.broadcast_to(row[:, 256 * r + 128 : 256 * r + 256], (8, 128))
                    z = jnp.where(blk8 == sub % 4, jnp.where(sub < 4, low, high), 0.0)
                    z = z + pltpu.roll(z, 64, 1)
                    tiles.append(z + pltpu.roll(z, 32, 1))
                taps.append(jnp.concatenate(tiles, axis=0))
            row0 = pl.multiple_of(a * 256, 256)
            for hp in range(8):
                for j in range(2):
                    block = jnp.zeros((32, 128), F32)
                    for b in range(3):
                        h = hp - b + 1
                        if h // 4 == j and 0 <= h < 8:
                            block = jnp.where(blk32 == h % 4, taps[b], block)
                    block = block.astype(BF16)
                    rows = pl.ds(pl.multiple_of(row0 + 32 * hp, 32), 32)
                    fwd_w[l, c, rows, 128 * j : 128 * j + 128] = block
                    bwd_w[l, c, 32 * hp : 32 * hp + 32, pl.ds(pl.multiple_of(row0 + 128 * j, 128), 128)] = block

    def conv(x, l, starts, forward):
        if forward:
            order = (0, 1, 2)
        else:
            order = (2, 1, 0)
        lhs = jnp.concatenate(
            [
                jnp.concatenate(
                    [ext[x, LAYER * (s + a) : LAYER * (s + a + 1), :] for s in starts], axis=0
                )
                for a in order
            ],
            axis=1,
        )
        if forward:
            outs = [jnp.dot(lhs, fwd_w[l, c], preferred_element_type=F32) for c in range(3)]
            return outs[1] + from_left(outs[0]) + from_right(outs[2])
        outs = [
            lax.dot_general(lhs, bwd_w[l, c], NT, preferred_element_type=F32) for c in range(3)
        ]
        return outs[1] + from_right(outs[0]) + from_left(outs[2])

    def halo_copies(x):
        low = pltpu.make_async_remote_copy(
            src_ref=ext.at[x, pl.ds(LAYER, LAYER), :],
            dst_ref=ext.at[x, pl.ds(5 * LAYER, LAYER), :],
            send_sem=halo_send.at[x, 0],
            recv_sem=halo_recv.at[x, 1],
            device_id=(me, lax.rem(d + 3, 4)),
            device_id_type=MESH,
        )
        high = pltpu.make_async_remote_copy(
            src_ref=ext.at[x, pl.ds(4 * LAYER, LAYER), :],
            dst_ref=ext.at[x, pl.ds(0, LAYER), :],
            send_sem=halo_send.at[x, 1],
            recv_sem=halo_recv.at[x, 0],
            device_id=(me, lax.rem(d + 1, 4)),
            device_id_type=MESH,
        )
        return low, high

    def halo_start(x):
        low, high = halo_copies(x)

        @pl.when(d > 0)
        def _():
            low.start()

        @pl.when(d < 3)
        def _():
            high.start()

    def halo_wait(x):
        low, high = halo_copies(x)

        @pl.when(d > 0)
        def _():
            low.wait_send()
            high.wait_recv()

        @pl.when(d < 3)
        def _():
            high.wait_send()
            low.wait_recv()

    def fill_pieces(slot, values, rows_from):
        n = values.shape[0] // 8
        at = rows_from // 8
        for j in range(2):
            pieces_out[slot, 32 * j + at : 32 * j + at + n] = (
                values[:, 128 * j : 128 * j + 128].reshape(n, 8, 128).astype(BF16)
            )

    def scatter_start(slot, phase, source, target):
        @pl.loop(1, crops)
        def _(k):
            peer = lax.rem(me + k, crops)
            pltpu.make_async_remote_copy(
                src_ref=source.at[slot, peer],
                dst_ref=target.at[slot, me],
                send_sem=a2a_send.at[slot, phase],
                recv_sem=a2a_recv.at[slot, phase],
                device_id=(peer, d),
                device_id_type=MESH,
            ).start()

        target[slot, me] = source[slot, me]

    def scatter_wait(slot, phase, source, target):
        copy = pltpu.make_async_remote_copy(
            src_ref=source.at[slot, pl.ds(0, crops - 1)],
            dst_ref=target.at[slot, pl.ds(0, crops - 1)],
            send_sem=a2a_send.at[slot, phase],
            recv_sem=a2a_recv.at[slot, phase],
            device_id=(me, mate),
            device_id_type=MESH,
        )
        copy.wait()

    def joined(slot):
        whole = mixed_in[slot].astype(F32)
        return jnp.concatenate(
            [whole[0:32].reshape(ROWS, 128), whole[32:64].reshape(ROWS, 128)], axis=1
        )

    def kernel_grad(l, x, g):
        stacked = jnp.concatenate(
            [from_right(g).astype(BF16), g.astype(BF16), from_left(g).astype(BF16)], axis=1
        )
        for a in range(3):
            u = ext[x, LAYER * a : LAYER * a + ROWS, :]
            for c in range(3):
                r = lax.dot_general(
                    u, stacked[:, 256 * c : 256 * c + 256], TN, preferred_element_type=F32
                )

                def at(hp, j):
                    return r[32 * hp : 32 * hp + 32, 128 * j : 128 * j + 128]

                g0 = at(1, 0) + at(5, 1)
                g1 = at(2, 0) + at(6, 1)
                g2 = jnp.where(blk32 >= 2, at(3, 0) + at(7, 1), at(3, 1))
                g3 = jnp.where(blk32 == 3, at(4, 0), at(4, 1) + jnp.where(blk32 < 2, at(0, 0), 0.0))
                total = (
                    g0 + pltpu.roll(g1, 96, 1) + pltpu.roll(g2, 64, 1) + pltpu.roll(g3, 32, 1)
                )
                part[l, 0, 3 * a + c] = total[0:16]
                part[l, 1, 3 * a + c] = total[16:32]
        kg_send[l] = part[l, 1 - core].astype(BF16)

    def pair_copy(l):
        return pltpu.make_async_remote_copy(
            src_ref=kg_send.at[l],
            dst_ref=kg_recv.at[l],
            send_sem=pair_sems.at[l, 0],
            recv_sem=pair_sems.at[l, 1],
            device_id=(me, mate),
            device_id_type=MESH,
        )

    def all_copies(l):
        return [
            pltpu.make_async_remote_copy(
                src_ref=kg_pair.at[l],
                dst_ref=kg_all.at[l, k],
                send_sem=all_send.at[l, k],
                recv_sem=all_recv.at[l, k],
                device_id=(me, to),
                device_id_type=MESH,
            )
            for k, to in enumerate((mate, far, far_mate))
        ]

    def reduce_pairs(l):
        pair_copy(l).wait()
        kg_pair[l] = (part[l, core] + kg_recv[l].astype(F32)).astype(BF16)
        for copy in all_copies(l):
            copy.start()

    def reduce_finish(l):
        for copy in all_copies(l):
            copy.wait()
        own = kg_pair[l].astype(F32) + kg_all[l, 1].astype(F32)
        other = kg_all[l, 0].astype(F32) + kg_all[l, 2].astype(F32)
        kg[l, core] = own
        kg[l, 1 - core] = other

    build(0)
    pl.semaphore_wait(barrier, crops - 1 + 3)

    halo_start(0)
    inner, outer = (1, 2), (0, 3)

    def store_inner(ref, values):
        ref[LAYER : 3 * LAYER, :] = values

    def store_outer(ref, values):
        ref[0:LAYER, :] = values[0:LAYER]
        ref[3 * LAYER :, :] = values[LAYER:]

    def first_layer(starts):
        v = conv(0, 0, starts, True)
        s = logistic(v)
        hidden = v * s
        slope = s * (1.0 + v * (1.0 - s))
        if starts == inner:
            store_inner(slope1, slope)
            fill_pieces(0, hidden, LAYER)
        else:
            store_outer(slope1, slope)
            fill_pieces(0, hidden[0:LAYER], 0)
            fill_pieces(0, hidden[LAYER:], 3 * LAYER)

    first_layer(inner)
    build(1)
    halo_wait(0)
    first_layer(outer)

    scatter_start(0, 0, pieces_out, pieces_in)
    build(2)
    for layer in range(4):
        cotr[LAYER * layer : LAYER * (layer + 1), :] = to_rows(cot[0, layer].astype(F32)).astype(
            BF16
        )
    scatter_wait(0, 0, pieces_out, pieces_in)

    def blend(n, carry):
        own = pieces_in[0, n].astype(F32)
        other = pieces_in[0, partner[n]].astype(F32)
        mixed_out[0, n] = (OWN_SHARE * own + PARTNER_SHARE * other).astype(BF16)
        return carry

    lax.fori_loop(0, crops, blend, 0, unroll=8)
    scatter_start(0, 1, mixed_out, mixed_in)
    scatter_wait(0, 1, mixed_out, mixed_in)
    ext[1, LAYER : 5 * LAYER, :] = joined(0).astype(BF16)
    halo_start(1)

    def second_layer(starts):
        v = conv(1, 1, starts, True)
        s = logistic(v)
        second = (v * s).astype(BF16)
        slope = s * (1.0 + v * (1.0 - s))
        at = ext.at[2, pl.ds(LAYER, ROWS), :]
        if starts == inner:
            store_inner(slope2, slope)
            store_inner(at, second)
        else:
            store_outer(slope2, slope)
            store_outer(at, second)

    second_layer(inner)
    halo_wait(1)
    second_layer(outer)
    halo_start(2)

    def third_layer(starts):
        v = conv(2, 2, starts, True)
        s = logistic(v)
        slope = s * (1.0 + v * (1.0 - s))
        at = ext.at[3, pl.ds(LAYER, ROWS), :]
        if starts == inner:
            store_inner(at, (cotr[LAYER : 3 * LAYER, :].astype(F32) * slope).astype(BF16))
        else:
            facing = jnp.concatenate([cotr[0:LAYER, :], cotr[3 * LAYER :, :]], axis=0)
            store_outer(at, (facing.astype(F32) * slope).astype(BF16))

    third_layer(inner)
    halo_wait(2)
    third_layer(outer)
    halo_start(3)

    def back_three(starts):
        g = conv(3, 2, starts, False)
        at = ext.at[4, pl.ds(LAYER, ROWS), :]
        if starts == inner:
            store_inner(at, (g * slope2[LAYER : 3 * LAYER, :]).astype(BF16))
        else:
            facing = jnp.concatenate([slope2[0:LAYER, :], slope2[3 * LAYER :, :]], axis=0)
            store_outer(at, (g * facing).astype(BF16))

    back_three(inner)
    kernel_grad(2, 2, ext[3, LAYER : 5 * LAYER, :].astype(F32))
    halo_wait(3)
    back_three(outer)
    halo_start(4)
    pair_copy(2).start()

    g = conv(4, 1, inner, False)
    fill_pieces(1, g, LAYER)
    halo_wait(4)
    g = conv(4, 1, outer, False)
    fill_pieces(1, g[0:LAYER], 0)
    fill_pieces(1, g[LAYER:], 3 * LAYER)
    scatter_start(1, 0, pieces_out, pieces_in)
    reduce_pairs(2)
    kernel_grad(1, 1, ext[4, LAYER : 5 * LAYER, :].astype(F32))
    pair_copy(1).start()
    scatter_wait(1, 0, pieces_out, pieces_in)

    def blend_back(n, carry):
        own = pieces_in[1, n].astype(F32)
        other = pieces_in[1, inverse[n]].astype(F32)
        mixed_out[1, n] = (OWN_SHARE * own + PARTNER_SHARE * other).astype(BF16)
        return carry

    lax.fori_loop(0, crops, blend_back, 0, unroll=8)
    scatter_start(1, 1, mixed_out, mixed_in)
    reduce_pairs(1)
    reduce_finish(2)
    scatter_wait(1, 1, mixed_out, mixed_in)

    g_one = joined(1) * slope1[...]
    ext[5, LAYER : 5 * LAYER, :] = g_one.astype(BF16)
    halo_start(5)
    kernel_grad(0, 0, ext[5, LAYER : 5 * LAYER, :].astype(F32))
    pair_copy(0).start()
    g = conv(5, 0, inner, False)
    gvol[0, 1] = from_rows(g[0:LAYER]).astype(BF16)
    gvol[0, 2] = from_rows(g[LAYER:]).astype(BF16)
    reduce_pairs(0)
    halo_wait(5)
    g = conv(5, 0, outer, False)
    gvol[0, 0] = from_rows(g[0:LAYER]).astype(BF16)
    gvol[0, 3] = from_rows(g[LAYER:]).astype(BF16)
    reduce_finish(1)
    reduce_finish(0)


def per_device(crops, volume, kernels, partner, cotangent):
    order = jnp.arange(crops, dtype=jnp.int32)
    inverse = jnp.sum(
        jnp.where(partner[None, :] == order[:, None], order[None, :], 0), axis=1, dtype=jnp.int32
    )
    vmem = pl.BlockSpec(memory_space=pltpu.VMEM)
    smem = pl.BlockSpec(memory_space=pltpu.SMEM)
    dma = pltpu.SemaphoreType.DMA
    grad_volume, kg = pl.pallas_call(
        functools.partial(kernel, crops),
        out_shape=(
            jax.ShapeDtypeStruct((1, 4, 8, 2048), BF16),
            jax.ShapeDtypeStruct((3, 2, 9, 16, 128), F32),
        ),
        in_specs=[smem, smem, vmem, vmem, vmem],
        out_specs=(vmem, vmem),
        scratch_shapes=[
            pltpu.VMEM((3, 27, 1024), F32),
            pltpu.VMEM((3, 3, 768, 256), BF16),
            pltpu.VMEM((3, 3, 256, 768), BF16),
            pltpu.VMEM((6, 384, 256), BF16),
            pltpu.VMEM((256, 256), BF16),
            pltpu.VMEM((256, 256), F32),
            pltpu.VMEM((256, 256), F32),
            pltpu.VMEM((3, 2, 9, 16, 128), F32),
            pltpu.VMEM((2, crops, 8, 128), BF16),
            pltpu.VMEM((2, crops, 8, 128), BF16),
            pltpu.VMEM((2, crops, 8, 128), BF16),
            pltpu.VMEM((2, crops, 8, 128), BF16),
            pltpu.VMEM((3, 9, 16, 128), BF16),
            pltpu.VMEM((3, 9, 16, 128), BF16),
            pltpu.VMEM((3, 9, 16, 128), BF16),
            pltpu.VMEM((3, 3, 9, 16, 128), BF16),
            dma((6, 2)),
            dma((6, 2)),
            dma((2, 2)),
            dma((2, 2)),
            dma((3, 2)),
            dma((3, 3)),
            dma((3, 3)),
        ],
        compiler_params=pltpu.CompilerParams(
            collective_id=0, has_side_effects=True, vmem_limit_bytes=48 * 1024 * 1024
        ),
    )(partner, inverse, volume, cotangent, kernels)
    kg = kg[..., :96].reshape(3, 2, 3, 3, 16, 3, CH)[:, :, :, :, :, ::-1]
    kg = jnp.transpose(kg, (0, 2, 5, 3, 1, 4, 6)).reshape(1, 3, 27, CH * CH)
    return grad_volume, kg


def solution(mesh):
    crops = mesh.shape["sample"]
    in_specs = (P("sample", "depth", None, None), P(), P(), P("sample", "depth", None, None))
    out_specs = (P("sample", "depth", None, None), P("sample", None, None, None))
    return jax.shard_map(
        functools.partial(per_device, crops),
        mesh=mesh,
        in_specs=in_specs,
        out_specs=out_specs,
        check_vma=False,
    )
```

```python
import functools

import jax
import jax.numpy as jnp
from jax import lax
from jax.experimental import pallas as pl
from jax.experimental.pallas import tpu as pltpu
from jax.sharding import PartitionSpec as P

CH = 32
OWN_SHARE = 0.6
PARTNER_SHARE = 0.4
MESH = pl.DeviceIdType.MESH
F32 = jnp.float32
BF16 = jnp.bfloat16
ROWS = 256
LANES = 256
LAYER = 64
NT = (((1,), (1,)), ((), ()))
TN = (((0,), (0,)), ((), ()))


def logistic(v):
    return 0.5 * jnp.tanh(0.5 * v) + 0.5


def block_transpose(y):
    sub = lax.broadcasted_iota(jnp.int32, y.shape, 1) % 4
    blk = lax.broadcasted_iota(jnp.int32, y.shape, 2) // 32
    delta = sub - blk
    turned = [y] + [pltpu.roll(y, 128 - 32 * m, 2) for m in (1, 2, 3)]
    out = y
    for m in (1, 2, 3):
        out = jnp.where(delta == m, pltpu.roll(turned[m], m, 1), out)
        out = jnp.where(delta == m - 4, pltpu.roll(turned[m], m + 4, 1), out)
    return out


def to_rows(v):
    even = jnp.stack([v[:, 256 * t : 256 * t + 128] for t in range(8)])
    odd = jnp.stack([v[:, 256 * t + 128 : 256 * t + 256] for t in range(8)])
    first = lax.broadcasted_iota(jnp.int32, even.shape, 1) < 4
    y0 = jnp.where(first, even, pltpu.roll(odd, 4, 1))
    y1 = jnp.where(first, pltpu.roll(even, 4, 1), odd)
    return jnp.concatenate(
        [block_transpose(y0).reshape(64, 128), block_transpose(y1).reshape(64, 128)], axis=1
    )


def from_rows(r):
    y0 = block_transpose(r[:, :128].reshape(8, 8, 128))
    y1 = block_transpose(r[:, 128:].reshape(8, 8, 128))
    first = lax.broadcasted_iota(jnp.int32, y0.shape, 1) < 4
    even = jnp.where(first, y0, pltpu.roll(y1, 4, 1))
    odd = jnp.where(first, pltpu.roll(y0, 4, 1), y1)
    return jnp.concatenate([part[t] for t in range(8) for part in (even, odd)], axis=1)


def width_index(shape):
    return lax.broadcasted_iota(jnp.int32, shape, 0) % LAYER


def from_left(x):
    return jnp.where(width_index(x.shape) == 0, 0.0, pltpu.roll(x, 1, 0))


def from_right(x):
    return jnp.where(width_index(x.shape) == LAYER - 1, 0.0, pltpu.roll(x, x.shape[0] - 1, 0))


def kernel(
    crops,
    partner_hbm,
    vol_hbm,
    cot_hbm,
    kern_hbm,
    gvol,
    kg,
    partner,
    partner_row,
    inverse_rows,
    inverse,
    vol,
    cot,
    kern,
    kf,
    fwd_w,
    bwd_w,
    ext,
    cotr,
    slope1,
    slope2,
    part,
    pieces_out,
    pieces_in,
    mixed_out,
    mixed_in,
    kg_send,
    kg_recv,
    kg_pair,
    kg_all,
    halo_send,
    halo_recv,
    a2a_send,
    a2a_recv,
    pair_sems,
    all_send,
    all_recv,
    load_sems,
):
    loads = [
        pltpu.make_async_copy(source, target, load_sems.at[k])
        for k, (source, target) in enumerate(
            (
                (vol_hbm, vol),
                (kern_hbm, kern),
                (partner_hbm, partner_row),
                (partner_hbm, partner),
                (cot_hbm, cot),
            )
        )
    ]
    turn = pltpu.make_async_copy(inverse_rows, inverse, load_sems.at[5])
    for load in loads:
        load.start()
    me = lax.axis_index("sample")
    d = lax.axis_index("depth")
    core = lax.rem(d, 2)
    mate = d + 1 - 2 * core
    far = lax.rem(d + 2, 4)
    far_mate = lax.rem(mate + 2, 4)

    barrier = pltpu.get_barrier_semaphore()

    @pl.loop(1, crops)
    def _(k):
        peer = lax.rem(me + k, crops)
        pl.semaphore_signal(barrier, inc=1, device_id=(peer, d), device_id_type=MESH)

    for k in (1, 2, 3):
        pl.semaphore_signal(
            barrier, inc=1, device_id=(me, lax.rem(d + k, 4)), device_id_type=MESH
        )

    loads[0].wait()
    for layer in range(4):
        ext[0, LAYER * (layer + 1) : LAYER * (layer + 2), :] = to_rows(
            vol[0, layer].astype(F32)
        ).astype(BF16)

    @pl.when(d == 0)
    def _():
        for k in range(6):
            ext[k, 0:LAYER, :] = jnp.zeros((LAYER, LANES), BF16)

    @pl.when(d == 3)
    def _():
        for k in range(6):
            ext[k, 5 * LAYER : 6 * LAYER, :] = jnp.zeros((LAYER, LANES), BF16)

    loads[1].wait()
    for l in range(3):
        kf[l] = kern[l].astype(F32)

    sub = lax.broadcasted_iota(jnp.int32, (8, 128), 0)
    blk8 = lax.broadcasted_iota(jnp.int32, (8, 128), 1) // 32
    sub32 = lax.broadcasted_iota(jnp.int32, (32, 128), 0) % 4
    blk32 = lax.broadcasted_iota(jnp.int32, (32, 128), 1) // 32

    diagonal = [(sub32 == q) & (blk32 == q) for q in range(4)]

    def build(l):
        @pl.loop(0, 9)
        def _(ac):
            a = ac // 3
            c = lax.rem(ac, 3)
            taps = []
            for b in range(3):
                row = kf[l, pl.ds(9 * a + 3 * b + c, 1), :]
                tiles = []
                for r in range(4):
                    low = jnp.broadcast_to(row[:, 256 * r : 256 * r + 128], (8, 128))
                    high = jnp.broadcast_to(row[:, 256 * r + 128 : 256 * r + 256], (8, 128))
                    z = jnp.where(blk8 == sub % 4, jnp.where(sub < 4, low, high), 0.0)
                    z = z + pltpu.roll(z, 64, 1)
                    tiles.append(z + pltpu.roll(z, 32, 1))
                taps.append(jnp.concatenate(tiles, axis=0))
            row0 = pl.multiple_of(a * 256, 256)
            for hp in range(8):
                for j in range(2):
                    block = jnp.zeros((32, 128), F32)
                    for b in range(3):
                        h = hp - b + 1
                        if h // 4 == j and 0 <= h < 8:
                            block = jnp.where(blk32 == h % 4, taps[b], block)
                    block = block.astype(BF16)
                    rows = pl.ds(pl.multiple_of(row0 + 32 * hp, 32), 32)
                    fwd_w[l, c, rows, 128 * j : 128 * j + 128] = block
                    bwd_w[l, c, 32 * hp : 32 * hp + 32, pl.ds(pl.multiple_of(row0 + 128 * j, 128), 128)] = block

    def conv(x, l, starts, forward):
        if forward:
            order = (0, 1, 2)
        else:
            order = (2, 1, 0)
        lhs = jnp.concatenate(
            [
                jnp.concatenate(
                    [ext[x, LAYER * (s + a) : LAYER * (s + a + 1), :] for s in starts], axis=0
                )
                for a in order
            ],
            axis=1,
        )
        if forward:
            outs = [jnp.dot(lhs, fwd_w[l, c], preferred_element_type=F32) for c in range(3)]
            return outs[1] + from_left(outs[0]) + from_right(outs[2])
        outs = [
            lax.dot_general(lhs, bwd_w[l, c], NT, preferred_element_type=F32) for c in range(3)
        ]
        return outs[1] + from_right(outs[0]) + from_left(outs[2])

    def halo_copies(x):
        low = pltpu.make_async_remote_copy(
            src_ref=ext.at[x, pl.ds(LAYER, LAYER), :],
            dst_ref=ext.at[x, pl.ds(5 * LAYER, LAYER), :],
            send_sem=halo_send.at[x, 0],
            recv_sem=halo_recv.at[x, 1],
            device_id=(me, lax.rem(d + 3, 4)),
            device_id_type=MESH,
        )
        high = pltpu.make_async_remote_copy(
            src_ref=ext.at[x, pl.ds(4 * LAYER, LAYER), :],
            dst_ref=ext.at[x, pl.ds(0, LAYER), :],
            send_sem=halo_send.at[x, 1],
            recv_sem=halo_recv.at[x, 0],
            device_id=(me, lax.rem(d + 1, 4)),
            device_id_type=MESH,
        )
        return low, high

    def halo_start(x):
        low, high = halo_copies(x)

        @pl.when(d > 0)
        def _():
            low.start()

        @pl.when(d < 3)
        def _():
            high.start()

    def halo_wait(x):
        low, high = halo_copies(x)

        @pl.when(d > 0)
        def _():
            low.wait_send()
            high.wait_recv()

        @pl.when(d < 3)
        def _():
            high.wait_send()
            low.wait_recv()

    def fill_pieces(slot, values, rows_from):
        n = values.shape[0] // 8
        at = rows_from // 8
        for j in range(2):
            pieces_out[slot, 32 * j + at : 32 * j + at + n] = (
                values[:, 128 * j : 128 * j + 128].reshape(n, 8, 128).astype(BF16)
            )

    def scatter_start(slot, phase, source, target):
        @pl.loop(1, crops)
        def _(k):
            peer = lax.rem(me + k, crops)
            pltpu.make_async_remote_copy(
                src_ref=source.at[slot, peer],
                dst_ref=target.at[slot, me],
                send_sem=a2a_send.at[slot, phase],
                recv_sem=a2a_recv.at[slot, phase],
                device_id=(peer, d),
                device_id_type=MESH,
            ).start()

        target[slot, me] = source[slot, me]

    def scatter_wait(slot, phase, source, target):
        copy = pltpu.make_async_remote_copy(
            src_ref=source.at[slot, pl.ds(0, crops - 1)],
            dst_ref=target.at[slot, pl.ds(0, crops - 1)],
            send_sem=a2a_send.at[slot, phase],
            recv_sem=a2a_recv.at[slot, phase],
            device_id=(me, mate),
            device_id_type=MESH,
        )
        copy.wait()

    def joined(slot):
        whole = mixed_in[slot].astype(F32)
        return jnp.concatenate(
            [whole[0:32].reshape(ROWS, 128), whole[32:64].reshape(ROWS, 128)], axis=1
        )

    def kernel_grad(l, x, g):
        stacked = jnp.concatenate(
            [from_right(g).astype(BF16), g.astype(BF16), from_left(g).astype(BF16)], axis=1
        )
        for a in range(3):
            u = ext[x, LAYER * a : LAYER * a + ROWS, :]
            for c in range(3):
                r = lax.dot_general(
                    u, stacked[:, 256 * c : 256 * c + 256], TN, preferred_element_type=F32
                )

                def at(hp, j):
                    return r[32 * hp : 32 * hp + 32, 128 * j : 128 * j + 128]

                g0 = at(1, 0) + at(5, 1)
                g1 = at(2, 0) + at(6, 1)
                g2 = jnp.where(blk32 >= 2, at(3, 0) + at(7, 1), at(3, 1))
                g3 = jnp.where(blk32 == 3, at(4, 0), at(4, 1) + jnp.where(blk32 < 2, at(0, 0), 0.0))
                total = (
                    g0 + pltpu.roll(g1, 96, 1) + pltpu.roll(g2, 64, 1) + pltpu.roll(g3, 32, 1)
                )
                part[l, 0, 3 * a + c] = total[0:16]
                part[l, 1, 3 * a + c] = total[16:32]
        kg_send[l] = part[l, 1 - core].astype(BF16)

    def pair_copy(l):
        return pltpu.make_async_remote_copy(
            src_ref=kg_send.at[l],
            dst_ref=kg_recv.at[l],
            send_sem=pair_sems.at[l, 0],
            recv_sem=pair_sems.at[l, 1],
            device_id=(me, mate),
            device_id_type=MESH,
        )

    def all_copies(l):
        return [
            pltpu.make_async_remote_copy(
                src_ref=kg_pair.at[l],
                dst_ref=kg_all.at[l, k],
                send_sem=all_send.at[l, k],
                recv_sem=all_recv.at[l, k],
                device_id=(me, to),
                device_id_type=MESH,
            )
            for k, to in enumerate((mate, far, far_mate))
        ]

    def reduce_pairs(l):
        pair_copy(l).wait()
        kg_pair[l] = (part[l, core] + kg_recv[l].astype(F32)).astype(BF16)
        for copy in all_copies(l):
            copy.start()

    def reduce_finish(l):
        for copy in all_copies(l):
            copy.wait()
        own = kg_pair[l].astype(F32) + kg_all[l, 1].astype(F32)
        other = kg_all[l, 0].astype(F32) + kg_all[l, 2].astype(F32)
        for a in range(3):
            for c in range(3):
                k = 3 * a + c
                x = jnp.concatenate(
                    [
                        jnp.where(core == 0, own[k], other[k]),
                        jnp.where(core == 0, other[k], own[k]),
                    ],
                    axis=0,
                )
                turned = [x] + [pltpu.roll(x, 32 * m, 1) for m in (1, 2, 3)]
                for b in range(3):
                    z = jnp.zeros_like(x)
                    for q in range(4):
                        z = jnp.where(diagonal[q], turned[(q - 2 + b) % 4], z)
                    z = z.reshape(4, 8, 128)
                    z = z + pltpu.roll(z, 7, 1)
                    z = z + pltpu.roll(z, 6, 1)
                    t = 27 * l + 9 * a + 3 * b + c
                    for r in range(4):
                        kg[t, 2 * r : 2 * r + 1, :] = z[r, 0:1, :]
                        kg[t, 2 * r + 1 : 2 * r + 2, :] = z[r, 4:5, :]

    build(0)
    for load in loads[2:]:
        load.wait()
    shape = (crops, crops)
    named = partner_row[...] == lax.broadcasted_iota(jnp.int32, shape, 0)
    found = jnp.where(named, lax.broadcasted_iota(jnp.int32, shape, 1), 0)
    inverse_rows[...] = jnp.broadcast_to(
        jnp.minimum(jnp.sum(found, axis=1, keepdims=True, dtype=jnp.int32), crops - 1),
        (crops, 128),
    )
    turn.start()
    pl.semaphore_wait(barrier, crops - 1 + 3)

    halo_start(0)
    inner, outer = (1, 2), (0, 3)

    def store_inner(ref, values):
        ref[LAYER : 3 * LAYER, :] = values

    def store_outer(ref, values):
        ref[0:LAYER, :] = values[0:LAYER]
        ref[3 * LAYER :, :] = values[LAYER:]

    def first_layer(starts):
        v = conv(0, 0, starts, True)
        s = logistic(v)
        hidden = v * s
        slope = s * (1.0 + v * (1.0 - s))
        if starts == inner:
            store_inner(slope1, slope)
            fill_pieces(0, hidden, LAYER)
        else:
            store_outer(slope1, slope)
            fill_pieces(0, hidden[0:LAYER], 0)
            fill_pieces(0, hidden[LAYER:], 3 * LAYER)

    first_layer(inner)
    build(1)
    halo_wait(0)
    first_layer(outer)

    scatter_start(0, 0, pieces_out, pieces_in)
    build(2)
    for layer in range(4):
        cotr[LAYER * layer : LAYER * (layer + 1), :] = to_rows(cot[0, layer].astype(F32)).astype(
            BF16
        )
    scatter_wait(0, 0, pieces_out, pieces_in)

    def blend(n, carry):
        own = pieces_in[0, n].astype(F32)
        other = pieces_in[0, partner[0, n]].astype(F32)
        mixed_out[0, n] = (OWN_SHARE * own + PARTNER_SHARE * other).astype(BF16)
        return carry

    lax.fori_loop(0, crops, blend, 0, unroll=8)
    scatter_start(0, 1, mixed_out, mixed_in)
    scatter_wait(0, 1, mixed_out, mixed_in)
    ext[1, LAYER : 5 * LAYER, :] = joined(0).astype(BF16)
    halo_start(1)

    def second_layer(starts):
        v = conv(1, 1, starts, True)
        s = logistic(v)
        second = (v * s).astype(BF16)
        slope = s * (1.0 + v * (1.0 - s))
        at = ext.at[2, pl.ds(LAYER, ROWS), :]
        if starts == inner:
            store_inner(slope2, slope)
            store_inner(at, second)
        else:
            store_outer(slope2, slope)
            store_outer(at, second)

    second_layer(inner)
    halo_wait(1)
    second_layer(outer)
    halo_start(2)

    def third_layer(starts):
        v = conv(2, 2, starts, True)
        s = logistic(v)
        slope = s * (1.0 + v * (1.0 - s))
        at = ext.at[3, pl.ds(LAYER, ROWS), :]
        if starts == inner:
            store_inner(at, (cotr[LAYER : 3 * LAYER, :].astype(F32) * slope).astype(BF16))
        else:
            facing = jnp.concatenate([cotr[0:LAYER, :], cotr[3 * LAYER :, :]], axis=0)
            store_outer(at, (facing.astype(F32) * slope).astype(BF16))

    third_layer(inner)
    halo_wait(2)
    third_layer(outer)
    halo_start(3)

    def back_three(starts):
        g = conv(3, 2, starts, False)
        at = ext.at[4, pl.ds(LAYER, ROWS), :]
        if starts == inner:
            store_inner(at, (g * slope2[LAYER : 3 * LAYER, :]).astype(BF16))
        else:
            facing = jnp.concatenate([slope2[0:LAYER, :], slope2[3 * LAYER :, :]], axis=0)
            store_outer(at, (g * facing).astype(BF16))

    back_three(inner)
    kernel_grad(2, 2, ext[3, LAYER : 5 * LAYER, :].astype(F32))
    halo_wait(3)
    back_three(outer)
    halo_start(4)
    pair_copy(2).start()

    g = conv(4, 1, inner, False)
    fill_pieces(1, g, LAYER)
    halo_wait(4)
    g = conv(4, 1, outer, False)
    fill_pieces(1, g[0:LAYER], 0)
    fill_pieces(1, g[LAYER:], 3 * LAYER)
    scatter_start(1, 0, pieces_out, pieces_in)
    reduce_pairs(2)
    kernel_grad(1, 1, ext[4, LAYER : 5 * LAYER, :].astype(F32))
    pair_copy(1).start()
    scatter_wait(1, 0, pieces_out, pieces_in)

    turn.wait()

    def blend_back(n, carry):
        own = pieces_in[1, n].astype(F32)
        other = pieces_in[1, inverse[n, 0]].astype(F32)
        mixed_out[1, n] = (OWN_SHARE * own + PARTNER_SHARE * other).astype(BF16)
        return carry

    lax.fori_loop(0, crops, blend_back, 0, unroll=8)
    scatter_start(1, 1, mixed_out, mixed_in)
    reduce_pairs(1)
    reduce_finish(2)
    scatter_wait(1, 1, mixed_out, mixed_in)

    g_one = joined(1) * slope1[...]
    ext[5, LAYER : 5 * LAYER, :] = g_one.astype(BF16)
    halo_start(5)
    kernel_grad(0, 0, ext[5, LAYER : 5 * LAYER, :].astype(F32))
    pair_copy(0).start()
    g = conv(5, 0, inner, False)
    gvol[0, 1] = from_rows(g[0:LAYER]).astype(BF16)
    gvol[0, 2] = from_rows(g[LAYER:]).astype(BF16)
    reduce_pairs(0)
    halo_wait(5)
    g = conv(5, 0, outer, False)
    gvol[0, 0] = from_rows(g[0:LAYER]).astype(BF16)
    gvol[0, 3] = from_rows(g[LAYER:]).astype(BF16)
    reduce_finish(1)
    reduce_finish(0)


def per_device(crops, volume, kernels, partner, cotangent):
    vmem = pl.BlockSpec(memory_space=pltpu.VMEM)
    hbm = pl.BlockSpec(memory_space=pltpu.HBM)
    dma = pltpu.SemaphoreType.DMA
    grad_volume, kg = pl.pallas_call(
        functools.partial(kernel, crops),
        out_shape=(
            jax.ShapeDtypeStruct((1, 4, 8, 2048), BF16),
            jax.ShapeDtypeStruct((81, 8, 128), F32),
        ),
        in_specs=[hbm] * 4,
        out_specs=(vmem, vmem),
        scratch_shapes=[
            pltpu.SMEM((1, crops), jnp.int32),
            pltpu.VMEM((1, crops), jnp.int32),
            pltpu.VMEM((crops, 128), jnp.int32),
            pltpu.SMEM((crops, 128), jnp.int32),
            pltpu.VMEM((1, 4, 8, 2048), BF16),
            pltpu.VMEM((1, 4, 8, 2048), BF16),
            pltpu.VMEM((3, 27, 1024), BF16),
            pltpu.VMEM((3, 27, 1024), F32),
            pltpu.VMEM((3, 3, 768, 256), BF16),
            pltpu.VMEM((3, 3, 256, 768), BF16),
            pltpu.VMEM((6, 384, 256), BF16),
            pltpu.VMEM((256, 256), BF16),
            pltpu.VMEM((256, 256), F32),
            pltpu.VMEM((256, 256), F32),
            pltpu.VMEM((3, 2, 9, 16, 128), F32),
            pltpu.VMEM((2, crops, 8, 128), BF16),
            pltpu.VMEM((2, crops, 8, 128), BF16),
            pltpu.VMEM((2, crops, 8, 128), BF16),
            pltpu.VMEM((2, crops, 8, 128), BF16),
            pltpu.VMEM((3, 9, 16, 128), BF16),
            pltpu.VMEM((3, 9, 16, 128), BF16),
            pltpu.VMEM((3, 9, 16, 128), BF16),
            pltpu.VMEM((3, 3, 9, 16, 128), BF16),
            dma((6, 2)),
            dma((6, 2)),
            dma((2, 2)),
            dma((2, 2)),
            dma((3, 2)),
            dma((3, 3)),
            dma((3, 3)),
            dma((6,)),
        ],
        compiler_params=pltpu.CompilerParams(
            collective_id=0, has_side_effects=True, vmem_limit_bytes=48 * 1024 * 1024
        ),
    )(*(pltpu.with_memory_space_constraint(x, pltpu.HBM) for x in (partner[None, :], volume, cotangent, kernels)))
    return grad_volume, kg.reshape(1, 3, 27, CH * CH)


def solution(mesh):
    crops = mesh.shape["sample"]
    in_specs = (P("sample", "depth", None, None), P(), P(), P("sample", "depth", None, None))
    out_specs = (P("sample", "depth", None, None), P("sample", None, None, None))
    return jax.shard_map(
        functools.partial(per_device, crops),
        mesh=mesh,
        in_specs=in_specs,
        out_specs=out_specs,
        check_vma=False,
    )
```

```python
import functools

import jax
import jax.numpy as jnp
from jax import lax
from jax.experimental import pallas as pl
from jax.experimental.pallas import tpu as pltpu
from jax.sharding import PartitionSpec as P

CH = 32
OWN_SHARE = 0.6
PARTNER_SHARE = 0.4
MESH = pl.DeviceIdType.MESH
F32 = jnp.float32
BF16 = jnp.bfloat16
ROWS = 256
LANES = 256
LAYER = 64
NT = (((1,), (1,)), ((), ()))
TN = (((0,), (0,)), ((), ()))


def logistic(v):
    return 0.5 * jnp.tanh(0.5 * v) + 0.5


def block_transpose(y):
    sub = lax.broadcasted_iota(jnp.int32, y.shape, 1) % 4
    blk = lax.broadcasted_iota(jnp.int32, y.shape, 2) // 32
    delta = sub - blk
    turned = [y] + [pltpu.roll(y, 128 - 32 * m, 2) for m in (1, 2, 3)]
    out = y
    for m in (1, 2, 3):
        out = jnp.where(delta == m, pltpu.roll(turned[m], m, 1), out)
        out = jnp.where(delta == m - 4, pltpu.roll(turned[m], m + 4, 1), out)
    return out


def to_rows(v):
    even = jnp.stack([v[:, 256 * t : 256 * t + 128] for t in range(8)])
    odd = jnp.stack([v[:, 256 * t + 128 : 256 * t + 256] for t in range(8)])
    first = lax.broadcasted_iota(jnp.int32, even.shape, 1) < 4
    y0 = jnp.where(first, even, pltpu.roll(odd, 4, 1))
    y1 = jnp.where(first, pltpu.roll(even, 4, 1), odd)
    return jnp.concatenate(
        [block_transpose(y0).reshape(64, 128), block_transpose(y1).reshape(64, 128)], axis=1
    )


def from_rows(r):
    y0 = block_transpose(r[:, :128].reshape(8, 8, 128))
    y1 = block_transpose(r[:, 128:].reshape(8, 8, 128))
    first = lax.broadcasted_iota(jnp.int32, y0.shape, 1) < 4
    even = jnp.where(first, y0, pltpu.roll(y1, 4, 1))
    odd = jnp.where(first, pltpu.roll(y0, 4, 1), y1)
    return jnp.concatenate([part[t] for t in range(8) for part in (even, odd)], axis=1)


def width_index(shape):
    return lax.broadcasted_iota(jnp.int32, shape, 0) % LAYER


def from_left(x):
    return jnp.where(width_index(x.shape) == 0, 0.0, pltpu.roll(x, 1, 0))


def from_right(x):
    return jnp.where(width_index(x.shape) == LAYER - 1, 0.0, pltpu.roll(x, x.shape[0] - 1, 0))


def kernel(
    crops,
    partner_hbm,
    vol_hbm,
    cot_hbm,
    kern_hbm,
    gvol,
    kg,
    partner,
    partner_row,
    inverse_rows,
    inverse,
    vol,
    cot,
    kern,
    kf,
    fwd_w,
    bwd_w,
    ext,
    wide,
    slope1,
    slope2,
    part,
    pieces_out,
    pieces_in,
    mixed_out,
    mixed_in,
    far_in,
    near_in,
    kg_send,
    kg_recv,
    kg_pair,
    kg_all,
    halo_send,
    halo_recv,
    cot_send,
    cot_recv,
    far_sems,
    near_sems,
    a2a_send,
    a2a_recv,
    pair_sems,
    all_send,
    all_recv,
    load_sems,
):
    loads = [
        pltpu.make_async_copy(source, target, load_sems.at[k])
        for k, (source, target) in enumerate(
            (
                (vol_hbm, vol),
                (kern_hbm, kern),
                (partner_hbm, partner_row),
                (partner_hbm, partner),
                (cot_hbm, cot),
            )
        )
    ]
    turn = pltpu.make_async_copy(inverse_rows, inverse, load_sems.at[5])
    for load in loads:
        load.start()
    me = lax.axis_index("sample")
    d = lax.axis_index("depth")
    core = lax.rem(d, 2)
    mate = d + 1 - 2 * core
    far = lax.rem(d + 2, 4)
    far_mate = lax.rem(mate + 2, 4)

    barrier = pltpu.get_barrier_semaphore()

    @pl.loop(1, crops)
    def _(k):
        peer = lax.rem(me + k, crops)
        pl.semaphore_signal(barrier, inc=1, device_id=(peer, d), device_id_type=MESH)

    for k in (1, 2, 3):
        pl.semaphore_signal(
            barrier, inc=1, device_id=(me, lax.rem(d + k, 4)), device_id_type=MESH
        )

    middle = (d == 1) | (d == 2)

    @pl.when(middle)
    def _():
        @pl.loop(1, crops)
        def _(k):
            peer = lax.rem(me + k, crops)
            pl.semaphore_signal(barrier, inc=1, device_id=(peer, 3 - d), device_id_type=MESH)

    loads[0].wait()
    for layer in range(4):
        ext[0, LAYER * (layer + 1) : LAYER * (layer + 2), :] = to_rows(
            vol[0, layer].astype(F32)
        ).astype(BF16)

    @pl.when(d == 0)
    def _():
        for k in range(2):
            ext[k, 0:LAYER, :] = jnp.zeros((LAYER, LANES), BF16)
        wide[0, 0 : 4 * LAYER, :] = jnp.zeros((4 * LAYER, LANES), BF16)

    @pl.when(d == 3)
    def _():
        for k in range(2):
            ext[k, 5 * LAYER : 6 * LAYER, :] = jnp.zeros((LAYER, LANES), BF16)
        wide[0, 8 * LAYER : 12 * LAYER, :] = jnp.zeros((4 * LAYER, LANES), BF16)

    loads[1].wait()
    for l in range(3):
        kf[l] = kern[l].astype(F32)

    sub = lax.broadcasted_iota(jnp.int32, (8, 128), 0)
    blk8 = lax.broadcasted_iota(jnp.int32, (8, 128), 1) // 32
    sub32 = lax.broadcasted_iota(jnp.int32, (32, 128), 0) % 4
    blk32 = lax.broadcasted_iota(jnp.int32, (32, 128), 1) // 32

    first_rows = (
        lax.broadcasted_iota(jnp.int32, (32, 128), 0) == lax.broadcasted_iota(jnp.int32, (32, 128), 1)
    ).astype(F32).astype(BF16)
    diagonal = [(sub32 == q) & (blk32 == q) for q in range(4)]

    def tap_tiles(l, a, c):
        taps = []
        for b in range(3):
            row = kf[l, pl.ds(9 * a + 3 * b + c, 1), :]
            tiles = []
            for r in range(4):
                low = jnp.broadcast_to(row[:, 256 * r : 256 * r + 128], (8, 128))
                high = jnp.broadcast_to(row[:, 256 * r + 128 : 256 * r + 256], (8, 128))
                z = jnp.where(blk8 == sub % 4, jnp.where(sub < 4, low, high), 0.0)
                z = z + pltpu.roll(z, 64, 1)
                tiles.append(z + pltpu.roll(z, 32, 1))
            taps.append(jnp.concatenate(tiles, axis=0))
        return taps

    def store_blocks(target, l, a, c, taps, step):
        row0 = pl.multiple_of(a * 256, 256)
        for hp in range(8):
            for j in range(2):
                block = jnp.zeros((32, 128), F32)
                for b in range(3):
                    h = hp + step * (b - 1)
                    if h // 4 == j and 0 <= h < 8:
                        block = jnp.where(blk32 == h % 4, taps[b], block)
                rows = pl.ds(pl.multiple_of(row0 + 32 * hp, 32), 32)
                target[l, c, rows, 128 * j : 128 * j + 128] = block.astype(BF16)

    def build(l, forward, backward):
        @pl.loop(0, 3)
        def _(a):
            for c in range(3):
                taps = tap_tiles(l, a, c)
                if forward:
                    store_blocks(fwd_w, l, a, c, taps, -1)
                if backward:
                    stacked = jnp.concatenate([tap for tap in taps for _ in range(4)], axis=0)
                    back = lax.dot_general(
                        first_rows, stacked.astype(BF16), NT, preferred_element_type=F32
                    )
                    store_blocks(
                        bwd_w, l, a, c, [back[:, 128 * b : 128 * b + 128] for b in range(3)], 1
                    )

    def conv(x, l, ranges, forward):
        lhs = []
        for a in range(3):
            shift = a - 1 if forward else 1 - a
            lhs.append(
                jnp.concatenate(
                    [x[LAYER * (s + shift) : LAYER * (t + shift), :] for s, t in ranges], axis=0
                )
            )
        lhs = jnp.concatenate(lhs, axis=1)
        weights = fwd_w if forward else bwd_w
        outs = [jnp.dot(lhs, weights[l, c], preferred_element_type=F32) for c in range(3)]
        if forward:
            return outs[1] + from_left(outs[0]) + from_right(outs[2])
        return outs[1] + from_right(outs[0]) + from_left(outs[2])

    def masked(values, s):
        parts = []
        n = values.shape[0] // LAYER
        for k in range(n):
            piece = values[LAYER * k : LAYER * (k + 1)]
            if s + k < 4:
                piece = jnp.where(d > 0, piece, 0.0)
            elif s + k >= 8:
                piece = jnp.where(d < 3, piece, 0.0)
            parts.append(piece)
        return jnp.concatenate(parts, axis=0)

    def halo_copies(x):
        low = pltpu.make_async_remote_copy(
            src_ref=ext.at[x, pl.ds(LAYER, LAYER), :],
            dst_ref=ext.at[x, pl.ds(5 * LAYER, LAYER), :],
            send_sem=halo_send.at[x, 0],
            recv_sem=halo_recv.at[x, 1],
            device_id=(me, lax.rem(d + 3, 4)),
            device_id_type=MESH,
        )
        high = pltpu.make_async_remote_copy(
            src_ref=ext.at[x, pl.ds(4 * LAYER, LAYER), :],
            dst_ref=ext.at[x, pl.ds(0, LAYER), :],
            send_sem=halo_send.at[x, 1],
            recv_sem=halo_recv.at[x, 0],
            device_id=(me, lax.rem(d + 1, 4)),
            device_id_type=MESH,
        )
        return low, high

    def halo_start(x):
        low, high = halo_copies(x)

        @pl.when(d > 0)
        def _():
            low.start()

        @pl.when(d < 3)
        def _():
            high.start()

    def halo_wait(x):
        low, high = halo_copies(x)

        @pl.when(d > 0)
        def _():
            low.wait_send()
            high.wait_recv()

        @pl.when(d < 3)
        def _():
            high.wait_send()
            low.wait_recv()

    def fill_pieces(slot, values, rows_from):
        n = values.shape[0] // 8
        at = rows_from // 8
        for j in range(2):
            pieces_out[slot, 32 * j + at : 32 * j + at + n] = (
                values[:, 128 * j : 128 * j + 128].reshape(n, 8, 128).astype(BF16)
            )

    def cot_copies():
        low = pltpu.make_async_remote_copy(
            src_ref=wide.at[4, pl.ds(4 * LAYER, 2 * LAYER), :],
            dst_ref=wide.at[4, pl.ds(8 * LAYER, 2 * LAYER), :],
            send_sem=cot_send.at[0],
            recv_sem=cot_recv.at[1],
            device_id=(me, lax.rem(d + 3, 4)),
            device_id_type=MESH,
        )
        high = pltpu.make_async_remote_copy(
            src_ref=wide.at[4, pl.ds(6 * LAYER, 2 * LAYER), :],
            dst_ref=wide.at[4, pl.ds(2 * LAYER, 2 * LAYER), :],
            send_sem=cot_send.at[1],
            recv_sem=cot_recv.at[0],
            device_id=(me, lax.rem(d + 1, 4)),
            device_id_type=MESH,
        )
        return low, high

    z = me // 16
    spread = ((3 - z), lax.rem(z + 2, 4), z + 1 - 2 * lax.rem(z, 2), z)

    ys = [lax.rem(me + 2 + k, 4) for k in range(4)]

    def peers_of(zt, send, skip_own):
        @pl.loop(0, 4)
        def _(k):
            row = 16 * zt + 4 * lax.rem(me // 4 + 2 + k, 4)
            for at, y in enumerate(ys):
                if skip_own and at == 2:

                    @pl.when(k != 2)
                    def _():
                        send(row + y)
                else:
                    send(row + y)

    def scatter_start(slot, phase, source, target):
        def send(peer):
            pltpu.make_async_remote_copy(
                src_ref=source.at[slot, peer],
                dst_ref=target.at[slot, me],
                send_sem=a2a_send.at[slot, phase],
                recv_sem=a2a_recv.at[slot, phase],
                device_id=(peer, d),
                device_id_type=MESH,
            ).start()

        for zt in spread:
            peers_of(zt, send, zt is z)
        target[slot, me] = source[slot, me]

    def far_start():
        @pl.when(middle)
        def _():
            def send(peer):
                pltpu.make_async_remote_copy(
                    src_ref=mixed_out.at[0, peer],
                    dst_ref=far_in.at[me],
                    send_sem=far_sems.at[0],
                    recv_sem=far_sems.at[1],
                    device_id=(peer, 3 - d),
                    device_id_type=MESH,
                ).start()

            for zt in spread[::-1]:
                peers_of(zt, send, False)

    def far_wait():
        @pl.when(middle)
        def _():
            pltpu.make_async_remote_copy(
                src_ref=mixed_out.at[0],
                dst_ref=far_in,
                send_sem=far_sems.at[0],
                recv_sem=far_sems.at[1],
                device_id=(me, mate),
                device_id_type=MESH,
            ).wait()

    def near_copy():
        return pltpu.make_async_remote_copy(
            src_ref=mixed_in.at[0],
            dst_ref=near_in,
            send_sem=near_sems.at[0],
            recv_sem=near_sems.at[1],
            device_id=(me, mate),
            device_id_type=MESH,
        )

    def scatter_wait(slot, phase, source, target):
        copy = pltpu.make_async_remote_copy(
            src_ref=source.at[slot, pl.ds(0, crops - 1)],
            dst_ref=target.at[slot, pl.ds(0, crops - 1)],
            send_sem=a2a_send.at[slot, phase],
            recv_sem=a2a_recv.at[slot, phase],
            device_id=(me, mate),
            device_id_type=MESH,
        )
        copy.wait()

    def joined(pieces):
        whole = pieces.astype(F32)
        return jnp.concatenate(
            [whole[0:32].reshape(ROWS, 128), whole[32:64].reshape(ROWS, 128)], axis=1
        )

    def kernel_grad(l, x, first, g):
        stacked = jnp.concatenate(
            [from_right(g).astype(BF16), g.astype(BF16), from_left(g).astype(BF16)], axis=1
        )
        for a in range(3):
            u = x[LAYER * (first + a) : LAYER * (first + a) + ROWS, :]
            for c in range(3):
                r = lax.dot_general(
                    u, stacked[:, 256 * c : 256 * c + 256], TN, preferred_element_type=F32
                )

                def at(hp, j):
                    return r[32 * hp : 32 * hp + 32, 128 * j : 128 * j + 128]

                g0 = at(1, 0) + at(5, 1)
                g1 = at(2, 0) + at(6, 1)
                g2 = jnp.where(blk32 >= 2, at(3, 0) + at(7, 1), at(3, 1))
                g3 = jnp.where(blk32 == 3, at(4, 0), at(4, 1) + jnp.where(blk32 < 2, at(0, 0), 0.0))
                total = (
                    g0 + pltpu.roll(g1, 96, 1) + pltpu.roll(g2, 64, 1) + pltpu.roll(g3, 32, 1)
                )
                part[l, 0, 3 * a + c] = total[0:16]
                part[l, 1, 3 * a + c] = total[16:32]
        kg_send[l] = part[l, 1 - core].astype(BF16)

    def pair_copy(l):
        return pltpu.make_async_remote_copy(
            src_ref=kg_send.at[l],
            dst_ref=kg_recv.at[l],
            send_sem=pair_sems.at[l, 0],
            recv_sem=pair_sems.at[l, 1],
            device_id=(me, mate),
            device_id_type=MESH,
        )

    def all_copies(l):
        return [
            pltpu.make_async_remote_copy(
                src_ref=kg_pair.at[l],
                dst_ref=kg_all.at[l, k],
                send_sem=all_send.at[l, k],
                recv_sem=all_recv.at[l, k],
                device_id=(me, to),
                device_id_type=MESH,
            )
            for k, to in enumerate((mate, far, far_mate))
        ]

    def reduce_pairs(l):
        pair_copy(l).wait()
        kg_pair[l] = (part[l, core] + kg_recv[l].astype(F32)).astype(BF16)
        for copy in all_copies(l):
            copy.start()

    def reduce_finish(l):
        for copy in all_copies(l):
            copy.wait()
        own = kg_pair[l].astype(F32) + kg_all[l, 1].astype(F32)
        other = kg_all[l, 0].astype(F32) + kg_all[l, 2].astype(F32)
        for a in range(3):
            for c in range(3):
                k = 3 * a + c
                x = jnp.concatenate(
                    [
                        jnp.where(core == 0, own[k], other[k]),
                        jnp.where(core == 0, other[k], own[k]),
                    ],
                    axis=0,
                )
                turned = [x] + [pltpu.roll(x, 32 * m, 1) for m in (1, 2, 3)]
                for b in range(3):
                    z = jnp.zeros_like(x)
                    for q in range(4):
                        z = jnp.where(diagonal[q], turned[(q - 2 + b) % 4], z)
                    z = z.reshape(4, 8, 128)
                    z = z + pltpu.roll(z, 7, 1)
                    z = z + pltpu.roll(z, 6, 1)
                    t = 27 * l + 9 * a + 3 * b + c
                    for r in range(4):
                        kg[t, 2 * r : 2 * r + 1, :] = z[r, 0:1, :]
                        kg[t, 2 * r + 1 : 2 * r + 2, :] = z[r, 4:5, :]

    build(0, True, False)
    for load in loads[2:4]:
        load.wait()
    shape = (crops, crops)
    named = partner_row[...] == lax.broadcasted_iota(jnp.int32, shape, 0)
    found = jnp.where(named, lax.broadcasted_iota(jnp.int32, shape, 1), 0)
    inverse_rows[...] = jnp.broadcast_to(
        jnp.minimum(jnp.sum(found, axis=1, keepdims=True, dtype=jnp.int32), crops - 1),
        (crops, 128),
    )
    turn.start()
    pl.semaphore_wait(barrier, crops + 2 + (crops - 1) * lax.rem((d + 1) // 2, 2))

    xv, g1 = ext.at[0], ext.at[1]
    xb, xs, g3, g2, cotr = (wide.at[k] for k in range(5))

    halo_start(0)

    def first_layer(ranges):
        v = conv(xv, 0, ranges, True)
        s = logistic(v)
        hidden = v * s
        slope = s * (1.0 + v * (1.0 - s))
        at = 0
        for first, last in ranges:
            n = LAYER * (last - first)
            slope1[LAYER * (first - 1) : LAYER * (last - 1), :] = slope[at : at + n]
            fill_pieces(0, hidden[at : at + n], LAYER * (first - 1))
            at += n

    first_layer(((2, 4),))
    loads[4].wait()
    for layer in range(4):
        cotr[LAYER * (layer + 4) : LAYER * (layer + 5), :] = to_rows(
            cot[0, layer].astype(F32)
        ).astype(BF16)
    build(1, True, False)
    halo_wait(0)
    first_layer(((1, 2), (4, 5)))

    scatter_start(0, 0, pieces_out, pieces_in)
    cot_low, cot_high = cot_copies()

    @pl.when(d > 0)
    def _():
        cot_low.start()

    @pl.when(d < 3)
    def _():
        cot_high.start()

    build(2, True, True)
    scatter_wait(0, 0, pieces_out, pieces_in)

    def blend(n, carry):
        own = pieces_in[0, n].astype(F32)
        other = pieces_in[0, partner[0, n]].astype(F32)
        mixed_out[0, n] = (OWN_SHARE * own + PARTNER_SHARE * other).astype(BF16)
        return carry

    lax.fori_loop(0, crops, blend, 0, unroll=8)
    far_start()
    scatter_start(0, 1, mixed_out, mixed_in)
    build(1, False, True)
    build(0, False, True)
    scatter_wait(0, 1, mixed_out, mixed_in)
    near_copy().start()
    xb[4 * LAYER : 8 * LAYER, :] = joined(mixed_in[0]).astype(BF16)

    def second_layer(s, t):
        v = conv(xb, 1, ((s, t),), True)
        gate = logistic(v)
        xs[LAYER * s : LAYER * t, :] = masked(v * gate, s).astype(BF16)
        slope2[LAYER * s : LAYER * t, :] = gate * (1.0 + v * (1.0 - gate))

    second_layer(5, 7)
    far_wait()

    @pl.when(middle)
    def _():
        xb[pl.ds(pl.multiple_of(512 * core, 512), 256), :] = joined(far_in[...]).astype(BF16)

    near_copy().wait()
    xb[pl.ds(pl.multiple_of(512 * (1 - core), 512), 256), :] = joined(near_in[...]).astype(BF16)
    second_layer(1, 5)
    second_layer(7, 11)

    @pl.when(d > 0)
    def _():
        cot_low.wait_send()
        cot_high.wait_recv()

    @pl.when(d < 3)
    def _():
        cot_high.wait_send()
        cot_low.wait_recv()

    def third_layer(s, t):
        v = conv(xs, 2, ((s, t),), True)
        gate = logistic(v)
        slope = gate * (1.0 + v * (1.0 - gate))
        facing = cotr[LAYER * s : LAYER * t, :].astype(F32)
        g3[LAYER * s : LAYER * t, :] = masked(facing * slope, s).astype(BF16)

    third_layer(2, 6)
    third_layer(6, 10)

    def back_three(s, t):
        g = conv(g3, 2, ((s, t),), False) * slope2[LAYER * s : LAYER * t, :]
        g2[LAYER * s : LAYER * t, :] = masked(g, s).astype(BF16)

    back_three(3, 6)
    back_three(6, 9)
    fill_pieces(1, conv(g2, 1, ((4, 8),), False), 0)
    scatter_start(1, 0, pieces_out, pieces_in)
    kernel_grad(2, xs, 3, g3[4 * LAYER : 8 * LAYER, :].astype(F32))
    pair_copy(2).start()
    kernel_grad(1, xb, 3, g2[4 * LAYER : 8 * LAYER, :].astype(F32))
    pair_copy(1).start()
    reduce_pairs(2)
    scatter_wait(1, 0, pieces_out, pieces_in)
    turn.wait()

    def blend_back(n, carry):
        own = pieces_in[1, n].astype(F32)
        other = pieces_in[1, inverse[n, 0]].astype(F32)
        mixed_out[1, n] = (OWN_SHARE * own + PARTNER_SHARE * other).astype(BF16)
        return carry

    lax.fori_loop(0, crops, blend_back, 0, unroll=8)
    scatter_start(1, 1, mixed_out, mixed_in)
    reduce_pairs(1)
    reduce_finish(2)
    scatter_wait(1, 1, mixed_out, mixed_in)

    g_one = (joined(mixed_in[1]) * slope1[...]).astype(BF16)
    g1[LAYER : 5 * LAYER, :] = g_one
    halo_start(1)
    kernel_grad(0, xv, 0, g_one.astype(F32))
    pair_copy(0).start()
    g = conv(g1, 0, ((2, 4),), False)
    gvol[0, 1] = from_rows(g[0:LAYER]).astype(BF16)
    gvol[0, 2] = from_rows(g[LAYER:]).astype(BF16)
    reduce_pairs(0)
    halo_wait(1)
    g = conv(g1, 0, ((1, 2), (4, 5)), False)
    gvol[0, 0] = from_rows(g[0:LAYER]).astype(BF16)
    gvol[0, 3] = from_rows(g[LAYER:]).astype(BF16)
    reduce_finish(1)
    reduce_finish(0)


def per_device(crops, volume, kernels, partner, cotangent):
    vmem = pl.BlockSpec(memory_space=pltpu.VMEM)
    hbm = pl.BlockSpec(memory_space=pltpu.HBM)
    dma = pltpu.SemaphoreType.DMA
    grad_volume, kg = pl.pallas_call(
        functools.partial(kernel, crops),
        out_shape=(
            jax.ShapeDtypeStruct((1, 4, 8, 2048), BF16),
            jax.ShapeDtypeStruct((81, 8, 128), F32),
        ),
        in_specs=[hbm] * 4,
        out_specs=(vmem, vmem),
        scratch_shapes=[
            pltpu.SMEM((1, crops), jnp.int32),
            pltpu.VMEM((1, crops), jnp.int32),
            pltpu.VMEM((crops, 128), jnp.int32),
            pltpu.SMEM((crops, 128), jnp.int32),
            pltpu.VMEM((1, 4, 8, 2048), BF16),
            pltpu.VMEM((1, 4, 8, 2048), BF16),
            pltpu.VMEM((3, 27, 1024), BF16),
            pltpu.VMEM((3, 27, 1024), F32),
            pltpu.VMEM((3, 3, 768, 256), BF16),
            pltpu.VMEM((3, 3, 768, 256), BF16),
            pltpu.VMEM((2, 384, 256), BF16),
            pltpu.VMEM((5, 768, 256), BF16),
            pltpu.VMEM((256, 256), F32),
            pltpu.VMEM((768, 256), F32),
            pltpu.VMEM((3, 2, 9, 16, 128), F32),
            pltpu.VMEM((2, crops, 8, 128), BF16),
            pltpu.VMEM((2, crops, 8, 128), BF16),
            pltpu.VMEM((2, crops, 8, 128), BF16),
            pltpu.VMEM((2, crops, 8, 128), BF16),
            pltpu.VMEM((crops, 8, 128), BF16),
            pltpu.VMEM((crops, 8, 128), BF16),
            pltpu.VMEM((3, 9, 16, 128), BF16),
            pltpu.VMEM((3, 9, 16, 128), BF16),
            pltpu.VMEM((3, 9, 16, 128), BF16),
            pltpu.VMEM((3, 3, 9, 16, 128), BF16),
            dma((2, 2)),
            dma((2, 2)),
            dma((2,)),
            dma((2,)),
            dma((2,)),
            dma((2,)),
            dma((2, 2)),
            dma((2, 2)),
            dma((3, 2)),
            dma((3, 3)),
            dma((3, 3)),
            dma((6,)),
        ],
        compiler_params=pltpu.CompilerParams(
            collective_id=0, has_side_effects=True, vmem_limit_bytes=48 * 1024 * 1024
        ),
    )(*(pltpu.with_memory_space_constraint(x, pltpu.HBM) for x in (partner[None, :], volume, cotangent, kernels)))
    return grad_volume, kg.reshape(1, 3, 27, CH * CH)


def solution(mesh):
    crops = mesh.shape["sample"]
    in_specs = (P("sample", "depth", None, None), P(), P(), P("sample", "depth", None, None))
    out_specs = (P("sample", "depth", None, None), P("sample", None, None, None))
    return jax.shard_map(
        functools.partial(per_device, crops),
        mesh=mesh,
        in_specs=in_specs,
        out_specs=out_specs,
        check_vma=False,
    )
```

```python
import functools

import jax
import jax.numpy as jnp
from jax import lax
from jax.experimental import pallas as pl
from jax.experimental.pallas import tpu as pltpu
from jax.sharding import PartitionSpec as P

CH = 32
OWN_SHARE = 0.6
PARTNER_SHARE = 0.4
MESH = pl.DeviceIdType.MESH
F32 = jnp.float32
BF16 = jnp.bfloat16
ROWS = 256
LANES = 256
LAYER = 64
NT = (((1,), (1,)), ((), ()))
TN = (((0,), (0,)), ((), ()))


def logistic(v):
    return 0.5 * jnp.tanh(0.5 * v) + 0.5


def block_transpose(y):
    sub = lax.broadcasted_iota(jnp.int32, y.shape, 1) % 4
    blk = lax.broadcasted_iota(jnp.int32, y.shape, 2) // 32
    delta = sub - blk
    turned = [y] + [pltpu.roll(y, 128 - 32 * m, 2) for m in (1, 2, 3)]
    out = y
    for m in (1, 2, 3):
        out = jnp.where(delta == m, pltpu.roll(turned[m], m, 1), out)
        out = jnp.where(delta == m - 4, pltpu.roll(turned[m], m + 4, 1), out)
    return out


def to_rows(v):
    even = jnp.stack([v[:, 256 * t : 256 * t + 128] for t in range(8)])
    odd = jnp.stack([v[:, 256 * t + 128 : 256 * t + 256] for t in range(8)])
    first = lax.broadcasted_iota(jnp.int32, even.shape, 1) < 4
    y0 = jnp.where(first, even, pltpu.roll(odd, 4, 1))
    y1 = jnp.where(first, pltpu.roll(even, 4, 1), odd)
    return jnp.concatenate(
        [block_transpose(y0).reshape(64, 128), block_transpose(y1).reshape(64, 128)], axis=1
    )


def from_rows(r):
    y0 = block_transpose(r[:, :128].reshape(8, 8, 128))
    y1 = block_transpose(r[:, 128:].reshape(8, 8, 128))
    first = lax.broadcasted_iota(jnp.int32, y0.shape, 1) < 4
    even = jnp.where(first, y0, pltpu.roll(y1, 4, 1))
    odd = jnp.where(first, pltpu.roll(y0, 4, 1), y1)
    return jnp.concatenate([part[t] for t in range(8) for part in (even, odd)], axis=1)


def width_index(shape):
    return lax.broadcasted_iota(jnp.int32, shape, 0) % LAYER


def from_left(x):
    return jnp.where(width_index(x.shape) == 0, 0.0, pltpu.roll(x, 1, 0))


def from_right(x):
    return jnp.where(width_index(x.shape) == LAYER - 1, 0.0, pltpu.roll(x, x.shape[0] - 1, 0))


def kernel(
    crops,
    partner_hbm,
    vol_hbm,
    cot_hbm,
    kern_hbm,
    gvol,
    kg,
    partner,
    partner_row,
    inverse_rows,
    inverse,
    vol,
    cot,
    kern,
    kf,
    fwd_w,
    bwd_w,
    ext,
    wide,
    slope1,
    slope2,
    part,
    pieces_out,
    pieces_in,
    mixed_out,
    mixed_in,
    far_in,
    near_in,
    kg_send,
    kg_recv,
    kg_pair,
    kg_all,
    kg_sum,
    kg_shared,
    halo_send,
    halo_recv,
    cot_send,
    cot_recv,
    far_sems,
    near_sems,
    a2a_send,
    a2a_recv,
    pair_sems,
    all_send,
    all_recv,
    share_sems,
    load_sems,
):
    loads = [
        pltpu.make_async_copy(source, target, load_sems.at[k])
        for k, (source, target) in enumerate(
            (
                (vol_hbm, vol),
                (kern_hbm, kern),
                (partner_hbm, partner_row),
                (partner_hbm, partner),
                (cot_hbm, cot),
            )
        )
    ]
    turn = pltpu.make_async_copy(inverse_rows, inverse, load_sems.at[5])
    for load in loads:
        load.start()
    me = lax.axis_index("sample")
    d = lax.axis_index("depth")
    core = lax.rem(d, 2)
    mate = d + 1 - 2 * core
    far = lax.rem(d + 2, 4)
    far_mate = lax.rem(mate + 2, 4)

    z = me // 16
    mid = (z == 1) | (z == 2)
    middle = (d == 1) | (d == 2)
    mid_count = lax.rem((z + 1) // 2, 2)
    middle_count = lax.rem((d + 1) // 2, 2)
    slot_here = me - 16
    ys = [lax.rem(me + 2 + k, 4) for k in range(4)]
    xs_far = me // 4 + 2

    def peers_of(zt, send, skip_own):
        @pl.loop(0, 4)
        def _(k):
            row = 16 * zt + 4 * lax.rem(xs_far + k, 4)
            for at, y in enumerate(ys):
                if skip_own and at == 2:

                    @pl.when((k != 2) | (zt != z))
                    def _():
                        send(row + y)
                else:
                    send(row + y)

    mids_first = 1 + mid_count * (2 - z) + (1 - mid_count) * (1 - z // 3)
    mid_order = (mids_first, 3 - mids_first)
    edge = 3 * (2 - z)
    all_order = (edge, 3 - edge, 3 - z, z)
    far_order = (z, 3 - z, 3 - edge, edge)

    barrier = pltpu.get_barrier_semaphore()

    def greet(depth):
        def signal(peer):
            pl.semaphore_signal(barrier, inc=1, device_id=(peer, depth), device_id_type=MESH)

        return signal

    for zt in mid_order:
        peers_of(zt, greet(d), True)

    @pl.when(mid)
    def _():
        for zt in (0, 3):
            peers_of(zt, greet(d), False)

    for k in (1, 2, 3):
        pl.semaphore_signal(
            barrier, inc=1, device_id=(me, lax.rem(d + k, 4)), device_id_type=MESH
        )

    @pl.when(middle)
    def _():
        for zt in mid_order:
            peers_of(zt, greet(3 - d), True)

    loads[0].wait()
    for layer in range(4):
        ext[0, LAYER * (layer + 1) : LAYER * (layer + 2), :] = to_rows(
            vol[0, layer].astype(F32)
        ).astype(BF16)

    @pl.when(d == 0)
    def _():
        for k in range(2):
            ext[k, 0:LAYER, :] = jnp.zeros((LAYER, LANES), BF16)
        wide[0, 0 : 4 * LAYER, :] = jnp.zeros((4 * LAYER, LANES), BF16)

    @pl.when(d == 3)
    def _():
        for k in range(2):
            ext[k, 5 * LAYER : 6 * LAYER, :] = jnp.zeros((LAYER, LANES), BF16)
        wide[0, 8 * LAYER : 12 * LAYER, :] = jnp.zeros((4 * LAYER, LANES), BF16)

    loads[1].wait()
    for l in range(3):
        kf[l] = kern[l].astype(F32)

    sub = lax.broadcasted_iota(jnp.int32, (8, 128), 0)
    blk8 = lax.broadcasted_iota(jnp.int32, (8, 128), 1) // 32
    sub32 = lax.broadcasted_iota(jnp.int32, (32, 128), 0) % 4
    blk32 = lax.broadcasted_iota(jnp.int32, (32, 128), 1) // 32

    first_rows = (
        lax.broadcasted_iota(jnp.int32, (32, 128), 0) == lax.broadcasted_iota(jnp.int32, (32, 128), 1)
    ).astype(F32).astype(BF16)
    diagonal = [(sub32 == q) & (blk32 == q) for q in range(4)]

    def tap_tiles(l, a, c):
        taps = []
        for b in range(3):
            row = kf[l, pl.ds(9 * a + 3 * b + c, 1), :]
            tiles = []
            for r in range(4):
                low = jnp.broadcast_to(row[:, 256 * r : 256 * r + 128], (8, 128))
                high = jnp.broadcast_to(row[:, 256 * r + 128 : 256 * r + 256], (8, 128))
                z = jnp.where(blk8 == sub % 4, jnp.where(sub < 4, low, high), 0.0)
                z = z + pltpu.roll(z, 64, 1)
                tiles.append(z + pltpu.roll(z, 32, 1))
            taps.append(jnp.concatenate(tiles, axis=0))
        return taps

    def store_blocks(target, l, a, c, taps, step):
        row0 = pl.multiple_of(a * 256, 256)
        for hp in range(8):
            for j in range(2):
                block = jnp.zeros((32, 128), F32)
                for b in range(3):
                    h = hp + step * (b - 1)
                    if h // 4 == j and 0 <= h < 8:
                        block = jnp.where(blk32 == h % 4, taps[b], block)
                rows = pl.ds(pl.multiple_of(row0 + 32 * hp, 32), 32)
                target[l, c, rows, 128 * j : 128 * j + 128] = block.astype(BF16)

    def build(l, forward, backward):
        @pl.loop(0, 3)
        def _(a):
            for c in range(3):
                taps = tap_tiles(l, a, c)
                if forward:
                    store_blocks(fwd_w, l, a, c, taps, -1)
                if backward:
                    stacked = jnp.concatenate([tap for tap in taps for _ in range(4)], axis=0)
                    back = lax.dot_general(
                        first_rows, stacked.astype(BF16), NT, preferred_element_type=F32
                    )
                    store_blocks(
                        bwd_w, l, a, c, [back[:, 128 * b : 128 * b + 128] for b in range(3)], 1
                    )

    def at_rows(s, n):
        start = LAYER * s
        if not isinstance(s, int):
            start = pl.multiple_of(start, LAYER)
        return pl.ds(start, LAYER * n)

    def taps_of(lhs, l, forward):
        weights = fwd_w if forward else bwd_w
        outs = [jnp.dot(lhs, weights[l, c], preferred_element_type=F32) for c in range(3)]
        if forward:
            return outs[1] + from_left(outs[0]) + from_right(outs[2])
        return outs[1] + from_right(outs[0]) + from_left(outs[2])

    def conv(x, l, s, n, forward):
        shifts = (-1, 0, 1) if forward else (1, 0, -1)
        lhs = jnp.concatenate([x[at_rows(s + shift, n), :] for shift in shifts], axis=1)
        return taps_of(lhs, l, forward)

    def conv_ranges(x, l, ranges, forward):
        shifts = (-1, 0, 1) if forward else (1, 0, -1)
        lhs = [
            jnp.concatenate(
                [x[LAYER * (s + shift) : LAYER * (t + shift), :] for s, t in ranges], axis=0
            )
            for shift in shifts
        ]
        return taps_of(jnp.concatenate(lhs, axis=1), l, forward)

    def masked(values, s):
        parts = []
        n = values.shape[0] // LAYER
        for k in range(n):
            piece = values[LAYER * k : LAYER * (k + 1)]
            if s + k < 4:
                piece = jnp.where(d > 0, piece, 0.0)
            elif s + k >= 8:
                piece = jnp.where(d < 3, piece, 0.0)
            parts.append(piece)
        return jnp.concatenate(parts, axis=0)

    def halo_copies(x):
        low = pltpu.make_async_remote_copy(
            src_ref=ext.at[x, pl.ds(LAYER, LAYER), :],
            dst_ref=ext.at[x, pl.ds(5 * LAYER, LAYER), :],
            send_sem=halo_send.at[x, 0],
            recv_sem=halo_recv.at[x, 1],
            device_id=(me, lax.rem(d + 3, 4)),
            device_id_type=MESH,
        )
        high = pltpu.make_async_remote_copy(
            src_ref=ext.at[x, pl.ds(4 * LAYER, LAYER), :],
            dst_ref=ext.at[x, pl.ds(0, LAYER), :],
            send_sem=halo_send.at[x, 1],
            recv_sem=halo_recv.at[x, 0],
            device_id=(me, lax.rem(d + 1, 4)),
            device_id_type=MESH,
        )
        return low, high

    def halo_start(x):
        low, high = halo_copies(x)

        @pl.when(d > 0)
        def _():
            low.start()

        @pl.when(d < 3)
        def _():
            high.start()

    def halo_wait(x):
        low, high = halo_copies(x)

        @pl.when(d > 0)
        def _():
            low.wait_send()
            high.wait_recv()

        @pl.when(d < 3)
        def _():
            high.wait_send()
            low.wait_recv()

    def fill_pieces(slot, values, rows_from):
        n = values.shape[0] // 16
        at = rows_from // 16
        for j in range(2):
            pieces_out[slot, 16 * j + at : 16 * j + at + n] = (
                values[:, 128 * j : 128 * j + 128].astype(BF16).reshape(n, 16, 128)
            )

    def cot_copies():
        low = pltpu.make_async_remote_copy(
            src_ref=wide.at[4, pl.ds(4 * LAYER, 2 * LAYER), :],
            dst_ref=wide.at[4, pl.ds(8 * LAYER, 2 * LAYER), :],
            send_sem=cot_send.at[0],
            recv_sem=cot_recv.at[1],
            device_id=(me, lax.rem(d + 3, 4)),
            device_id_type=MESH,
        )
        high = pltpu.make_async_remote_copy(
            src_ref=wide.at[4, pl.ds(6 * LAYER, 2 * LAYER), :],
            dst_ref=wide.at[4, pl.ds(2 * LAYER, 2 * LAYER), :],
            send_sem=cot_send.at[1],
            recv_sem=cot_recv.at[0],
            device_id=(me, lax.rem(d + 1, 4)),
            device_id_type=MESH,
        )
        return low, high

    def first_copy(slot, source, target, to):
        return pltpu.make_async_remote_copy(
            src_ref=source,
            dst_ref=target,
            send_sem=a2a_send.at[slot, 0],
            recv_sem=a2a_recv.at[slot, 0],
            device_id=(to, d),
            device_id_type=MESH,
        )

    def scatter_start(slot):
        def send(peer):
            first_copy(slot, pieces_out.at[slot, peer - 16], pieces_in.at[slot, me], peer).start()

        for zt in mid_order:
            peers_of(zt, send, True)

        @pl.when(mid)
        def _():
            pieces_in[slot, me] = pieces_out[slot, slot_here]

    def scatter_wait(slot):
        @pl.when(mid)
        def _():
            span = pieces_in.at[slot, pl.ds(0, 31)]
            first_copy(slot, pieces_out.at[slot, pl.ds(0, 31)], span, me).wait_send()
            span = pieces_in.at[slot, pl.ds(0, crops - 1)]
            first_copy(slot, span, span, me).wait_recv()

        @pl.when(jnp.logical_not(mid))
        def _():
            span = pieces_in.at[slot, pl.ds(0, 32)]
            first_copy(slot, pieces_out.at[slot], span, me).wait_send()

    def second_copy(slot, source, target, to):
        return pltpu.make_async_remote_copy(
            src_ref=source,
            dst_ref=target,
            send_sem=a2a_send.at[slot, 1],
            recv_sem=a2a_recv.at[slot, 1],
            device_id=(to, d),
            device_id_type=MESH,
        )

    def gather_start(slot):
        def send(peer):
            second_copy(
                slot, mixed_out.at[slot, peer], mixed_in.at[slot, slot_here], peer
            ).start()

        for zt in all_order:
            peers_of(zt, send, True)
        mixed_in[slot, slot_here] = mixed_out[slot, me]

    def gather_wait(slot):
        @pl.when(mid)
        def _():
            span = mixed_out.at[slot, pl.ds(0, crops - 1)]
            second_copy(slot, span, span, me).wait_send()
            span = mixed_in.at[slot, pl.ds(0, 31)]
            second_copy(slot, span, span, me).wait_recv()

        @pl.when(jnp.logical_not(mid))
        def _():
            span = mixed_in.at[slot]
            second_copy(slot, span, span, me).wait_recv()

    def far_copy(source, target, to):
        return pltpu.make_async_remote_copy(
            src_ref=source,
            dst_ref=target,
            send_sem=far_sems.at[0],
            recv_sem=far_sems.at[1],
            device_id=(to, 3 - d),
            device_id_type=MESH,
        )

    def far_start():
        @pl.when(middle)
        def _():
            def send(peer):
                far_copy(mixed_out.at[0, peer], far_in.at[slot_here], peer).start()

            for zt in far_order:
                peers_of(zt, send, False)

    def far_wait():
        @pl.when(middle)
        def _():
            @pl.when(mid)
            def _():
                far_copy(mixed_out.at[0], mixed_out.at[0], me).wait_send()

            far_copy(far_in, far_in, me).wait_recv()

    def near_copy():
        return pltpu.make_async_remote_copy(
            src_ref=mixed_in.at[0],
            dst_ref=near_in,
            send_sem=near_sems.at[0],
            recv_sem=near_sems.at[1],
            device_id=(me, mate),
            device_id_type=MESH,
        )

    def joined(pieces):
        return jnp.concatenate(
            [pieces[0:16].reshape(ROWS, 128), pieces[16:32].reshape(ROWS, 128)], axis=1
        )

    def kernel_grad(l, x, first, g):
        stacked = jnp.concatenate(
            [from_right(g).astype(BF16), g.astype(BF16), from_left(g).astype(BF16)], axis=1
        )
        for a in range(3):
            u = x[LAYER * (first + a) : LAYER * (first + a) + ROWS, :]
            for c in range(3):
                r = lax.dot_general(
                    u, stacked[:, 256 * c : 256 * c + 256], TN, preferred_element_type=F32
                )

                def at(hp, j):
                    return r[32 * hp : 32 * hp + 32, 128 * j : 128 * j + 128]

                g0 = at(1, 0) + at(5, 1)
                g1 = at(2, 0) + at(6, 1)
                g2 = jnp.where(blk32 >= 2, at(3, 0) + at(7, 1), at(3, 1))
                g3 = jnp.where(blk32 == 3, at(4, 0), at(4, 1) + jnp.where(blk32 < 2, at(0, 0), 0.0))
                total = (
                    g0 + pltpu.roll(g1, 96, 1) + pltpu.roll(g2, 64, 1) + pltpu.roll(g3, 32, 1)
                )
                part[l, 0, 3 * a + c] = total[0:16]
                part[l, 1, 3 * a + c] = total[16:32]
        kg_send[l] = part[l, 1 - core].astype(BF16)

    def pair_copy(l):
        return pltpu.make_async_remote_copy(
            src_ref=kg_send.at[l],
            dst_ref=kg_recv.at[l],
            send_sem=pair_sems.at[l, 0],
            recv_sem=pair_sems.at[l, 1],
            device_id=(me, mate),
            device_id_type=MESH,
        )

    def all_copies(l):
        return [
            pltpu.make_async_remote_copy(
                src_ref=kg_pair.at[l],
                dst_ref=kg_all.at[l, k],
                send_sem=all_send.at[l, k],
                recv_sem=all_recv.at[l, k],
                device_id=(me, to),
                device_id_type=MESH,
            )
            for k, to in enumerate((mate, far, far_mate))
        ]

    def pair_sum(l):
        pair_copy(l).wait()
        kg_pair[l] = (part[l, core] + kg_recv[l].astype(F32)).astype(BF16)

    def reduce_pairs(l):
        pair_sum(l)
        for copy in all_copies(l):
            copy.start()

    def reduce_finish(l):
        for copy in all_copies(l):
            copy.wait()
        own = kg_pair[l].astype(F32) + kg_all[l, 1].astype(F32)
        other = kg_all[l, 0].astype(F32) + kg_all[l, 2].astype(F32)
        store_grads(l, own, other)

    def share_copy(l):
        return pltpu.make_async_remote_copy(
            src_ref=kg_sum.at[l - 1],
            dst_ref=kg_shared.at[l - 1],
            send_sem=share_sems.at[l - 1, 0],
            recv_sem=share_sems.at[l - 1, 1],
            device_id=(me, mate),
            device_id_type=MESH,
        )

    def reduce_share(l):
        all_copies(l)[1].wait()
        kg_sum[l - 1] = kg_pair[l].astype(F32) + kg_all[l, 1].astype(F32)
        share_copy(l).start()

    def share_finish(l):
        share_copy(l).wait()
        store_grads(l, kg_sum[l - 1], kg_shared[l - 1])

    def store_grads(l, own, other):
        for a in range(3):
            for c in range(3):
                k = 3 * a + c
                x = jnp.concatenate(
                    [
                        jnp.where(core == 0, own[k], other[k]),
                        jnp.where(core == 0, other[k], own[k]),
                    ],
                    axis=0,
                )
                turned = [x] + [pltpu.roll(x, 32 * m, 1) for m in (1, 2, 3)]
                for b in range(3):
                    z = jnp.zeros_like(x)
                    for q in range(4):
                        z = jnp.where(diagonal[q], turned[(q - 2 + b) % 4], z)
                    z = z.reshape(4, 8, 128)
                    z = z + pltpu.roll(z, 7, 1)
                    z = z + pltpu.roll(z, 6, 1)
                    t = 27 * l + 9 * a + 3 * b + c
                    for r in range(4):
                        kg[t, 2 * r : 2 * r + 1, :] = z[r, 0:1, :]
                        kg[t, 2 * r + 1 : 2 * r + 2, :] = z[r, 4:5, :]

    build(0, True, False)
    for load in loads[2:4]:
        load.wait()
    shape = (crops, crops)
    named = partner_row[...] == lax.broadcasted_iota(jnp.int32, shape, 0)
    found = jnp.where(named, lax.broadcasted_iota(jnp.int32, shape, 1), 0)
    inverse_rows[...] = jnp.broadcast_to(
        jnp.minimum(jnp.sum(found, axis=1, keepdims=True, dtype=jnp.int32), crops - 1),
        (crops, 128),
    )
    turn.start()
    pl.semaphore_wait(barrier, 35 + 31 * mid_count + 63 * mid_count * middle_count)

    xv, g1 = ext.at[0], ext.at[1]
    xb, xs, g3, g2, cotr = (wide.at[k] for k in range(5))

    halo_start(0)

    def first_layer(ranges):
        v = conv_ranges(xv, 0, ranges, True)
        s = logistic(v)
        hidden = v * s
        slope = s * (1.0 + v * (1.0 - s))
        at = 0
        for first, last in ranges:
            n = LAYER * (last - first)
            slope1[LAYER * (first - 1) : LAYER * (last - 1), :] = slope[at : at + n]
            fill_pieces(0, hidden[at : at + n], LAYER * (first - 1))
            at += n

    first_layer(((2, 4),))
    loads[4].wait()
    for layer in range(4):
        cotr[LAYER * (layer + 4) : LAYER * (layer + 5), :] = to_rows(
            cot[0, layer].astype(F32)
        ).astype(BF16)
    build(1, True, False)
    halo_wait(0)
    first_layer(((1, 2), (4, 5)))

    scatter_start(0)
    cot_low, cot_high = cot_copies()

    @pl.when(d > 0)
    def _():
        cot_low.start()

    @pl.when(d < 3)
    def _():
        cot_high.start()

    build(2, True, True)
    scatter_wait(0)

    def mix(slot, other_of):
        def step(n, carry):
            own = pieces_in[slot, n].astype(F32)
            other = pieces_in[slot, other_of(n)].astype(F32)
            mixed_out[slot, n] = (OWN_SHARE * own + PARTNER_SHARE * other).astype(BF16)
            return carry

        lax.fori_loop(0, crops, step, 0, unroll=8)

    @pl.when(mid)
    def _():
        mix(0, lambda n: partner[0, n])
        gather_start(0)
        far_start()

    build(1, False, True)
    build(0, False, True)
    gather_wait(0)
    near_copy().start()
    xb[4 * LAYER : 8 * LAYER, :] = joined(mixed_in[0])

    def far_masked(values):
        parts = []
        for k in range(4):
            piece = values[LAYER * k : LAYER * (k + 1)]
            if k == 0:
                keep = middle | (core == 1)
            elif k == 3:
                keep = middle | (core == 0)
            else:
                keep = middle
            parts.append(jnp.where(keep, piece, 0.0))
        return jnp.concatenate(parts, axis=0)

    def second_layer(s, n, mask):
        v = conv(xb, 1, s, n, True)
        gate = logistic(v)
        second = v * gate
        rows = at_rows(s, n)
        xs[rows, :] = (far_masked(second) if mask else second).astype(BF16)
        slope2[rows, :] = gate * (1.0 + v * (1.0 - gate))

    second_layer(5, 2, False)
    far_wait()

    @pl.when(middle)
    def _():
        xb[pl.ds(pl.multiple_of(512 * core, 512), 256), :] = joined(far_in[...])

    second_layer(1 + 6 * core, 4, True)

    @pl.when(d > 0)
    def _():
        cot_low.wait_send()
        cot_high.wait_recv()

    @pl.when(d < 3)
    def _():
        cot_high.wait_send()
        cot_low.wait_recv()

    def third_layer(s, far_side):
        v = conv(xs, 2, s, 4, True)
        gate = logistic(v)
        slope = gate * (1.0 + v * (1.0 - gate))
        rows = at_rows(s, 4)
        values = cotr[rows, :].astype(F32) * slope
        if far_side:
            parts = []
            for k in range(4):
                piece = values[LAYER * k : LAYER * (k + 1)]
                keep = middle | ((core == 1) if k < 2 else (core == 0))
                parts.append(jnp.where(keep, piece, 0.0))
            values = jnp.concatenate(parts, axis=0)
        g3[rows, :] = values.astype(BF16)

    third_layer(2 + 4 * core, True)
    near_copy().wait()
    xb[pl.ds(pl.multiple_of(512 * (1 - core), 512), 256), :] = joined(near_in[...])
    second_layer(7 - 6 * core, 4, False)
    third_layer(6 - 4 * core, False)

    def back_three(s, n):
        g = conv(g3, 2, s, n, False) * slope2[LAYER * s : LAYER * (s + n), :]
        g2[LAYER * s : LAYER * (s + n), :] = masked(g, s).astype(BF16)

    back_three(3, 3)
    back_three(6, 3)
    fill_pieces(1, conv(g2, 1, 4, 4, False), 0)
    scatter_start(1)
    kernel_grad(2, xs, 3, g3[4 * LAYER : 8 * LAYER, :].astype(F32))
    pair_copy(2).start()
    kernel_grad(1, xb, 3, g2[4 * LAYER : 8 * LAYER, :].astype(F32))
    pair_copy(1).start()
    pair_sum(2)
    all_copies(2)[1].start()
    pair_sum(1)
    all_copies(1)[1].start()
    turn.wait()
    scatter_wait(1)

    @pl.when(mid)
    def _():
        mix(1, lambda n: inverse[n, 0])
        gather_start(1)

    reduce_share(2)
    reduce_share(1)
    share_finish(2)
    share_finish(1)
    gather_wait(1)

    g_one = (joined(mixed_in[1]).astype(F32) * slope1[...]).astype(BF16)
    g1[LAYER : 5 * LAYER, :] = g_one
    halo_start(1)
    kernel_grad(0, xv, 0, g_one.astype(F32))
    pair_copy(0).start()
    g = conv(g1, 0, 2, 2, False)
    gvol[0, 1] = from_rows(g[0:LAYER]).astype(BF16)
    gvol[0, 2] = from_rows(g[LAYER:]).astype(BF16)
    reduce_pairs(0)
    halo_wait(1)
    g = conv_ranges(g1, 0, ((1, 2), (4, 5)), False)
    gvol[0, 0] = from_rows(g[0:LAYER]).astype(BF16)
    gvol[0, 3] = from_rows(g[LAYER:]).astype(BF16)
    reduce_finish(0)


def per_device(crops, volume, kernels, partner, cotangent):
    vmem = pl.BlockSpec(memory_space=pltpu.VMEM)
    hbm = pl.BlockSpec(memory_space=pltpu.HBM)
    dma = pltpu.SemaphoreType.DMA
    grad_volume, kg = pl.pallas_call(
        functools.partial(kernel, crops),
        out_shape=(
            jax.ShapeDtypeStruct((1, 4, 8, 2048), BF16),
            jax.ShapeDtypeStruct((81, 8, 128), F32),
        ),
        in_specs=[hbm] * 4,
        out_specs=(vmem, vmem),
        scratch_shapes=[
            pltpu.SMEM((1, crops), jnp.int32),
            pltpu.VMEM((1, crops), jnp.int32),
            pltpu.VMEM((crops, 128), jnp.int32),
            pltpu.SMEM((crops, 128), jnp.int32),
            pltpu.VMEM((1, 4, 8, 2048), BF16),
            pltpu.VMEM((1, 4, 8, 2048), BF16),
            pltpu.VMEM((3, 27, 1024), BF16),
            pltpu.VMEM((3, 27, 1024), F32),
            pltpu.VMEM((3, 3, 768, 256), BF16),
            pltpu.VMEM((3, 3, 768, 256), BF16),
            pltpu.VMEM((2, 384, 256), BF16),
            pltpu.VMEM((5, 768, 256), BF16),
            pltpu.VMEM((256, 256), F32),
            pltpu.VMEM((768, 256), F32),
            pltpu.VMEM((3, 2, 9, 16, 128), F32),
            pltpu.VMEM((2, 32, 16, 128), BF16),
            pltpu.VMEM((2, crops, 16, 128), BF16),
            pltpu.VMEM((2, crops, 16, 128), BF16),
            pltpu.VMEM((2, 32, 16, 128), BF16),
            pltpu.VMEM((32, 16, 128), BF16),
            pltpu.VMEM((32, 16, 128), BF16),
            pltpu.VMEM((3, 9, 16, 128), BF16),
            pltpu.VMEM((3, 9, 16, 128), BF16),
            pltpu.VMEM((3, 9, 16, 128), BF16),
            pltpu.VMEM((3, 3, 9, 16, 128), BF16),
            pltpu.VMEM((2, 9, 16, 128), F32),
            pltpu.VMEM((2, 9, 16, 128), F32),
            dma((2, 2)),
            dma((2, 2)),
            dma((2,)),
            dma((2,)),
            dma((2,)),
            dma((2,)),
            dma((2, 2)),
            dma((2, 2)),
            dma((3, 2)),
            dma((3, 3)),
            dma((3, 3)),
            dma((2, 2)),
            dma((6,)),
        ],
        compiler_params=pltpu.CompilerParams(
            collective_id=0, has_side_effects=True, vmem_limit_bytes=48 * 1024 * 1024
        ),
    )(*(pltpu.with_memory_space_constraint(x, pltpu.HBM) for x in (partner[None, :], volume, cotangent, kernels)))
    return grad_volume, kg.reshape(1, 3, 27, CH * CH)


def solution(mesh):
    crops = mesh.shape["sample"]
    in_specs = (P("sample", "depth", None, None), P(), P(), P("sample", "depth", None, None))
    out_specs = (P("sample", "depth", None, None), P("sample", None, None, None))
    return jax.shard_map(
        functools.partial(per_device, crops),
        mesh=mesh,
        in_specs=in_specs,
        out_specs=out_specs,
        check_vma=False,
    )
```

```python
import functools

import jax
import jax.numpy as jnp
from jax import lax
from jax.experimental import pallas as pl
from jax.experimental.pallas import tpu as pltpu
from jax.sharding import PartitionSpec as P

CH = 32
OWN_SHARE = 0.6
PARTNER_SHARE = 0.4
MESH = pl.DeviceIdType.MESH
F32 = jnp.float32
BF16 = jnp.bfloat16
ROWS = 256
LANES = 256
LAYER = 64
NT = (((1,), (1,)), ((), ()))
TN = (((0,), (0,)), ((), ()))


def logistic(v):
    return 0.5 * jnp.tanh(0.5 * v) + 0.5


def block_transpose(y):
    sub = lax.broadcasted_iota(jnp.int32, y.shape, 1) % 4
    blk = lax.broadcasted_iota(jnp.int32, y.shape, 2) // 32
    delta = sub - blk
    turned = [y] + [pltpu.roll(y, 128 - 32 * m, 2) for m in (1, 2, 3)]
    out = y
    for m in (1, 2, 3):
        out = jnp.where(delta == m, pltpu.roll(turned[m], m, 1), out)
        out = jnp.where(delta == m - 4, pltpu.roll(turned[m], m + 4, 1), out)
    return out


def to_rows(v):
    even = jnp.stack([v[:, 256 * t : 256 * t + 128] for t in range(8)])
    odd = jnp.stack([v[:, 256 * t + 128 : 256 * t + 256] for t in range(8)])
    first = lax.broadcasted_iota(jnp.int32, even.shape, 1) < 4
    y0 = jnp.where(first, even, pltpu.roll(odd, 4, 1))
    y1 = jnp.where(first, pltpu.roll(even, 4, 1), odd)
    return jnp.concatenate(
        [block_transpose(y0).reshape(64, 128), block_transpose(y1).reshape(64, 128)], axis=1
    )


def from_rows(r):
    y0 = block_transpose(r[:, :128].reshape(8, 8, 128))
    y1 = block_transpose(r[:, 128:].reshape(8, 8, 128))
    first = lax.broadcasted_iota(jnp.int32, y0.shape, 1) < 4
    even = jnp.where(first, y0, pltpu.roll(y1, 4, 1))
    odd = jnp.where(first, pltpu.roll(y0, 4, 1), y1)
    return jnp.concatenate([part[t] for t in range(8) for part in (even, odd)], axis=1)


def width_index(shape):
    return lax.broadcasted_iota(jnp.int32, shape, 0) % LAYER


def from_left(x):
    return jnp.where(width_index(x.shape) == 0, 0.0, pltpu.roll(x, 1, 0))


def from_right(x):
    return jnp.where(width_index(x.shape) == LAYER - 1, 0.0, pltpu.roll(x, x.shape[0] - 1, 0))


def kernel(
    crops,
    partner_hbm,
    vol_hbm,
    cot_hbm,
    kern_hbm,
    gvol,
    kg,
    partner,
    partner_row,
    inverse_rows,
    inverse,
    vol,
    cot,
    kern,
    kf,
    fwd_w,
    bwd_w,
    ext,
    wide,
    slope1,
    slope2,
    part,
    pieces_out,
    pieces_in,
    mixed_out,
    mixed_in,
    far_in,
    near_in,
    kg_send,
    kg_recv,
    kg_pair,
    kg_all,
    kg_sum,
    kg_shared,
    halo_send,
    halo_recv,
    cot_send,
    cot_recv,
    far_sems,
    near_sems,
    a2a_send,
    a2a_recv,
    pair_sems,
    all_send,
    all_recv,
    share_sems,
    load_sems,
):
    loads = [
        pltpu.make_async_copy(source, target, load_sems.at[k])
        for k, (source, target) in enumerate(
            (
                (vol_hbm, vol),
                (kern_hbm, kern),
                (partner_hbm, partner_row),
                (partner_hbm, partner),
                (cot_hbm, cot),
            )
        )
    ]
    turn = pltpu.make_async_copy(inverse_rows, inverse, load_sems.at[5])
    for load in loads:
        load.start()
    me = lax.axis_index("sample")
    d = lax.axis_index("depth")
    core = lax.rem(d, 2)
    mate = d + 1 - 2 * core
    far = lax.rem(d + 2, 4)
    far_mate = lax.rem(mate + 2, 4)

    z = me // 16
    mid = (z == 1) | (z == 2)
    middle = (d == 1) | (d == 2)
    mid_count = lax.rem((z + 1) // 2, 2)
    slot_here = me - 16
    ys = [lax.rem(me + 2 + k, 4) for k in range(4)]
    xs_far = me // 4 + 2

    def peers_of(zt, send, skip_own):
        @pl.loop(0, 4)
        def _(k):
            row = 16 * zt + 4 * lax.rem(xs_far + k, 4)
            for at, y in enumerate(ys):
                if skip_own and at == 2:

                    @pl.when((k != 2) | (zt != z))
                    def _():
                        send(row + y)
                else:
                    send(row + y)

    mids_first = 1 + mid_count * (2 - z) + (1 - mid_count) * (1 - z // 3)
    mid_order = (mids_first, 3 - mids_first)
    edge = 3 * (2 - z)
    all_order = (edge, 3 - edge, 3 - z, z)
    far_order = (z, 3 - z, 3 - edge, edge)

    barrier = pltpu.get_barrier_semaphore()

    def greet(depth):
        def signal(peer):
            pl.semaphore_signal(barrier, inc=1, device_id=(peer, depth), device_id_type=MESH)

        return signal

    for zt in mid_order:
        peers_of(zt, greet(d), True)

    @pl.when(mid)
    def _():
        for zt in (0, 3):
            peers_of(zt, greet(d), False)

    for k in (1, 2, 3):
        pl.semaphore_signal(
            barrier, inc=1, device_id=(me, lax.rem(d + k, 4)), device_id_type=MESH
        )

    loads[0].wait()
    for layer in range(4):
        ext[0, LAYER * (layer + 1) : LAYER * (layer + 2), :] = to_rows(
            vol[0, layer].astype(F32)
        ).astype(BF16)

    @pl.when(d == 0)
    def _():
        for k in range(2):
            ext[k, 0:LAYER, :] = jnp.zeros((LAYER, LANES), BF16)
        wide[0, 0 : 4 * LAYER, :] = jnp.zeros((4 * LAYER, LANES), BF16)

    @pl.when(d == 3)
    def _():
        for k in range(2):
            ext[k, 5 * LAYER : 6 * LAYER, :] = jnp.zeros((LAYER, LANES), BF16)
        wide[0, 8 * LAYER : 12 * LAYER, :] = jnp.zeros((4 * LAYER, LANES), BF16)

    loads[1].wait()
    for l in range(3):
        kf[l] = kern[l].astype(F32)

    sub = lax.broadcasted_iota(jnp.int32, (8, 128), 0)
    blk8 = lax.broadcasted_iota(jnp.int32, (8, 128), 1) // 32
    sub32 = lax.broadcasted_iota(jnp.int32, (32, 128), 0) % 4
    blk32 = lax.broadcasted_iota(jnp.int32, (32, 128), 1) // 32

    first_rows = (
        lax.broadcasted_iota(jnp.int32, (32, 128), 0) == lax.broadcasted_iota(jnp.int32, (32, 128), 1)
    ).astype(F32).astype(BF16)
    diagonal = [(sub32 == q) & (blk32 == q) for q in range(4)]

    def tap_tiles(l, a, c):
        taps = []
        for b in range(3):
            row = kf[l, pl.ds(9 * a + 3 * b + c, 1), :]
            tiles = []
            for r in range(4):
                low = jnp.broadcast_to(row[:, 256 * r : 256 * r + 128], (8, 128))
                high = jnp.broadcast_to(row[:, 256 * r + 128 : 256 * r + 256], (8, 128))
                z = jnp.where(blk8 == sub % 4, jnp.where(sub < 4, low, high), 0.0)
                z = z + pltpu.roll(z, 64, 1)
                tiles.append(z + pltpu.roll(z, 32, 1))
            taps.append(jnp.concatenate(tiles, axis=0))
        return taps

    def store_blocks(target, l, a, c, taps, step):
        row0 = pl.multiple_of(a * 256, 256)
        for hp in range(8):
            for j in range(2):
                block = jnp.zeros((32, 128), F32)
                for b in range(3):
                    h = hp + step * (b - 1)
                    if h // 4 == j and 0 <= h < 8:
                        block = jnp.where(blk32 == h % 4, taps[b], block)
                rows = pl.ds(pl.multiple_of(row0 + 32 * hp, 32), 32)
                target[l, c, rows, 128 * j : 128 * j + 128] = block.astype(BF16)

    def build(l, forward, backward):
        @pl.loop(0, 3)
        def _(a):
            for c in range(3):
                taps = tap_tiles(l, a, c)
                if forward:
                    store_blocks(fwd_w, l, a, c, taps, -1)
                if backward:
                    stacked = jnp.concatenate([tap for tap in taps for _ in range(4)], axis=0)
                    back = lax.dot_general(
                        first_rows, stacked.astype(BF16), NT, preferred_element_type=F32
                    )
                    store_blocks(
                        bwd_w, l, a, c, [back[:, 128 * b : 128 * b + 128] for b in range(3)], 1
                    )

    def at_rows(s, n):
        start = LAYER * s
        if not isinstance(s, int):
            start = pl.multiple_of(start, LAYER)
        return pl.ds(start, LAYER * n)

    def taps_of(lhs, l, forward):
        weights = fwd_w if forward else bwd_w
        outs = [jnp.dot(lhs, weights[l, c], preferred_element_type=F32) for c in range(3)]
        if forward:
            return outs[1] + from_left(outs[0]) + from_right(outs[2])
        return outs[1] + from_right(outs[0]) + from_left(outs[2])

    def conv(x, l, s, n, forward):
        shifts = (-1, 0, 1) if forward else (1, 0, -1)
        lhs = jnp.concatenate([x[at_rows(s + shift, n), :] for shift in shifts], axis=1)
        return taps_of(lhs, l, forward)

    def conv_ranges(x, l, ranges, forward):
        shifts = (-1, 0, 1) if forward else (1, 0, -1)
        lhs = [
            jnp.concatenate(
                [x[LAYER * (s + shift) : LAYER * (t + shift), :] for s, t in ranges], axis=0
            )
            for shift in shifts
        ]
        return taps_of(jnp.concatenate(lhs, axis=1), l, forward)

    def masked(values, s):
        parts = []
        n = values.shape[0] // LAYER
        for k in range(n):
            piece = values[LAYER * k : LAYER * (k + 1)]
            if s + k < 4:
                piece = jnp.where(d > 0, piece, 0.0)
            elif s + k >= 8:
                piece = jnp.where(d < 3, piece, 0.0)
            parts.append(piece)
        return jnp.concatenate(parts, axis=0)

    def halo_copies(x):
        low = pltpu.make_async_remote_copy(
            src_ref=ext.at[x, pl.ds(LAYER, LAYER), :],
            dst_ref=ext.at[x, pl.ds(5 * LAYER, LAYER), :],
            send_sem=halo_send.at[x, 0],
            recv_sem=halo_recv.at[x, 1],
            device_id=(me, lax.rem(d + 3, 4)),
            device_id_type=MESH,
        )
        high = pltpu.make_async_remote_copy(
            src_ref=ext.at[x, pl.ds(4 * LAYER, LAYER), :],
            dst_ref=ext.at[x, pl.ds(0, LAYER), :],
            send_sem=halo_send.at[x, 1],
            recv_sem=halo_recv.at[x, 0],
            device_id=(me, lax.rem(d + 1, 4)),
            device_id_type=MESH,
        )
        return low, high

    def halo_start(x):
        low, high = halo_copies(x)

        @pl.when(d > 0)
        def _():
            low.start()

        @pl.when(d < 3)
        def _():
            high.start()

    def halo_wait(x):
        low, high = halo_copies(x)

        @pl.when(d > 0)
        def _():
            low.wait_send()
            high.wait_recv()

        @pl.when(d < 3)
        def _():
            high.wait_send()
            low.wait_recv()

    def fill_pieces(slot, values, rows_from):
        n = values.shape[0] // 16
        at = rows_from // 16
        for j in range(2):
            pieces_out[slot, 16 * j + at : 16 * j + at + n] = (
                values[:, 128 * j : 128 * j + 128].astype(BF16).reshape(n, 16, 128)
            )

    def cot_copies():
        low = pltpu.make_async_remote_copy(
            src_ref=wide.at[4, pl.ds(4 * LAYER, 2 * LAYER), :],
            dst_ref=wide.at[4, pl.ds(8 * LAYER, 2 * LAYER), :],
            send_sem=cot_send.at[0],
            recv_sem=cot_recv.at[1],
            device_id=(me, lax.rem(d + 3, 4)),
            device_id_type=MESH,
        )
        high = pltpu.make_async_remote_copy(
            src_ref=wide.at[4, pl.ds(6 * LAYER, 2 * LAYER), :],
            dst_ref=wide.at[4, pl.ds(2 * LAYER, 2 * LAYER), :],
            send_sem=cot_send.at[1],
            recv_sem=cot_recv.at[0],
            device_id=(me, lax.rem(d + 1, 4)),
            device_id_type=MESH,
        )
        return low, high

    def first_copy(slot, source, target, to):
        return pltpu.make_async_remote_copy(
            src_ref=source,
            dst_ref=target,
            send_sem=a2a_send.at[slot, 0],
            recv_sem=a2a_recv.at[slot, 0],
            device_id=(to, d),
            device_id_type=MESH,
        )

    def scatter_start(slot):
        def send(peer):
            first_copy(slot, pieces_out.at[slot, peer - 16], pieces_in.at[slot, me], peer).start()

        for zt in mid_order:
            peers_of(zt, send, True)

        @pl.when(mid)
        def _():
            pieces_in[slot, me] = pieces_out[slot, slot_here]

    def scatter_wait(slot):
        @pl.when(mid)
        def _():
            span = pieces_in.at[slot, pl.ds(0, 31)]
            first_copy(slot, pieces_out.at[slot, pl.ds(0, 31)], span, me).wait_send()
            span = pieces_in.at[slot, pl.ds(0, crops - 1)]
            first_copy(slot, span, span, me).wait_recv()

        @pl.when(jnp.logical_not(mid))
        def _():
            span = pieces_in.at[slot, pl.ds(0, 32)]
            first_copy(slot, pieces_out.at[slot], span, me).wait_send()

    def second_copy(slot, source, target, to):
        return pltpu.make_async_remote_copy(
            src_ref=source,
            dst_ref=target,
            send_sem=a2a_send.at[slot, 1],
            recv_sem=a2a_recv.at[slot, 1],
            device_id=(to, d),
            device_id_type=MESH,
        )

    def gather_start(slot):
        def send(peer):
            second_copy(
                slot, mixed_out.at[slot, peer], mixed_in.at[slot, slot_here], peer
            ).start()

        for zt in all_order:
            peers_of(zt, send, True)
        mixed_in[slot, slot_here] = mixed_out[slot, me]

    def gather_wait(slot):
        @pl.when(mid)
        def _():
            span = mixed_out.at[slot, pl.ds(0, crops - 1)]
            second_copy(slot, span, span, me).wait_send()
            span = mixed_in.at[slot, pl.ds(0, 31)]
            second_copy(slot, span, span, me).wait_recv()

        @pl.when(jnp.logical_not(mid))
        def _():
            span = mixed_in.at[slot]
            second_copy(slot, span, span, me).wait_recv()

    def far_copy(source, target, to):
        return pltpu.make_async_remote_copy(
            src_ref=source,
            dst_ref=target,
            send_sem=far_sems.at[0],
            recv_sem=far_sems.at[1],
            device_id=(to, 3 - d),
            device_id_type=MESH,
        )

    def far_start():
        @pl.when(middle)
        def _():
            def send(peer):
                far_copy(mixed_out.at[0, peer], far_in.at[slot_here], peer).start()

            for zt in far_order:
                peers_of(zt, send, False)

    def far_wait():
        @pl.when(middle)
        def _():
            @pl.when(mid)
            def _():
                far_copy(mixed_out.at[0], mixed_out.at[0], me).wait_send()

            far_copy(far_in, far_in, me).wait_recv()

    def near_copy():
        return pltpu.make_async_remote_copy(
            src_ref=mixed_in.at[0],
            dst_ref=near_in,
            send_sem=near_sems.at[0],
            recv_sem=near_sems.at[1],
            device_id=(me, mate),
            device_id_type=MESH,
        )

    def joined(pieces):
        return jnp.concatenate(
            [pieces[0:16].reshape(ROWS, 128), pieces[16:32].reshape(ROWS, 128)], axis=1
        )

    def kernel_grad(l, x, first, g):
        stacked = jnp.concatenate(
            [from_right(g).astype(BF16), g.astype(BF16), from_left(g).astype(BF16)], axis=1
        )
        totals = []
        for a in range(3):
            u = x[LAYER * (first + a) : LAYER * (first + a) + ROWS, :]
            for c in range(3):
                r = lax.dot_general(
                    u, stacked[:, 256 * c : 256 * c + 256], TN, preferred_element_type=F32
                )

                def at(hp, j):
                    return r[32 * hp : 32 * hp + 32, 128 * j : 128 * j + 128]

                g0 = at(1, 0) + at(5, 1)
                g1 = at(2, 0) + at(6, 1)
                g2 = jnp.where(blk32 >= 2, at(3, 0) + at(7, 1), at(3, 1))
                g3 = jnp.where(blk32 == 3, at(4, 0), at(4, 1) + jnp.where(blk32 < 2, at(0, 0), 0.0))
                total = (
                    g0 + pltpu.roll(g1, 96, 1) + pltpu.roll(g2, 64, 1) + pltpu.roll(g3, 32, 1)
                )
                totals.append(total)
        for k in range(6):
            extra = pltpu.roll(totals[6 + k // 3], 32 * (3 - k % 3), 1)
            packed = jnp.where(blk32 == 3, extra, totals[k])
            part[l, 0, k] = packed[0:16]
            part[l, 1, k] = packed[16:32]
        part[l, 0, 6] = totals[8][0:16]
        part[l, 1, 6] = totals[8][16:32]
        kg_send[l] = part[l, 1 - core].astype(BF16)

    def pair_copy(l):
        return pltpu.make_async_remote_copy(
            src_ref=kg_send.at[l],
            dst_ref=kg_recv.at[l],
            send_sem=pair_sems.at[l, 0],
            recv_sem=pair_sems.at[l, 1],
            device_id=(me, mate),
            device_id_type=MESH,
        )

    def all_copies(l):
        return [
            pltpu.make_async_remote_copy(
                src_ref=kg_pair.at[l],
                dst_ref=kg_all.at[l, k],
                send_sem=all_send.at[l, k],
                recv_sem=all_recv.at[l, k],
                device_id=(me, to),
                device_id_type=MESH,
            )
            for k, to in enumerate((mate, far, far_mate))
        ]

    def pair_sum(l):
        pair_copy(l).wait()
        kg_pair[l] = (part[l, core] + kg_recv[l].astype(F32)).astype(BF16)

    def reduce_pairs(l):
        pair_sum(l)
        for copy in all_copies(l):
            copy.start()

    def reduce_finish(l):
        for copy in all_copies(l):
            copy.wait()
        own = kg_pair[l].astype(F32) + kg_all[l, 1].astype(F32)
        other = kg_all[l, 0].astype(F32) + kg_all[l, 2].astype(F32)
        store_grads(l, own, other)

    def share_copy(l):
        return pltpu.make_async_remote_copy(
            src_ref=kg_sum.at[l - 1],
            dst_ref=kg_shared.at[l - 1],
            send_sem=share_sems.at[l - 1, 0],
            recv_sem=share_sems.at[l - 1, 1],
            device_id=(me, mate),
            device_id_type=MESH,
        )

    def reduce_share(l):
        all_copies(l)[1].wait()
        kg_sum[l - 1] = kg_pair[l].astype(F32) + kg_all[l, 1].astype(F32)
        share_copy(l).start()

    def share_finish(l):
        share_copy(l).wait()
        store_grads(l, kg_sum[l - 1], kg_shared[l - 1])

    def store_grads(l, own, other):
        tiles = [
            jnp.concatenate(
                [
                    jnp.where(core == 0, own[k], other[k]),
                    jnp.where(core == 0, other[k], own[k]),
                ],
                axis=0,
            )
            for k in range(7)
        ]
        terms = tiles[:6]
        for k in (0, 3):
            term = pltpu.roll(tiles[k], 32, 1)
            for m in (1, 2):
                term = jnp.where(blk32 == m, pltpu.roll(tiles[k + m], 32 * (m + 1), 1), term)
            terms.append(term)
        terms.append(tiles[6])
        for a in range(3):
            for c in range(3):
                x = terms[3 * a + c]
                turned = [x] + [pltpu.roll(x, 32 * m, 1) for m in (1, 2, 3)]
                for b in range(3):
                    z = jnp.zeros_like(x)
                    for q in range(4):
                        z = jnp.where(diagonal[q], turned[(q - 2 + b) % 4], z)
                    z = z.reshape(4, 8, 128)
                    z = z + pltpu.roll(z, 7, 1)
                    z = z + pltpu.roll(z, 6, 1)
                    t = 27 * l + 9 * a + 3 * b + c
                    for r in range(4):
                        kg[t, 2 * r : 2 * r + 1, :] = z[r, 0:1, :]
                        kg[t, 2 * r + 1 : 2 * r + 2, :] = z[r, 4:5, :]

    build(0, True, False)
    for load in loads[2:4]:
        load.wait()
    shape = (crops, crops)
    named = partner_row[...] == lax.broadcasted_iota(jnp.int32, shape, 0)
    found = jnp.where(named, lax.broadcasted_iota(jnp.int32, shape, 1), 0)
    inverse_rows[...] = jnp.broadcast_to(
        jnp.minimum(jnp.sum(found, axis=1, keepdims=True, dtype=jnp.int32), crops - 1),
        (crops, 128),
    )
    turn.start()
    pl.semaphore_wait(barrier, 35 + 31 * mid_count)

    xv, g1 = ext.at[0], ext.at[1]
    xb, xs, g3, g2, cotr = (wide.at[k] for k in range(5))

    halo_start(0)

    def first_layer(ranges):
        v = conv_ranges(xv, 0, ranges, True)
        s = logistic(v)
        hidden = v * s
        slope = s * (1.0 + v * (1.0 - s))
        at = 0
        for first, last in ranges:
            n = LAYER * (last - first)
            slope1[LAYER * (first - 1) : LAYER * (last - 1), :] = slope[at : at + n]
            fill_pieces(0, hidden[at : at + n], LAYER * (first - 1))
            at += n

    first_layer(((2, 4),))
    loads[4].wait()
    for layer in range(4):
        cotr[LAYER * (layer + 4) : LAYER * (layer + 5), :] = to_rows(
            cot[0, layer].astype(F32)
        ).astype(BF16)
    build(1, True, False)
    halo_wait(0)
    first_layer(((1, 2), (4, 5)))

    scatter_start(0)
    cot_low, cot_high = cot_copies()

    @pl.when(d > 0)
    def _():
        cot_low.start()

    @pl.when(d < 3)
    def _():
        cot_high.start()

    build(2, True, True)
    scatter_wait(0)

    def mix(slot, other_of):
        def step(n, carry):
            own = pieces_in[slot, n].astype(F32)
            other = pieces_in[slot, other_of(n)].astype(F32)
            mixed_out[slot, n] = (OWN_SHARE * own + PARTNER_SHARE * other).astype(BF16)
            return carry

        lax.fori_loop(0, crops, step, 0, unroll=8)

    @pl.when(mid)
    def _():
        mix(0, lambda n: partner[0, n])
        far_start()
        gather_start(0)

    build(1, False, True)
    build(0, False, True)
    gather_wait(0)
    near_copy().start()
    xb[4 * LAYER : 8 * LAYER, :] = joined(mixed_in[0])

    def far_masked(values):
        parts = []
        for k in range(4):
            piece = values[LAYER * k : LAYER * (k + 1)]
            if k == 0:
                keep = middle | (core == 1)
            elif k == 3:
                keep = middle | (core == 0)
            else:
                keep = middle
            parts.append(jnp.where(keep, piece, 0.0))
        return jnp.concatenate(parts, axis=0)

    def second_layer(s, n, mask):
        v = conv(xb, 1, s, n, True)
        gate = logistic(v)
        second = v * gate
        rows = at_rows(s, n)
        xs[rows, :] = (far_masked(second) if mask else second).astype(BF16)
        slope2[rows, :] = gate * (1.0 + v * (1.0 - gate))

    second_layer(5, 2, False)
    far_wait()

    @pl.when(middle)
    def _():
        xb[pl.ds(pl.multiple_of(512 * core, 512), 256), :] = joined(far_in[...])

    second_layer(1 + 6 * core, 4, True)

    @pl.when(d > 0)
    def _():
        cot_low.wait_send()
        cot_high.wait_recv()

    @pl.when(d < 3)
    def _():
        cot_high.wait_send()
        cot_low.wait_recv()

    def third_layer(s, far_side):
        v = conv(xs, 2, s, 4, True)
        gate = logistic(v)
        slope = gate * (1.0 + v * (1.0 - gate))
        rows = at_rows(s, 4)
        values = cotr[rows, :].astype(F32) * slope
        if far_side:
            parts = []
            for k in range(4):
                piece = values[LAYER * k : LAYER * (k + 1)]
                keep = middle | ((core == 1) if k < 2 else (core == 0))
                parts.append(jnp.where(keep, piece, 0.0))
            values = jnp.concatenate(parts, axis=0)
        g3[rows, :] = values.astype(BF16)

    third_layer(2 + 4 * core, True)
    near_copy().wait()
    xb[pl.ds(pl.multiple_of(512 * (1 - core), 512), 256), :] = joined(near_in[...])
    second_layer(7 - 6 * core, 4, False)
    third_layer(6 - 4 * core, False)

    def back_three(s, n):
        g = conv(g3, 2, s, n, False) * slope2[LAYER * s : LAYER * (s + n), :]
        g2[LAYER * s : LAYER * (s + n), :] = masked(g, s).astype(BF16)

    back_three(3, 3)
    back_three(6, 3)
    fill_pieces(1, conv(g2, 1, 4, 4, False), 0)
    scatter_start(1)
    kernel_grad(2, xs, 3, g3[4 * LAYER : 8 * LAYER, :].astype(F32))
    pair_copy(2).start()
    kernel_grad(1, xb, 3, g2[4 * LAYER : 8 * LAYER, :].astype(F32))
    pair_copy(1).start()
    pair_sum(2)
    all_copies(2)[1].start()
    pair_sum(1)
    all_copies(1)[1].start()
    turn.wait()
    scatter_wait(1)

    @pl.when(mid)
    def _():
        mix(1, lambda n: inverse[n, 0])
        gather_start(1)

    reduce_share(2)
    reduce_share(1)
    share_finish(2)
    share_finish(1)
    gather_wait(1)

    g_one = (joined(mixed_in[1]).astype(F32) * slope1[...]).astype(BF16)
    g1[LAYER : 5 * LAYER, :] = g_one
    halo_start(1)
    kernel_grad(0, xv, 0, g_one.astype(F32))
    pair_copy(0).start()
    g = conv(g1, 0, 2, 2, False)
    gvol[0, 1] = from_rows(g[0:LAYER]).astype(BF16)
    gvol[0, 2] = from_rows(g[LAYER:]).astype(BF16)
    reduce_pairs(0)
    halo_wait(1)
    g = conv_ranges(g1, 0, ((1, 2), (4, 5)), False)
    gvol[0, 0] = from_rows(g[0:LAYER]).astype(BF16)
    gvol[0, 3] = from_rows(g[LAYER:]).astype(BF16)
    reduce_finish(0)


def per_device(crops, volume, kernels, partner, cotangent):
    vmem = pl.BlockSpec(memory_space=pltpu.VMEM)
    hbm = pl.BlockSpec(memory_space=pltpu.HBM)
    dma = pltpu.SemaphoreType.DMA
    grad_volume, kg = pl.pallas_call(
        functools.partial(kernel, crops),
        out_shape=(
            jax.ShapeDtypeStruct((1, 4, 8, 2048), BF16),
            jax.ShapeDtypeStruct((81, 8, 128), F32),
        ),
        in_specs=[hbm] * 4,
        out_specs=(vmem, vmem),
        scratch_shapes=[
            pltpu.SMEM((1, crops), jnp.int32),
            pltpu.VMEM((1, crops), jnp.int32),
            pltpu.VMEM((crops, 128), jnp.int32),
            pltpu.SMEM((crops, 128), jnp.int32),
            pltpu.VMEM((1, 4, 8, 2048), BF16),
            pltpu.VMEM((1, 4, 8, 2048), BF16),
            pltpu.VMEM((3, 27, 1024), BF16),
            pltpu.VMEM((3, 27, 1024), F32),
            pltpu.VMEM((3, 3, 768, 256), BF16),
            pltpu.VMEM((3, 3, 768, 256), BF16),
            pltpu.VMEM((2, 384, 256), BF16),
            pltpu.VMEM((5, 768, 256), BF16),
            pltpu.VMEM((256, 256), F32),
            pltpu.VMEM((768, 256), F32),
            pltpu.VMEM((3, 2, 7, 16, 128), F32),
            pltpu.VMEM((2, 32, 16, 128), BF16),
            pltpu.VMEM((2, crops, 16, 128), BF16),
            pltpu.VMEM((2, crops, 16, 128), BF16),
            pltpu.VMEM((2, 32, 16, 128), BF16),
            pltpu.VMEM((32, 16, 128), BF16),
            pltpu.VMEM((32, 16, 128), BF16),
            pltpu.VMEM((3, 7, 16, 128), BF16),
            pltpu.VMEM((3, 7, 16, 128), BF16),
            pltpu.VMEM((3, 7, 16, 128), BF16),
            pltpu.VMEM((3, 3, 7, 16, 128), BF16),
            pltpu.VMEM((2, 7, 16, 128), F32),
            pltpu.VMEM((2, 7, 16, 128), F32),
            dma((2, 2)),
            dma((2, 2)),
            dma((2,)),
            dma((2,)),
            dma((2,)),
            dma((2,)),
            dma((2, 2)),
            dma((2, 2)),
            dma((3, 2)),
            dma((3, 3)),
            dma((3, 3)),
            dma((2, 2)),
            dma((6,)),
        ],
        compiler_params=pltpu.CompilerParams(
            collective_id=0, has_side_effects=True, vmem_limit_bytes=48 * 1024 * 1024
        ),
    )(*(pltpu.with_memory_space_constraint(x, pltpu.HBM) for x in (partner[None, :], volume, cotangent, kernels)))
    return grad_volume, kg.reshape(1, 3, 27, CH * CH)


def solution(mesh):
    crops = mesh.shape["sample"]
    in_specs = (P("sample", "depth", None, None), P(), P(), P("sample", "depth", None, None))
    out_specs = (P("sample", "depth", None, None), P("sample", None, None, None))
    return jax.shard_map(
        functools.partial(per_device, crops),
        mesh=mesh,
        in_specs=in_specs,
        out_specs=out_specs,
        check_vma=False,
    )
```

```python
import functools

import jax
import jax.numpy as jnp
from jax import lax
from jax.experimental import pallas as pl
from jax.experimental.pallas import tpu as pltpu
from jax.sharding import PartitionSpec as P

CH = 32
OWN_SHARE = 0.6
PARTNER_SHARE = 0.4
MESH = pl.DeviceIdType.MESH
F32 = jnp.float32
BF16 = jnp.bfloat16
ROWS = 256
LANES = 256
LAYER = 64
NT = (((1,), (1,)), ((), ()))
TN = (((0,), (0,)), ((), ()))


def logistic(v):
    return 0.5 * jnp.tanh(0.5 * v) + 0.5


def block_transpose(y):
    sub = lax.broadcasted_iota(jnp.int32, y.shape, 1) % 4
    blk = lax.broadcasted_iota(jnp.int32, y.shape, 2) // 32
    delta = sub - blk
    turned = [y] + [pltpu.roll(y, 128 - 32 * m, 2) for m in (1, 2, 3)]
    out = y
    for m in (1, 2, 3):
        out = jnp.where(delta == m, pltpu.roll(turned[m], m, 1), out)
        out = jnp.where(delta == m - 4, pltpu.roll(turned[m], m + 4, 1), out)
    return out


def to_rows(v):
    even = jnp.stack([v[:, 256 * t : 256 * t + 128] for t in range(8)])
    odd = jnp.stack([v[:, 256 * t + 128 : 256 * t + 256] for t in range(8)])
    first = lax.broadcasted_iota(jnp.int32, even.shape, 1) < 4
    y0 = jnp.where(first, even, pltpu.roll(odd, 4, 1))
    y1 = jnp.where(first, pltpu.roll(even, 4, 1), odd)
    return jnp.concatenate(
        [block_transpose(y0).reshape(64, 128), block_transpose(y1).reshape(64, 128)], axis=1
    )


def from_rows(r):
    y0 = block_transpose(r[:, :128].reshape(8, 8, 128))
    y1 = block_transpose(r[:, 128:].reshape(8, 8, 128))
    first = lax.broadcasted_iota(jnp.int32, y0.shape, 1) < 4
    even = jnp.where(first, y0, pltpu.roll(y1, 4, 1))
    odd = jnp.where(first, pltpu.roll(y0, 4, 1), y1)
    return jnp.concatenate([part[t] for t in range(8) for part in (even, odd)], axis=1)


def width_index(shape):
    return lax.broadcasted_iota(jnp.int32, shape, 0) % LAYER


def from_left(x):
    return jnp.where(width_index(x.shape) == 0, 0.0, pltpu.roll(x, 1, 0))


def from_right(x):
    return jnp.where(width_index(x.shape) == LAYER - 1, 0.0, pltpu.roll(x, x.shape[0] - 1, 0))


def kernel(
    crops,
    partner_hbm,
    vol_hbm,
    cot_hbm,
    kern_hbm,
    gvol,
    kg,
    partner,
    partner_row,
    inverse_rows,
    inverse,
    vol,
    cot,
    kern,
    kf,
    fwd_w,
    bwd_w,
    ext,
    wide,
    slope1,
    slope2,
    part,
    pieces_out,
    pieces_in,
    mixed_out,
    mixed_in,
    far_in,
    near_in,
    kg_send,
    kg_recv,
    kg_pair,
    kg_all,
    kg_sum,
    kg_shared,
    halo_send,
    halo_recv,
    cot_send,
    cot_recv,
    far_sems,
    near_sems,
    a2a_send,
    a2a_recv,
    pair_sems,
    all_send,
    all_recv,
    share_sems,
    load_sems,
    levels,
):
    loads = [
        pltpu.make_async_copy(source, target, load_sems.at[k])
        for k, (source, target) in enumerate(
            (
                (vol_hbm, vol),
                (kern_hbm, kern),
                (partner_hbm, partner_row),
                (partner_hbm, partner),
                (cot_hbm, cot),
            )
        )
    ]
    turn = pltpu.make_async_copy(inverse_rows, inverse, load_sems.at[5])
    for load in loads:
        load.start()
    me = lax.axis_index("sample")
    d = lax.axis_index("depth")
    core = lax.rem(d, 2)
    mate = d + 1 - 2 * core
    far = lax.rem(d + 2, 4)
    far_mate = lax.rem(mate + 2, 4)

    z = me // 16
    mid = (z == 1) | (z == 2)
    middle = (d == 1) | (d == 2)
    mid_count = lax.rem((z + 1) // 2, 2)
    slot_here = me - 16
    ys = [lax.rem(me + 2 + k, 4) for k in range(4)]
    xs_far = me // 4 + 2

    def peers_of(zts, send, skip_own):
        @pl.loop(0, 4)
        def _(k):
            row = 4 * lax.rem(xs_far + k, 4)
            for at, y in enumerate(ys):
                for zt in zts:
                    if skip_own and at == 2:

                        @pl.when((k != 2) | (zt != z))
                        def _():
                            send(16 * zt + row + y)
                    else:
                        send(16 * zt + row + y)

    mids_first = 1 + mid_count * (2 - z) + (1 - mid_count) * (1 - z // 3)
    mid_order = (mids_first, 3 - mids_first)
    edge = 3 * (2 - z)
    all_order = (edge, 3 - edge, 3 - z, z)
    far_order = (z, 3 - z, 3 - edge, edge)

    barrier = pltpu.get_barrier_semaphore()

    x_line = [16 * z + 4 * lax.rem(me // 4 + k, 4) + lax.rem(me, 4) for k in (1, 2, 3)]
    y_line = [4 * (me // 4) + lax.rem(me + k, 4) for k in (1, 2, 3)]
    z_line = [16 * lax.rem(z + k, 4) + lax.rem(me, 16) for k in (2, 1, 3)]
    for k in (2, 3, 1):
        pl.semaphore_signal(
            barrier, inc=1, device_id=(me, lax.rem(d + k, 4)), device_id_type=MESH
        )
    for peer in z_line + x_line + y_line:
        pl.semaphore_signal(barrier, inc=1, device_id=(peer, d), device_id_type=MESH)

    def tell(level, peers):
        for peer in peers:
            pl.semaphore_signal(
                levels.at[level], inc=1, device_id=(peer, d), device_id_type=MESH
            )

    loads[0].wait()
    for layer in range(4):
        ext[0, LAYER * (layer + 1) : LAYER * (layer + 2), :] = to_rows(
            vol[0, layer].astype(F32)
        ).astype(BF16)

    @pl.when(d == 0)
    def _():
        for k in range(2):
            ext[k, 0:LAYER, :] = jnp.zeros((LAYER, LANES), BF16)
        wide[0, 0 : 4 * LAYER, :] = jnp.zeros((4 * LAYER, LANES), BF16)

    @pl.when(d == 3)
    def _():
        for k in range(2):
            ext[k, 5 * LAYER : 6 * LAYER, :] = jnp.zeros((LAYER, LANES), BF16)
        wide[0, 8 * LAYER : 12 * LAYER, :] = jnp.zeros((4 * LAYER, LANES), BF16)


    sub = lax.broadcasted_iota(jnp.int32, (8, 128), 0)
    blk8 = lax.broadcasted_iota(jnp.int32, (8, 128), 1) // 32
    sub32 = lax.broadcasted_iota(jnp.int32, (32, 128), 0) % 4
    blk32 = lax.broadcasted_iota(jnp.int32, (32, 128), 1) // 32

    first_rows = (
        lax.broadcasted_iota(jnp.int32, (32, 128), 0) == lax.broadcasted_iota(jnp.int32, (32, 128), 1)
    ).astype(F32).astype(BF16)
    diagonal = [(sub32 == q) & (blk32 == q) for q in range(4)]

    def tap_tiles(l, a, c):
        taps = []
        for b in range(3):
            row = kf[l, pl.ds(9 * a + 3 * b + c, 1), :]
            tiles = []
            for r in range(4):
                low = jnp.broadcast_to(row[:, 256 * r : 256 * r + 128], (8, 128))
                high = jnp.broadcast_to(row[:, 256 * r + 128 : 256 * r + 256], (8, 128))
                z = jnp.where(blk8 == sub % 4, jnp.where(sub < 4, low, high), 0.0)
                z = z + pltpu.roll(z, 64, 1)
                tiles.append(z + pltpu.roll(z, 32, 1))
            taps.append(jnp.concatenate(tiles, axis=0))
        return taps

    def store_blocks(target, l, a, c, taps, step):
        row0 = pl.multiple_of(a * 256, 256)
        for hp in range(8):
            for j in range(2):
                block = jnp.zeros((32, 128), F32)
                for b in range(3):
                    h = hp + step * (b - 1)
                    if h // 4 == j and 0 <= h < 8:
                        block = jnp.where(blk32 == h % 4, taps[b], block)
                rows = pl.ds(pl.multiple_of(row0 + 32 * hp, 32), 32)
                target[l, c, rows, 128 * j : 128 * j + 128] = block.astype(BF16)

    def build(l, forward, backward):
        @pl.loop(0, 3)
        def _(a):
            for c in range(3):
                taps = tap_tiles(l, a, c)
                if forward:
                    store_blocks(fwd_w, l, a, c, taps, -1)
                if backward:
                    stacked = jnp.concatenate([tap for tap in taps for _ in range(4)], axis=0)
                    back = lax.dot_general(
                        first_rows, stacked.astype(BF16), NT, preferred_element_type=F32
                    )
                    store_blocks(
                        bwd_w, l, a, c, [back[:, 128 * b : 128 * b + 128] for b in range(3)], 1
                    )

    def at_rows(s, n):
        start = LAYER * s
        if not isinstance(s, int):
            start = pl.multiple_of(start, LAYER)
        return pl.ds(start, LAYER * n)

    def taps_of(lhs, l, forward):
        weights = fwd_w if forward else bwd_w
        outs = [jnp.dot(lhs, weights[l, c], preferred_element_type=F32) for c in range(3)]
        if forward:
            return outs[1] + from_left(outs[0]) + from_right(outs[2])
        return outs[1] + from_right(outs[0]) + from_left(outs[2])

    def conv(x, l, s, n, forward):
        shifts = (-1, 0, 1) if forward else (1, 0, -1)
        lhs = jnp.concatenate([x[at_rows(s + shift, n), :] for shift in shifts], axis=1)
        return taps_of(lhs, l, forward)

    def conv_ranges(x, l, ranges, forward):
        shifts = (-1, 0, 1) if forward else (1, 0, -1)
        lhs = [
            jnp.concatenate(
                [x[LAYER * (s + shift) : LAYER * (t + shift), :] for s, t in ranges], axis=0
            )
            for shift in shifts
        ]
        return taps_of(jnp.concatenate(lhs, axis=1), l, forward)

    def masked(values, s):
        parts = []
        n = values.shape[0] // LAYER
        for k in range(n):
            piece = values[LAYER * k : LAYER * (k + 1)]
            if s + k < 4:
                piece = jnp.where(d > 0, piece, 0.0)
            elif s + k >= 8:
                piece = jnp.where(d < 3, piece, 0.0)
            parts.append(piece)
        return jnp.concatenate(parts, axis=0)

    def halo_copies(x):
        low = pltpu.make_async_remote_copy(
            src_ref=ext.at[x, pl.ds(LAYER, LAYER), :],
            dst_ref=ext.at[x, pl.ds(5 * LAYER, LAYER), :],
            send_sem=halo_send.at[x, 0],
            recv_sem=halo_recv.at[x, 1],
            device_id=(me, lax.rem(d + 3, 4)),
            device_id_type=MESH,
        )
        high = pltpu.make_async_remote_copy(
            src_ref=ext.at[x, pl.ds(4 * LAYER, LAYER), :],
            dst_ref=ext.at[x, pl.ds(0, LAYER), :],
            send_sem=halo_send.at[x, 1],
            recv_sem=halo_recv.at[x, 0],
            device_id=(me, lax.rem(d + 1, 4)),
            device_id_type=MESH,
        )
        return low, high

    def halo_start(x):
        low, high = halo_copies(x)

        @pl.when(d > 0)
        def _():
            low.start()

        @pl.when(d < 3)
        def _():
            high.start()

    def halo_wait(x):
        low, high = halo_copies(x)

        @pl.when(d > 0)
        def _():
            low.wait_send()
            high.wait_recv()

        @pl.when(d < 3)
        def _():
            high.wait_send()
            low.wait_recv()

    def fill_pieces(slot, values, rows_from):
        n = values.shape[0] // 16
        at = rows_from // 16
        for j in range(2):
            pieces_out[slot, 16 * j + at : 16 * j + at + n] = (
                values[:, 128 * j : 128 * j + 128].astype(BF16).reshape(n, 16, 128)
            )

    def cot_copies():
        low = pltpu.make_async_remote_copy(
            src_ref=wide.at[4, pl.ds(4 * LAYER, 2 * LAYER), :],
            dst_ref=wide.at[4, pl.ds(8 * LAYER, 2 * LAYER), :],
            send_sem=cot_send.at[0],
            recv_sem=cot_recv.at[1],
            device_id=(me, lax.rem(d + 3, 4)),
            device_id_type=MESH,
        )
        high = pltpu.make_async_remote_copy(
            src_ref=wide.at[4, pl.ds(6 * LAYER, 2 * LAYER), :],
            dst_ref=wide.at[4, pl.ds(2 * LAYER, 2 * LAYER), :],
            send_sem=cot_send.at[1],
            recv_sem=cot_recv.at[0],
            device_id=(me, lax.rem(d + 1, 4)),
            device_id_type=MESH,
        )
        return low, high

    def first_copy(slot, source, target, to):
        return pltpu.make_async_remote_copy(
            src_ref=source,
            dst_ref=target,
            send_sem=a2a_send.at[slot, 0],
            recv_sem=a2a_recv.at[slot, 0],
            device_id=(to, d),
            device_id_type=MESH,
        )

    def scatter_start(slot):
        def send(peer):
            first_copy(slot, pieces_out.at[slot, peer - 16], pieces_in.at[slot, me], peer).start()

        peers_of(mid_order, send, True)

        @pl.when(mid)
        def _():
            pieces_in[slot, me] = pieces_out[slot, slot_here]

    def scatter_wait(slot):
        @pl.when(mid)
        def _():
            span = pieces_in.at[slot, pl.ds(0, 31)]
            first_copy(slot, pieces_out.at[slot, pl.ds(0, 31)], span, me).wait_send()
            span = pieces_in.at[slot, pl.ds(0, crops - 1)]
            first_copy(slot, span, span, me).wait_recv()

        @pl.when(jnp.logical_not(mid))
        def _():
            span = pieces_in.at[slot, pl.ds(0, 32)]
            first_copy(slot, pieces_out.at[slot], span, me).wait_send()

    def second_copy(slot, source, target, to):
        return pltpu.make_async_remote_copy(
            src_ref=source,
            dst_ref=target,
            send_sem=a2a_send.at[slot, 1],
            recv_sem=a2a_recv.at[slot, 1],
            device_id=(to, d),
            device_id_type=MESH,
        )

    def gather_start(slot):
        def send(peer):
            second_copy(
                slot, mixed_out.at[slot, peer], mixed_in.at[slot, slot_here], peer
            ).start()

        peers_of(all_order, send, True)
        mixed_in[slot, slot_here] = mixed_out[slot, me]

    def gather_wait(slot):
        @pl.when(mid)
        def _():
            span = mixed_out.at[slot, pl.ds(0, crops - 1)]
            second_copy(slot, span, span, me).wait_send()
            span = mixed_in.at[slot, pl.ds(0, 31)]
            second_copy(slot, span, span, me).wait_recv()

        @pl.when(jnp.logical_not(mid))
        def _():
            span = mixed_in.at[slot]
            second_copy(slot, span, span, me).wait_recv()

    def far_copy(source, target, to):
        return pltpu.make_async_remote_copy(
            src_ref=source,
            dst_ref=target,
            send_sem=far_sems.at[0],
            recv_sem=far_sems.at[1],
            device_id=(to, 3 - d),
            device_id_type=MESH,
        )

    def far_start():
        @pl.when(middle)
        def _():
            def send(peer):
                far_copy(mixed_out.at[0, peer], far_in.at[slot_here], peer).start()

            peers_of(far_order, send, False)

    def far_wait():
        @pl.when(middle)
        def _():
            @pl.when(mid)
            def _():
                far_copy(mixed_out.at[0], mixed_out.at[0], me).wait_send()

            far_copy(far_in, far_in, me).wait_recv()

    def near_copy():
        return pltpu.make_async_remote_copy(
            src_ref=mixed_in.at[0],
            dst_ref=near_in,
            send_sem=near_sems.at[0],
            recv_sem=near_sems.at[1],
            device_id=(me, mate),
            device_id_type=MESH,
        )

    def joined(pieces):
        return jnp.concatenate(
            [pieces[0:16].reshape(ROWS, 128), pieces[16:32].reshape(ROWS, 128)], axis=1
        )

    def kernel_grad(l, x, first, g):
        stacked = jnp.concatenate(
            [from_right(g).astype(BF16), g.astype(BF16), from_left(g).astype(BF16)], axis=1
        )
        totals = []
        for a in range(3):
            u = x[LAYER * (first + a) : LAYER * (first + a) + ROWS, :]
            for c in range(3):
                r = lax.dot_general(
                    u, stacked[:, 256 * c : 256 * c + 256], TN, preferred_element_type=F32
                )

                def at(hp, j):
                    return r[32 * hp : 32 * hp + 32, 128 * j : 128 * j + 128]

                g0 = at(1, 0) + at(5, 1)
                g1 = at(2, 0) + at(6, 1)
                g2 = jnp.where(blk32 >= 2, at(3, 0) + at(7, 1), at(3, 1))
                g3 = jnp.where(blk32 == 3, at(4, 0), at(4, 1) + jnp.where(blk32 < 2, at(0, 0), 0.0))
                total = (
                    g0 + pltpu.roll(g1, 96, 1) + pltpu.roll(g2, 64, 1) + pltpu.roll(g3, 32, 1)
                )
                totals.append(total)
        for k in range(6):
            extra = pltpu.roll(totals[6 + k // 3], 32 * (3 - k % 3), 1)
            packed = jnp.where(blk32 == 3, extra, totals[k])
            part[l, 0, k] = packed[0:16]
            part[l, 1, k] = packed[16:32]
        part[l, 0, 6] = totals[8][0:16]
        part[l, 1, 6] = totals[8][16:32]
        kg_send[l] = part[l, 1 - core].astype(BF16)

    def pair_copy(l):
        return pltpu.make_async_remote_copy(
            src_ref=kg_send.at[l],
            dst_ref=kg_recv.at[l],
            send_sem=pair_sems.at[l, 0],
            recv_sem=pair_sems.at[l, 1],
            device_id=(me, mate),
            device_id_type=MESH,
        )

    def all_copies(l):
        return [
            pltpu.make_async_remote_copy(
                src_ref=kg_pair.at[l],
                dst_ref=kg_all.at[l, k],
                send_sem=all_send.at[l, k],
                recv_sem=all_recv.at[l, k],
                device_id=(me, to),
                device_id_type=MESH,
            )
            for k, to in enumerate((mate, far, far_mate))
        ]

    def pair_sum(l):
        pair_copy(l).wait()
        kg_pair[l] = (part[l, core] + kg_recv[l].astype(F32)).astype(BF16)

    def reduce_pairs(l):
        pair_sum(l)
        for copy in all_copies(l):
            copy.start()

    def reduce_finish(l):
        for copy in all_copies(l):
            copy.wait()
        own = kg_pair[l].astype(F32) + kg_all[l, 1].astype(F32)
        other = kg_all[l, 0].astype(F32) + kg_all[l, 2].astype(F32)
        store_grads(l, own, other)

    def share_copy(l):
        return pltpu.make_async_remote_copy(
            src_ref=kg_sum.at[l - 1],
            dst_ref=kg_shared.at[l - 1],
            send_sem=share_sems.at[l - 1, 0],
            recv_sem=share_sems.at[l - 1, 1],
            device_id=(me, mate),
            device_id_type=MESH,
        )

    def reduce_share(l):
        all_copies(l)[1].wait()
        kg_sum[l - 1] = kg_pair[l].astype(F32) + kg_all[l, 1].astype(F32)
        share_copy(l).start()

    def share_finish(l):
        share_copy(l).wait()
        store_grads(l, kg_sum[l - 1], kg_shared[l - 1])

    def store_grads(l, own, other):
        tiles = [
            jnp.concatenate(
                [
                    jnp.where(core == 0, own[k], other[k]),
                    jnp.where(core == 0, other[k], own[k]),
                ],
                axis=0,
            )
            for k in range(7)
        ]
        terms = tiles[:6]
        for k in (0, 3):
            term = pltpu.roll(tiles[k], 32, 1)
            for m in (1, 2):
                term = jnp.where(blk32 == m, pltpu.roll(tiles[k + m], 32 * (m + 1), 1), term)
            terms.append(term)
        terms.append(tiles[6])
        for a in range(3):
            for c in range(3):
                x = terms[3 * a + c]
                turned = [x] + [pltpu.roll(x, 32 * m, 1) for m in (1, 2, 3)]
                for b in range(3):
                    z = jnp.zeros_like(x)
                    for q in range(4):
                        z = jnp.where(diagonal[q], turned[(q - 2 + b) % 4], z)
                    z = z.reshape(4, 8, 128)
                    z = z + pltpu.roll(z, 7, 1)
                    z = z + pltpu.roll(z, 6, 1)
                    t = 27 * l + 9 * a + 3 * b + c
                    for r in range(4):
                        kg[t, 2 * r : 2 * r + 1, :] = z[r, 0:1, :]
                        kg[t, 2 * r + 1 : 2 * r + 2, :] = z[r, 4:5, :]

    pl.semaphore_wait(barrier, 12)
    halo_start(0)
    tell(0, x_line)
    loads[1].wait()
    for l in range(3):
        kf[l] = kern[l].astype(F32)
    build(0, True, False)
    for load in loads[2:4]:
        load.wait()
    shape = (crops, crops)
    named = partner_row[...] == lax.broadcasted_iota(jnp.int32, shape, 0)
    found = jnp.where(named, lax.broadcasted_iota(jnp.int32, shape, 1), 0)
    inverse_rows[...] = jnp.broadcast_to(
        jnp.minimum(jnp.sum(found, axis=1, keepdims=True, dtype=jnp.int32), crops - 1),
        (crops, 128),
    )
    turn.start()

    xv, g1 = ext.at[0], ext.at[1]
    xb, xs, g3, g2, cotr = (wide.at[k] for k in range(5))


    def first_layer(ranges):
        v = conv_ranges(xv, 0, ranges, True)
        s = logistic(v)
        hidden = v * s
        slope = s * (1.0 + v * (1.0 - s))
        at = 0
        for first, last in ranges:
            n = LAYER * (last - first)
            slope1[LAYER * (first - 1) : LAYER * (last - 1), :] = slope[at : at + n]
            fill_pieces(0, hidden[at : at + n], LAYER * (first - 1))
            at += n

    first_layer(((2, 4),))
    loads[4].wait()
    for layer in range(4):
        cotr[LAYER * (layer + 4) : LAYER * (layer + 5), :] = to_rows(
            cot[0, layer].astype(F32)
        ).astype(BF16)
    pl.semaphore_wait(levels.at[0], 3)
    tell(1, z_line)
    build(1, True, False)
    halo_wait(0)
    first_layer(((1, 2), (4, 5)))

    pl.semaphore_wait(levels.at[1], 3)
    scatter_start(0)
    cot_low, cot_high = cot_copies()

    @pl.when(d > 0)
    def _():
        cot_low.start()

    @pl.when(d < 3)
    def _():
        cot_high.start()

    build(2, True, True)
    scatter_wait(0)

    def mix(slot, other_of):
        def step(n, carry):
            own = pieces_in[slot, n].astype(F32)
            other = pieces_in[slot, other_of(n)].astype(F32)
            mixed_out[slot, n] = (OWN_SHARE * own + PARTNER_SHARE * other).astype(BF16)
            return carry

        lax.fori_loop(0, crops, step, 0, unroll=8)

    @pl.when(mid)
    def _():
        mix(0, lambda n: partner[0, n])
        far_start()
        gather_start(0)

    build(1, False, True)
    build(0, False, True)
    gather_wait(0)
    near_copy().start()
    xb[4 * LAYER : 8 * LAYER, :] = joined(mixed_in[0])

    def far_masked(values):
        parts = []
        for k in range(4):
            piece = values[LAYER * k : LAYER * (k + 1)]
            if k == 0:
                keep = middle | (core == 1)
            elif k == 3:
                keep = middle | (core == 0)
            else:
                keep = middle
            parts.append(jnp.where(keep, piece, 0.0))
        return jnp.concatenate(parts, axis=0)

    def second_layer(s, n, mask):
        v = conv(xb, 1, s, n, True)
        gate = logistic(v)
        second = v * gate
        rows = at_rows(s, n)
        xs[rows, :] = (far_masked(second) if mask else second).astype(BF16)
        slope2[rows, :] = gate * (1.0 + v * (1.0 - gate))

    second_layer(5, 2, False)
    far_wait()

    @pl.when(middle)
    def _():
        xb[pl.ds(pl.multiple_of(512 * core, 512), 256), :] = joined(far_in[...])

    second_layer(1 + 6 * core, 4, True)

    @pl.when(d > 0)
    def _():
        cot_low.wait_send()
        cot_high.wait_recv()

    @pl.when(d < 3)
    def _():
        cot_high.wait_send()
        cot_low.wait_recv()

    def third_layer(s, far_side):
        v = conv(xs, 2, s, 4, True)
        gate = logistic(v)
        slope = gate * (1.0 + v * (1.0 - gate))
        rows = at_rows(s, 4)
        values = cotr[rows, :].astype(F32) * slope
        if far_side:
            parts = []
            for k in range(4):
                piece = values[LAYER * k : LAYER * (k + 1)]
                keep = middle | ((core == 1) if k < 2 else (core == 0))
                parts.append(jnp.where(keep, piece, 0.0))
            values = jnp.concatenate(parts, axis=0)
        g3[rows, :] = values.astype(BF16)

    third_layer(2 + 4 * core, True)
    near_copy().wait()
    xb[pl.ds(pl.multiple_of(512 * (1 - core), 512), 256), :] = joined(near_in[...])
    second_layer(7 - 6 * core, 4, False)
    third_layer(6 - 4 * core, False)

    def back_three(s, n):
        g = conv(g3, 2, s, n, False) * slope2[LAYER * s : LAYER * (s + n), :]
        g2[LAYER * s : LAYER * (s + n), :] = masked(g, s).astype(BF16)

    back_three(3, 3)
    back_three(6, 3)
    fill_pieces(1, conv(g2, 1, 4, 4, False), 0)
    scatter_start(1)
    kernel_grad(2, xs, 3, g3[4 * LAYER : 8 * LAYER, :].astype(F32))
    pair_copy(2).start()
    kernel_grad(1, xb, 3, g2[4 * LAYER : 8 * LAYER, :].astype(F32))
    pair_copy(1).start()
    pair_sum(2)
    all_copies(2)[1].start()
    pair_sum(1)
    all_copies(1)[1].start()
    turn.wait()
    scatter_wait(1)

    @pl.when(mid)
    def _():
        mix(1, lambda n: inverse[n, 0])
        gather_start(1)

    reduce_share(2)
    reduce_share(1)
    share_finish(2)
    share_finish(1)
    gather_wait(1)

    g_one = (joined(mixed_in[1]).astype(F32) * slope1[...]).astype(BF16)
    g1[LAYER : 5 * LAYER, :] = g_one
    halo_start(1)
    kernel_grad(0, xv, 0, g_one.astype(F32))
    pair_copy(0).start()
    g = conv(g1, 0, 2, 2, False)
    gvol[0, 1] = from_rows(g[0:LAYER]).astype(BF16)
    gvol[0, 2] = from_rows(g[LAYER:]).astype(BF16)
    reduce_pairs(0)
    halo_wait(1)
    g = conv_ranges(g1, 0, ((1, 2), (4, 5)), False)
    gvol[0, 0] = from_rows(g[0:LAYER]).astype(BF16)
    gvol[0, 3] = from_rows(g[LAYER:]).astype(BF16)
    reduce_finish(0)


def write_out(gvol, kg, gvol_out, kg_out, sems):
    copies = (
        pltpu.make_async_copy(gvol, gvol_out, sems.at[0]),
        pltpu.make_async_copy(kg, kg_out, sems.at[1]),
    )
    for copy in copies:
        copy.start()
    for copy in copies:
        copy.wait()


def per_device(crops, volume, kernels, partner, cotangent):
    vmem = pl.BlockSpec(memory_space=pltpu.VMEM)
    hbm = pl.BlockSpec(memory_space=pltpu.HBM)
    dma = pltpu.SemaphoreType.DMA
    grad_volume, kg = pl.pallas_call(
        functools.partial(kernel, crops),
        out_shape=(
            jax.ShapeDtypeStruct((1, 4, 8, 2048), BF16),
            jax.ShapeDtypeStruct((81, 8, 128), F32),
        ),
        in_specs=[hbm] * 4,
        out_specs=(vmem, vmem),
        scratch_shapes=[
            pltpu.SMEM((1, crops), jnp.int32),
            pltpu.VMEM((1, crops), jnp.int32),
            pltpu.VMEM((crops, 128), jnp.int32),
            pltpu.SMEM((crops, 128), jnp.int32),
            pltpu.VMEM((1, 4, 8, 2048), BF16),
            pltpu.VMEM((1, 4, 8, 2048), BF16),
            pltpu.VMEM((3, 27, 1024), BF16),
            pltpu.VMEM((3, 27, 1024), F32),
            pltpu.VMEM((3, 3, 768, 256), BF16),
            pltpu.VMEM((3, 3, 768, 256), BF16),
            pltpu.VMEM((2, 384, 256), BF16),
            pltpu.VMEM((5, 768, 256), BF16),
            pltpu.VMEM((256, 256), F32),
            pltpu.VMEM((768, 256), F32),
            pltpu.VMEM((3, 2, 7, 16, 128), F32),
            pltpu.VMEM((2, 32, 16, 128), BF16),
            pltpu.VMEM((2, crops, 16, 128), BF16),
            pltpu.VMEM((2, crops, 16, 128), BF16),
            pltpu.VMEM((2, 32, 16, 128), BF16),
            pltpu.VMEM((32, 16, 128), BF16),
            pltpu.VMEM((32, 16, 128), BF16),
            pltpu.VMEM((3, 7, 16, 128), BF16),
            pltpu.VMEM((3, 7, 16, 128), BF16),
            pltpu.VMEM((3, 7, 16, 128), BF16),
            pltpu.VMEM((3, 3, 7, 16, 128), BF16),
            pltpu.VMEM((2, 7, 16, 128), F32),
            pltpu.VMEM((2, 7, 16, 128), F32),
            dma((2, 2)),
            dma((2, 2)),
            dma((2,)),
            dma((2,)),
            dma((2,)),
            dma((2,)),
            dma((2, 2)),
            dma((2, 2)),
            dma((3, 2)),
            dma((3, 3)),
            dma((3, 3)),
            dma((2, 2)),
            dma((6,)),
            pltpu.SemaphoreType.REGULAR((2,)),
        ],
        compiler_params=pltpu.CompilerParams(
            collective_id=0, has_side_effects=True, vmem_limit_bytes=48 * 1024 * 1024
        ),
    )(*(pltpu.with_memory_space_constraint(x, pltpu.HBM) for x in (partner[None, :], volume, cotangent, kernels)))
    grad_volume, kg = pl.pallas_call(
        write_out,
        out_shape=(
            jax.ShapeDtypeStruct((1, 4, 8, 2048), BF16),
            jax.ShapeDtypeStruct((81, 8, 128), F32),
        ),
        in_specs=[vmem, vmem],
        out_specs=(hbm, hbm),
        scratch_shapes=[dma((2,))],
        compiler_params=pltpu.CompilerParams(vmem_limit_bytes=1024 * 1024),
    )(grad_volume, kg)
    return grad_volume, kg.reshape(1, 3, 27, CH * CH)


def solution(mesh):
    crops = mesh.shape["sample"]
    in_specs = (P("sample", "depth", None, None), P(), P(), P("sample", "depth", None, None))
    out_specs = (P("sample", "depth", None, None), P("sample", None, None, None))
    return jax.shard_map(
        functools.partial(per_device, crops),
        mesh=mesh,
        in_specs=in_specs,
        out_specs=out_specs,
        check_vma=False,
    )
```

```python
import functools

import jax
import jax.numpy as jnp
from jax import lax
from jax.experimental import pallas as pl
from jax.experimental.pallas import tpu as pltpu
from jax.sharding import PartitionSpec as P

CH = 32
OWN_SHARE = 0.6
PARTNER_SHARE = 0.4
MESH = pl.DeviceIdType.MESH
F32 = jnp.float32
BF16 = jnp.bfloat16
ROWS = 256
LANES = 256
LAYER = 64
NT = (((1,), (1,)), ((), ()))
TN = (((0,), (0,)), ((), ()))


def logistic(v):
    return 0.5 * jnp.tanh(0.5 * v) + 0.5


def block_transpose(y):
    sub = lax.broadcasted_iota(jnp.int32, y.shape, 1) % 4
    blk = lax.broadcasted_iota(jnp.int32, y.shape, 2) // 32
    delta = sub - blk
    turned = [y] + [pltpu.roll(y, 128 - 32 * m, 2) for m in (1, 2, 3)]
    out = y
    for m in (1, 2, 3):
        out = jnp.where(delta == m, pltpu.roll(turned[m], m, 1), out)
        out = jnp.where(delta == m - 4, pltpu.roll(turned[m], m + 4, 1), out)
    return out


def to_rows(v):
    even = jnp.stack([v[:, 256 * t : 256 * t + 128] for t in range(8)])
    odd = jnp.stack([v[:, 256 * t + 128 : 256 * t + 256] for t in range(8)])
    first = lax.broadcasted_iota(jnp.int32, even.shape, 1) < 4
    y0 = jnp.where(first, even, pltpu.roll(odd, 4, 1))
    y1 = jnp.where(first, pltpu.roll(even, 4, 1), odd)
    return jnp.concatenate(
        [block_transpose(y0).reshape(64, 128), block_transpose(y1).reshape(64, 128)], axis=1
    )


def from_rows(r):
    y0 = block_transpose(r[:, :128].reshape(8, 8, 128))
    y1 = block_transpose(r[:, 128:].reshape(8, 8, 128))
    first = lax.broadcasted_iota(jnp.int32, y0.shape, 1) < 4
    even = jnp.where(first, y0, pltpu.roll(y1, 4, 1))
    odd = jnp.where(first, pltpu.roll(y0, 4, 1), y1)
    return jnp.concatenate([part[t] for t in range(8) for part in (even, odd)], axis=1)


def width_index(shape):
    return lax.broadcasted_iota(jnp.int32, shape, 0) % LAYER


def from_left(x):
    return jnp.where(width_index(x.shape) == 0, 0.0, pltpu.roll(x, 1, 0))


def from_right(x):
    return jnp.where(width_index(x.shape) == LAYER - 1, 0.0, pltpu.roll(x, x.shape[0] - 1, 0))


def kernel(
    crops,
    partner_hbm,
    vol_hbm,
    cot_hbm,
    kern_hbm,
    gvol,
    kg,
    partner,
    partner_row,
    inverse_rows,
    inverse,
    vol,
    cot,
    kern,
    kf,
    fwd_w,
    bwd_w,
    ext,
    wide,
    slope1,
    slope2,
    part,
    pieces_out,
    pieces_in,
    mixed_out,
    mixed_in,
    far_in,
    near_in,
    kg_send,
    kg_recv,
    kg_pair,
    kg_all,
    kg_sum,
    kg_shared,
    halo_send,
    halo_recv,
    cot_send,
    cot_recv,
    far_sems,
    near_sems,
    a2a_send,
    a2a_recv,
    pair_sems,
    all_send,
    all_recv,
    share_sems,
    load_sems,
    levels,
):
    loads = [
        pltpu.make_async_copy(source, target, load_sems.at[k])
        for k, (source, target) in enumerate(
            (
                (vol_hbm, vol),
                (kern_hbm, kern),
                (partner_hbm, partner_row),
                (partner_hbm, partner),
                (cot_hbm, cot),
            )
        )
    ]
    turn = pltpu.make_async_copy(inverse_rows, inverse, load_sems.at[5])
    for load in loads:
        load.start()
    me = lax.axis_index("sample")
    d = lax.axis_index("depth")
    core = lax.rem(d, 2)
    mate = d + 1 - 2 * core
    far = lax.rem(d + 2, 4)
    far_mate = lax.rem(mate + 2, 4)

    z = me // 16
    mid = (z == 1) | (z == 2)
    middle = (d == 1) | (d == 2)
    mid_count = lax.rem((z + 1) // 2, 2)
    slot_here = me - 16
    ys = [lax.rem(me + 2 + k, 4) for k in range(4)]
    xs_far = me // 4 + 2

    def peers_of(zts, send, skip_own):
        @pl.loop(0, 4)
        def _(k):
            row = 4 * lax.rem(xs_far + k, 4)
            for at, y in enumerate(ys):
                for zt in zts:
                    if skip_own and at == 2:

                        @pl.when((k != 2) | (zt != z))
                        def _():
                            send(16 * zt + row + y)
                    else:
                        send(16 * zt + row + y)

    mids_first = 1 + mid_count * (2 - z) + (1 - mid_count) * (1 - z // 3)
    mid_order = (mids_first, 3 - mids_first)
    edge = 3 * (2 - z)
    all_order = (edge, 3 - edge, 3 - z, z)
    far_order = (z, 3 - z, 3 - edge, edge)

    barrier = pltpu.get_barrier_semaphore()

    x_line = [16 * z + 4 * lax.rem(me // 4 + k, 4) + lax.rem(me, 4) for k in (1, 2, 3)]
    y_line = [4 * (me // 4) + lax.rem(me + k, 4) for k in (1, 2, 3)]
    z_line = [16 * lax.rem(z + k, 4) + lax.rem(me, 16) for k in (2, 1, 3)]
    for k in (2, 3, 1):
        pl.semaphore_signal(
            barrier, inc=1, device_id=(me, lax.rem(d + k, 4)), device_id_type=MESH
        )
    for peer in z_line + x_line + y_line:
        pl.semaphore_signal(barrier, inc=1, device_id=(peer, d), device_id_type=MESH)

    def tell(level, peers):
        for peer in peers:
            pl.semaphore_signal(
                levels.at[level], inc=1, device_id=(peer, d), device_id_type=MESH
            )

    loads[0].wait()
    for layer in range(4):
        ext[0, LAYER * (layer + 1) : LAYER * (layer + 2), :] = to_rows(
            vol[0, layer].astype(F32)
        ).astype(BF16)

    @pl.when(d == 0)
    def _():
        for k in range(2):
            ext[k, 0:LAYER, :] = jnp.zeros((LAYER, LANES), BF16)
        wide[0, 0 : 4 * LAYER, :] = jnp.zeros((4 * LAYER, LANES), BF16)

    @pl.when(d == 3)
    def _():
        for k in range(2):
            ext[k, 5 * LAYER : 6 * LAYER, :] = jnp.zeros((LAYER, LANES), BF16)
        wide[0, 8 * LAYER : 12 * LAYER, :] = jnp.zeros((4 * LAYER, LANES), BF16)


    sub = lax.broadcasted_iota(jnp.int32, (8, 128), 0)
    blk8 = lax.broadcasted_iota(jnp.int32, (8, 128), 1) // 32
    sub32 = lax.broadcasted_iota(jnp.int32, (32, 128), 0) % 4
    blk32 = lax.broadcasted_iota(jnp.int32, (32, 128), 1) // 32

    first_rows = (
        lax.broadcasted_iota(jnp.int32, (32, 128), 0) == lax.broadcasted_iota(jnp.int32, (32, 128), 1)
    ).astype(F32).astype(BF16)
    diagonal = [(sub32 == q) & (blk32 == q) for q in range(4)]

    def tap_tiles(l, a, c):
        taps = []
        for b in range(3):
            row = kf[l, pl.ds(9 * a + 3 * b + c, 1), :]
            tiles = []
            for r in range(4):
                low = jnp.broadcast_to(row[:, 256 * r : 256 * r + 128], (8, 128))
                high = jnp.broadcast_to(row[:, 256 * r + 128 : 256 * r + 256], (8, 128))
                z = jnp.where(blk8 == sub % 4, jnp.where(sub < 4, low, high), 0.0)
                z = z + pltpu.roll(z, 64, 1)
                tiles.append(z + pltpu.roll(z, 32, 1))
            taps.append(jnp.concatenate(tiles, axis=0))
        return taps

    def store_blocks(target, l, a, c, taps, step):
        row0 = pl.multiple_of(a * 256, 256)
        for hp in range(8):
            for j in range(2):
                block = jnp.zeros((32, 128), F32)
                for b in range(3):
                    h = hp + step * (b - 1)
                    if h // 4 == j and 0 <= h < 8:
                        block = jnp.where(blk32 == h % 4, taps[b], block)
                rows = pl.ds(pl.multiple_of(row0 + 32 * hp, 32), 32)
                target[l, c, rows, 128 * j : 128 * j + 128] = block.astype(BF16)

    def build(l, forward, backward):
        @pl.loop(0, 3)
        def _(a):
            for c in range(3):
                taps = tap_tiles(l, a, c)
                if forward:
                    store_blocks(fwd_w, l, a, c, taps, -1)
                if backward:
                    stacked = jnp.concatenate([tap for tap in taps for _ in range(4)], axis=0)
                    back = lax.dot_general(
                        first_rows, stacked.astype(BF16), NT, preferred_element_type=F32
                    )
                    store_blocks(
                        bwd_w, l, a, c, [back[:, 128 * b : 128 * b + 128] for b in range(3)], 1
                    )

    def at_rows(s, n):
        start = LAYER * s
        if not isinstance(s, int):
            start = pl.multiple_of(start, LAYER)
        return pl.ds(start, LAYER * n)

    def taps_of(lhs, l, forward):
        weights = fwd_w if forward else bwd_w
        outs = [jnp.dot(lhs, weights[l, c], preferred_element_type=F32) for c in range(3)]
        if forward:
            return outs[1] + from_left(outs[0]) + from_right(outs[2])
        return outs[1] + from_right(outs[0]) + from_left(outs[2])

    def conv(x, l, s, n, forward):
        shifts = (-1, 0, 1) if forward else (1, 0, -1)
        lhs = jnp.concatenate([x[at_rows(s + shift, n), :] for shift in shifts], axis=1)
        return taps_of(lhs, l, forward)

    def conv_ranges(x, l, ranges, forward):
        shifts = (-1, 0, 1) if forward else (1, 0, -1)
        lhs = [
            jnp.concatenate(
                [x[LAYER * (s + shift) : LAYER * (t + shift), :] for s, t in ranges], axis=0
            )
            for shift in shifts
        ]
        return taps_of(jnp.concatenate(lhs, axis=1), l, forward)

    def masked(values, s):
        parts = []
        n = values.shape[0] // LAYER
        for k in range(n):
            piece = values[LAYER * k : LAYER * (k + 1)]
            if s + k < 4:
                piece = jnp.where(d > 0, piece, 0.0)
            elif s + k >= 8:
                piece = jnp.where(d < 3, piece, 0.0)
            parts.append(piece)
        return jnp.concatenate(parts, axis=0)

    def halo_copies(x):
        low = pltpu.make_async_remote_copy(
            src_ref=ext.at[x, pl.ds(LAYER, LAYER), :],
            dst_ref=ext.at[x, pl.ds(5 * LAYER, LAYER), :],
            send_sem=halo_send.at[x, 0],
            recv_sem=halo_recv.at[x, 1],
            device_id=(me, lax.rem(d + 3, 4)),
            device_id_type=MESH,
        )
        high = pltpu.make_async_remote_copy(
            src_ref=ext.at[x, pl.ds(4 * LAYER, LAYER), :],
            dst_ref=ext.at[x, pl.ds(0, LAYER), :],
            send_sem=halo_send.at[x, 1],
            recv_sem=halo_recv.at[x, 0],
            device_id=(me, lax.rem(d + 1, 4)),
            device_id_type=MESH,
        )
        return low, high

    def halo_start(x):
        low, high = halo_copies(x)

        @pl.when(d > 0)
        def _():
            low.start()

        @pl.when(d < 3)
        def _():
            high.start()

    def halo_wait(x):
        low, high = halo_copies(x)

        @pl.when(d > 0)
        def _():
            low.wait_send()
            high.wait_recv()

        @pl.when(d < 3)
        def _():
            high.wait_send()
            low.wait_recv()

    def fill_pieces(slot, values, rows_from):
        n = values.shape[0] // 16
        at = rows_from // 16
        for j in range(2):
            pieces_out[slot, 16 * j + at : 16 * j + at + n] = (
                values[:, 128 * j : 128 * j + 128].astype(BF16).reshape(n, 16, 128)
            )

    def cot_copies():
        low = pltpu.make_async_remote_copy(
            src_ref=wide.at[4, pl.ds(4 * LAYER, 2 * LAYER), :],
            dst_ref=wide.at[4, pl.ds(8 * LAYER, 2 * LAYER), :],
            send_sem=cot_send.at[0],
            recv_sem=cot_recv.at[1],
            device_id=(me, lax.rem(d + 3, 4)),
            device_id_type=MESH,
        )
        high = pltpu.make_async_remote_copy(
            src_ref=wide.at[4, pl.ds(6 * LAYER, 2 * LAYER), :],
            dst_ref=wide.at[4, pl.ds(2 * LAYER, 2 * LAYER), :],
            send_sem=cot_send.at[1],
            recv_sem=cot_recv.at[0],
            device_id=(me, lax.rem(d + 1, 4)),
            device_id_type=MESH,
        )
        return low, high

    def first_copy(slot, source, target, to):
        return pltpu.make_async_remote_copy(
            src_ref=source,
            dst_ref=target,
            send_sem=a2a_send.at[slot, 0],
            recv_sem=a2a_recv.at[slot, 0],
            device_id=(to, d),
            device_id_type=MESH,
        )

    def scatter_start(slot):
        def send(peer):
            first_copy(slot, pieces_out.at[slot, peer - 16], pieces_in.at[slot, me], peer).start()

        peers_of(mid_order, send, True)

        @pl.when(mid)
        def _():
            pieces_in[slot, me] = pieces_out[slot, slot_here]

    def scatter_wait(slot):
        @pl.when(mid)
        def _():
            span = pieces_in.at[slot, pl.ds(0, 31)]
            first_copy(slot, pieces_out.at[slot, pl.ds(0, 31)], span, me).wait_send()
            span = pieces_in.at[slot, pl.ds(0, crops - 1)]
            first_copy(slot, span, span, me).wait_recv()

        @pl.when(jnp.logical_not(mid))
        def _():
            span = pieces_in.at[slot, pl.ds(0, 32)]
            first_copy(slot, pieces_out.at[slot], span, me).wait_send()

    def second_copy(slot, source, target, to):
        return pltpu.make_async_remote_copy(
            src_ref=source,
            dst_ref=target,
            send_sem=a2a_send.at[slot, 1],
            recv_sem=a2a_recv.at[slot, 1],
            device_id=(to, d),
            device_id_type=MESH,
        )

    def gather_start(slot):
        def send(peer):
            second_copy(
                slot, mixed_out.at[slot, peer], mixed_in.at[slot, slot_here], peer
            ).start()

        peers_of(all_order, send, True)
        mixed_in[slot, slot_here] = mixed_out[slot, me]

    def gather_wait(slot):
        @pl.when(mid)
        def _():
            span = mixed_out.at[slot, pl.ds(0, crops - 1)]
            second_copy(slot, span, span, me).wait_send()
            span = mixed_in.at[slot, pl.ds(0, 31)]
            second_copy(slot, span, span, me).wait_recv()

        @pl.when(jnp.logical_not(mid))
        def _():
            span = mixed_in.at[slot]
            second_copy(slot, span, span, me).wait_recv()

    def far_copy(source, target, to):
        return pltpu.make_async_remote_copy(
            src_ref=source,
            dst_ref=target,
            send_sem=far_sems.at[0],
            recv_sem=far_sems.at[1],
            device_id=(to, 3 - d),
            device_id_type=MESH,
        )

    def far_start():
        @pl.when(middle)
        def _():
            def send(peer):
                far_copy(mixed_out.at[0, peer], far_in.at[slot_here], peer).start()

            peers_of(far_order, send, False)

    def far_wait():
        @pl.when(middle)
        def _():
            @pl.when(mid)
            def _():
                far_copy(mixed_out.at[0], mixed_out.at[0], me).wait_send()

            far_copy(far_in, far_in, me).wait_recv()

    def near_copy():
        return pltpu.make_async_remote_copy(
            src_ref=mixed_in.at[0],
            dst_ref=near_in,
            send_sem=near_sems.at[0],
            recv_sem=near_sems.at[1],
            device_id=(me, mate),
            device_id_type=MESH,
        )

    def joined(pieces):
        return jnp.concatenate(
            [pieces[0:16].reshape(ROWS, 128), pieces[16:32].reshape(ROWS, 128)], axis=1
        )

    def kernel_grad(l, x, first, g):
        stacked = jnp.concatenate(
            [from_right(g).astype(BF16), g.astype(BF16), from_left(g).astype(BF16)], axis=1
        )
        totals = []
        for a in range(3):
            u = x[LAYER * (first + a) : LAYER * (first + a) + ROWS, :]
            for c in range(3):
                r = lax.dot_general(
                    u, stacked[:, 256 * c : 256 * c + 256], TN, preferred_element_type=F32
                )

                def at(hp, j):
                    return r[32 * hp : 32 * hp + 32, 128 * j : 128 * j + 128]

                g0 = at(1, 0) + at(5, 1)
                g1 = at(2, 0) + at(6, 1)
                g2 = jnp.where(blk32 >= 2, at(3, 0) + at(7, 1), at(3, 1))
                g3 = jnp.where(blk32 == 3, at(4, 0), at(4, 1) + jnp.where(blk32 < 2, at(0, 0), 0.0))
                total = (
                    g0 + pltpu.roll(g1, 96, 1) + pltpu.roll(g2, 64, 1) + pltpu.roll(g3, 32, 1)
                )
                totals.append(total)
        for k in range(6):
            extra = pltpu.roll(totals[6 + k // 3], 32 * (3 - k % 3), 1)
            packed = jnp.where(blk32 == 3, extra, totals[k])
            part[l, 0, k] = packed[0:16]
            part[l, 1, k] = packed[16:32]
        part[l, 0, 6] = totals[8][0:16]
        part[l, 1, 6] = totals[8][16:32]
        kg_send[l] = part[l, 1 - core].astype(BF16)

    def pair_copy(l):
        return pltpu.make_async_remote_copy(
            src_ref=kg_send.at[l],
            dst_ref=kg_recv.at[l],
            send_sem=pair_sems.at[l, 0],
            recv_sem=pair_sems.at[l, 1],
            device_id=(me, mate),
            device_id_type=MESH,
        )

    def all_copies(l):
        return [
            pltpu.make_async_remote_copy(
                src_ref=kg_pair.at[l],
                dst_ref=kg_all.at[l, k],
                send_sem=all_send.at[l, k],
                recv_sem=all_recv.at[l, k],
                device_id=(me, to),
                device_id_type=MESH,
            )
            for k, to in enumerate((mate, far, far_mate))
        ]

    def pair_sum(l):
        pair_copy(l).wait()
        kg_pair[l] = (part[l, core] + kg_recv[l].astype(F32)).astype(BF16)

    def reduce_pairs(l):
        pair_sum(l)
        for copy in all_copies(l):
            copy.start()

    def reduce_finish(l):
        for copy in all_copies(l):
            copy.wait()
        own = kg_pair[l].astype(F32) + kg_all[l, 1].astype(F32)
        other = kg_all[l, 0].astype(F32) + kg_all[l, 2].astype(F32)
        store_grads(l, own, other)

    def share_copy(l):
        return pltpu.make_async_remote_copy(
            src_ref=kg_sum.at[l - 1],
            dst_ref=kg_shared.at[l - 1],
            send_sem=share_sems.at[l - 1, 0],
            recv_sem=share_sems.at[l - 1, 1],
            device_id=(me, mate),
            device_id_type=MESH,
        )

    def reduce_share(l):
        all_copies(l)[1].wait()
        kg_sum[l - 1] = kg_pair[l].astype(F32) + kg_all[l, 1].astype(F32)
        share_copy(l).start()

    def share_finish(l):
        share_copy(l).wait()
        store_grads(l, kg_sum[l - 1], kg_shared[l - 1])

    def store_grads(l, own, other):
        tiles = [
            jnp.concatenate(
                [
                    jnp.where(core == 0, own[k], other[k]),
                    jnp.where(core == 0, other[k], own[k]),
                ],
                axis=0,
            )
            for k in range(7)
        ]
        terms = tiles[:6]
        for k in (0, 3):
            term = pltpu.roll(tiles[k], 32, 1)
            for m in (1, 2):
                term = jnp.where(blk32 == m, pltpu.roll(tiles[k + m], 32 * (m + 1), 1), term)
            terms.append(term)
        terms.append(tiles[6])
        for a in range(3):
            for c in range(3):
                x = terms[3 * a + c]
                turned = [x] + [pltpu.roll(x, 32 * m, 1) for m in (1, 2, 3)]
                for b in range(3):
                    z = jnp.zeros_like(x)
                    for q in range(4):
                        z = jnp.where(diagonal[q], turned[(q - 2 + b) % 4], z)
                    z = z.reshape(4, 8, 128)
                    z = z + pltpu.roll(z, 7, 1)
                    z = z + pltpu.roll(z, 6, 1)
                    t = 27 * l + 9 * a + 3 * b + c
                    for r in range(4):
                        kg[t, 2 * r : 2 * r + 1, :] = z[r, 0:1, :]
                        kg[t, 2 * r + 1 : 2 * r + 2, :] = z[r, 4:5, :]

    pl.semaphore_wait(barrier, 12)
    halo_start(0)
    tell(0, x_line)
    loads[1].wait()
    for l in range(3):
        kf[l] = kern[l].astype(F32)
    build(0, True, False)
    for load in loads[2:4]:
        load.wait()
    shape = (crops, crops)
    named = partner_row[...] == lax.broadcasted_iota(jnp.int32, shape, 0)
    found = jnp.where(named, lax.broadcasted_iota(jnp.int32, shape, 1), 0)
    inverse_rows[...] = jnp.broadcast_to(
        jnp.minimum(jnp.sum(found, axis=1, keepdims=True, dtype=jnp.int32), crops - 1),
        (crops, 128),
    )
    turn.start()

    xv, g1 = ext.at[0], ext.at[1]
    xb, xs, g3, g2, cotr = (wide.at[k] for k in range(5))


    def first_layer(ranges):
        v = conv_ranges(xv, 0, ranges, True)
        s = logistic(v)
        hidden = v * s
        slope = s * (1.0 + v * (1.0 - s))
        at = 0
        for first, last in ranges:
            n = LAYER * (last - first)
            slope1[LAYER * (first - 1) : LAYER * (last - 1), :] = slope[at : at + n]
            fill_pieces(0, hidden[at : at + n], LAYER * (first - 1))
            at += n

    first_layer(((2, 4),))
    loads[4].wait()
    for layer in range(4):
        cotr[LAYER * (layer + 4) : LAYER * (layer + 5), :] = to_rows(
            cot[0, layer].astype(F32)
        ).astype(BF16)
    cot_low, cot_high = cot_copies()

    @pl.when(d > 0)
    def _():
        cot_low.start()

    @pl.when(d < 3)
    def _():
        cot_high.start()

    pl.semaphore_wait(levels.at[0], 3)
    tell(1, z_line)
    build(1, True, False)
    halo_wait(0)
    first_layer(((1, 2), (4, 5)))

    pl.semaphore_wait(levels.at[1], 3)
    scatter_start(0)
    build(2, True, True)
    scatter_wait(0)

    def mix(slot, other_of):
        def step(n, carry):
            own = pieces_in[slot, n].astype(F32)
            other = pieces_in[slot, other_of(n)].astype(F32)
            mixed_out[slot, n] = (OWN_SHARE * own + PARTNER_SHARE * other).astype(BF16)
            return carry

        lax.fori_loop(0, crops, step, 0, unroll=8)

    @pl.when(mid)
    def _():
        mix(0, lambda n: partner[0, n])
        far_start()
        gather_start(0)

    build(1, False, True)
    build(0, False, True)
    gather_wait(0)
    near_copy().start()
    xb[4 * LAYER : 8 * LAYER, :] = joined(mixed_in[0])

    def far_masked(values):
        parts = []
        for k in range(4):
            piece = values[LAYER * k : LAYER * (k + 1)]
            if k == 0:
                keep = middle | (core == 1)
            elif k == 3:
                keep = middle | (core == 0)
            else:
                keep = middle
            parts.append(jnp.where(keep, piece, 0.0))
        return jnp.concatenate(parts, axis=0)

    def second_layer(s, n, mask):
        v = conv(xb, 1, s, n, True)
        gate = logistic(v)
        second = v * gate
        rows = at_rows(s, n)
        xs[rows, :] = (far_masked(second) if mask else second).astype(BF16)
        slope2[rows, :] = gate * (1.0 + v * (1.0 - gate))

    second_layer(5, 2, False)
    far_wait()

    @pl.when(middle)
    def _():
        xb[pl.ds(pl.multiple_of(512 * core, 512), 256), :] = joined(far_in[...])

    second_layer(1 + 6 * core, 4, True)

    @pl.when(d > 0)
    def _():
        cot_low.wait_send()
        cot_high.wait_recv()

    @pl.when(d < 3)
    def _():
        cot_high.wait_send()
        cot_low.wait_recv()

    def third_layer(s, far_side):
        v = conv(xs, 2, s, 4, True)
        gate = logistic(v)
        slope = gate * (1.0 + v * (1.0 - gate))
        rows = at_rows(s, 4)
        values = cotr[rows, :].astype(F32) * slope
        if far_side:
            parts = []
            for k in range(4):
                piece = values[LAYER * k : LAYER * (k + 1)]
                keep = middle | ((core == 1) if k < 2 else (core == 0))
                parts.append(jnp.where(keep, piece, 0.0))
            values = jnp.concatenate(parts, axis=0)
        g3[rows, :] = values.astype(BF16)

    third_layer(2 + 4 * core, True)
    near_copy().wait()
    xb[pl.ds(pl.multiple_of(512 * (1 - core), 512), 256), :] = joined(near_in[...])
    second_layer(7 - 6 * core, 4, False)
    third_layer(6 - 4 * core, False)

    def back_three(s, n):
        g = conv(g3, 2, s, n, False) * slope2[LAYER * s : LAYER * (s + n), :]
        g2[LAYER * s : LAYER * (s + n), :] = masked(g, s).astype(BF16)

    back_three(3, 3)
    back_three(6, 3)
    fill_pieces(1, conv(g2, 1, 4, 4, False), 0)
    scatter_start(1)
    kernel_grad(2, xs, 3, g3[4 * LAYER : 8 * LAYER, :].astype(F32))
    pair_copy(2).start()
    kernel_grad(1, xb, 3, g2[4 * LAYER : 8 * LAYER, :].astype(F32))
    pair_copy(1).start()
    turn.wait()
    scatter_wait(1)

    @pl.when(mid)
    def _():
        mix(1, lambda n: inverse[n, 0])
        gather_start(1)

    pair_sum(2)
    all_copies(2)[1].start()
    pair_sum(1)
    all_copies(1)[1].start()
    gather_wait(1)

    g_one = (joined(mixed_in[1]).astype(F32) * slope1[...]).astype(BF16)
    g1[LAYER : 5 * LAYER, :] = g_one
    halo_start(1)
    kernel_grad(0, xv, 0, g_one.astype(F32))
    pair_copy(0).start()
    reduce_share(2)
    reduce_share(1)
    g = conv(g1, 0, 2, 2, False)
    gvol[0, 1] = from_rows(g[0:LAYER]).astype(BF16)
    gvol[0, 2] = from_rows(g[LAYER:]).astype(BF16)
    reduce_pairs(0)
    halo_wait(1)
    g = conv_ranges(g1, 0, ((1, 2), (4, 5)), False)
    gvol[0, 0] = from_rows(g[0:LAYER]).astype(BF16)
    gvol[0, 3] = from_rows(g[LAYER:]).astype(BF16)
    share_finish(2)
    share_finish(1)
    reduce_finish(0)


def write_out(gvol, kg, gvol_out, kg_out, sems):
    copies = (
        pltpu.make_async_copy(gvol, gvol_out, sems.at[0]),
        pltpu.make_async_copy(kg, kg_out, sems.at[1]),
    )
    for copy in copies:
        copy.start()
    for copy in copies:
        copy.wait()


def per_device(crops, volume, kernels, partner, cotangent):
    vmem = pl.BlockSpec(memory_space=pltpu.VMEM)
    hbm = pl.BlockSpec(memory_space=pltpu.HBM)
    dma = pltpu.SemaphoreType.DMA
    grad_volume, kg = pl.pallas_call(
        functools.partial(kernel, crops),
        out_shape=(
            jax.ShapeDtypeStruct((1, 4, 8, 2048), BF16),
            jax.ShapeDtypeStruct((81, 8, 128), F32),
        ),
        in_specs=[hbm] * 4,
        out_specs=(vmem, vmem),
        scratch_shapes=[
            pltpu.SMEM((1, crops), jnp.int32),
            pltpu.VMEM((1, crops), jnp.int32),
            pltpu.VMEM((crops, 128), jnp.int32),
            pltpu.SMEM((crops, 128), jnp.int32),
            pltpu.VMEM((1, 4, 8, 2048), BF16),
            pltpu.VMEM((1, 4, 8, 2048), BF16),
            pltpu.VMEM((3, 27, 1024), BF16),
            pltpu.VMEM((3, 27, 1024), F32),
            pltpu.VMEM((3, 3, 768, 256), BF16),
            pltpu.VMEM((3, 3, 768, 256), BF16),
            pltpu.VMEM((2, 384, 256), BF16),
            pltpu.VMEM((5, 768, 256), BF16),
            pltpu.VMEM((256, 256), F32),
            pltpu.VMEM((768, 256), F32),
            pltpu.VMEM((3, 2, 7, 16, 128), F32),
            pltpu.VMEM((2, 32, 16, 128), BF16),
            pltpu.VMEM((2, crops, 16, 128), BF16),
            pltpu.VMEM((2, crops, 16, 128), BF16),
            pltpu.VMEM((2, 32, 16, 128), BF16),
            pltpu.VMEM((32, 16, 128), BF16),
            pltpu.VMEM((32, 16, 128), BF16),
            pltpu.VMEM((3, 7, 16, 128), BF16),
            pltpu.VMEM((3, 7, 16, 128), BF16),
            pltpu.VMEM((3, 7, 16, 128), BF16),
            pltpu.VMEM((3, 3, 7, 16, 128), BF16),
            pltpu.VMEM((2, 7, 16, 128), F32),
            pltpu.VMEM((2, 7, 16, 128), F32),
            dma((2, 2)),
            dma((2, 2)),
            dma((2,)),
            dma((2,)),
            dma((2,)),
            dma((2,)),
            dma((2, 2)),
            dma((2, 2)),
            dma((3, 2)),
            dma((3, 3)),
            dma((3, 3)),
            dma((2, 2)),
            dma((6,)),
            pltpu.SemaphoreType.REGULAR((2,)),
        ],
        compiler_params=pltpu.CompilerParams(
            collective_id=0, has_side_effects=True, vmem_limit_bytes=48 * 1024 * 1024
        ),
    )(*(pltpu.with_memory_space_constraint(x, pltpu.HBM) for x in (partner[None, :], volume, cotangent, kernels)))
    grad_volume, kg = pl.pallas_call(
        write_out,
        out_shape=(
            jax.ShapeDtypeStruct((1, 4, 8, 2048), BF16),
            jax.ShapeDtypeStruct((81, 8, 128), F32),
        ),
        in_specs=[vmem, vmem],
        out_specs=(hbm, hbm),
        scratch_shapes=[dma((2,))],
        compiler_params=pltpu.CompilerParams(vmem_limit_bytes=1024 * 1024),
    )(grad_volume, kg)
    return grad_volume, kg.reshape(1, 3, 27, CH * CH)


def solution(mesh):
    crops = mesh.shape["sample"]
    in_specs = (P("sample", "depth", None, None), P(), P(), P("sample", "depth", None, None))
    out_specs = (P("sample", "depth", None, None), P("sample", None, None, None))
    return jax.shard_map(
        functools.partial(per_device, crops),
        mesh=mesh,
        in_specs=in_specs,
        out_specs=out_specs,
        check_vma=False,
    )
```

```python
import functools

import jax
import jax.numpy as jnp
from jax import lax
from jax.experimental import pallas as pl
from jax.experimental.pallas import tpu as pltpu
from jax.sharding import PartitionSpec as P

CH = 32
OWN_SHARE = 0.6
PARTNER_SHARE = 0.4
MESH = pl.DeviceIdType.MESH
F32 = jnp.float32
BF16 = jnp.bfloat16
ROWS = 256
LANES = 256
LAYER = 64
NT = (((1,), (1,)), ((), ()))
TN = (((0,), (0,)), ((), ()))


def logistic(v):
    return 0.5 * jnp.tanh(0.5 * v) + 0.5


def block_transpose(y):
    sub = lax.broadcasted_iota(jnp.int32, y.shape, 1) % 4
    blk = lax.broadcasted_iota(jnp.int32, y.shape, 2) // 32
    delta = sub - blk
    turned = [y] + [pltpu.roll(y, 128 - 32 * m, 2) for m in (1, 2, 3)]
    out = y
    for m in (1, 2, 3):
        out = jnp.where(delta == m, pltpu.roll(turned[m], m, 1), out)
        out = jnp.where(delta == m - 4, pltpu.roll(turned[m], m + 4, 1), out)
    return out


def to_rows(v):
    even = jnp.stack([v[:, 256 * t : 256 * t + 128] for t in range(8)])
    odd = jnp.stack([v[:, 256 * t + 128 : 256 * t + 256] for t in range(8)])
    first = lax.broadcasted_iota(jnp.int32, even.shape, 1) < 4
    y0 = jnp.where(first, even, pltpu.roll(odd, 4, 1))
    y1 = jnp.where(first, pltpu.roll(even, 4, 1), odd)
    return jnp.concatenate(
        [block_transpose(y0).reshape(64, 128), block_transpose(y1).reshape(64, 128)], axis=1
    )


def from_rows(r):
    y0 = block_transpose(r[:, :128].reshape(8, 8, 128))
    y1 = block_transpose(r[:, 128:].reshape(8, 8, 128))
    first = lax.broadcasted_iota(jnp.int32, y0.shape, 1) < 4
    even = jnp.where(first, y0, pltpu.roll(y1, 4, 1))
    odd = jnp.where(first, pltpu.roll(y0, 4, 1), y1)
    return jnp.concatenate([part[t] for t in range(8) for part in (even, odd)], axis=1)


def width_index(shape):
    return lax.broadcasted_iota(jnp.int32, shape, 0) % LAYER


def from_left(x):
    return jnp.where(width_index(x.shape) == 0, 0.0, pltpu.roll(x, 1, 0))


def from_right(x):
    return jnp.where(width_index(x.shape) == LAYER - 1, 0.0, pltpu.roll(x, x.shape[0] - 1, 0))


def kernel(
    crops,
    partner_hbm,
    vol_hbm,
    cot_hbm,
    kern_hbm,
    gvol,
    kg,
    partner,
    partner_row,
    inverse_rows,
    inverse,
    vol,
    cot,
    kern,
    kf,
    fwd_w,
    bwd_w,
    ext,
    wide,
    slope1,
    slope2,
    part,
    pieces_out,
    pieces_in,
    mixed_out,
    mixed_in,
    far_in,
    near_in,
    kg_send,
    kg_recv,
    kg_pair,
    kg_all,
    kg_sum,
    kg_shared,
    halo_send,
    halo_recv,
    cot_send,
    cot_recv,
    far_sems,
    near_sems,
    a2a_send,
    a2a_recv,
    pair_sems,
    all_send,
    all_recv,
    share_sems,
    load_sems,
    levels,
):
    loads = [
        pltpu.make_async_copy(source, target, load_sems.at[k])
        for k, (source, target) in enumerate(
            (
                (vol_hbm, vol),
                (kern_hbm, kern),
                (partner_hbm, partner_row),
                (partner_hbm, partner),
                (cot_hbm, cot),
            )
        )
    ]
    turn = pltpu.make_async_copy(inverse_rows, inverse, load_sems.at[5])
    for load in loads:
        load.start()
    me = lax.axis_index("sample")
    d = lax.axis_index("depth")
    core = lax.rem(d, 2)
    mate = d + 1 - 2 * core
    far = lax.rem(d + 2, 4)
    far_mate = lax.rem(mate + 2, 4)

    z = me // 16
    mid = (z == 1) | (z == 2)
    middle = (d == 1) | (d == 2)
    mid_count = lax.rem((z + 1) // 2, 2)
    slot_here = me - 16
    ys = [lax.rem(me + 2 + k, 4) for k in range(4)]
    xs_far = me // 4 + 2

    def peers_of(zts, send, skip_own):
        @pl.loop(0, 4)
        def _(k):
            row = 4 * lax.rem(xs_far + k, 4)
            for at, y in enumerate(ys):
                for zt in zts:
                    if skip_own and at == 2:

                        @pl.when((k != 2) | (zt != z))
                        def _():
                            send(16 * zt + row + y)
                    else:
                        send(16 * zt + row + y)

    mids_first = 1 + mid_count * (2 - z) + (1 - mid_count) * (1 - z // 3)
    mid_order = (mids_first, 3 - mids_first)
    edge = 3 * (2 - z)
    all_order = (edge, 3 - edge, 3 - z, z)
    far_order = (z, 3 - z, 3 - edge, edge)

    barrier = pltpu.get_barrier_semaphore()

    x_line = [16 * z + 4 * lax.rem(me // 4 + k, 4) + lax.rem(me, 4) for k in (1, 2, 3)]
    y_line = [4 * (me // 4) + lax.rem(me + k, 4) for k in (1, 2, 3)]
    z_line = [16 * lax.rem(z + k, 4) + lax.rem(me, 16) for k in (2, 1, 3)]
    for k in (2, 3, 1):
        pl.semaphore_signal(
            barrier, inc=1, device_id=(me, lax.rem(d + k, 4)), device_id_type=MESH
        )
    for peer in z_line + x_line + y_line:
        pl.semaphore_signal(barrier, inc=1, device_id=(peer, d), device_id_type=MESH)

    def tell(level, peers):
        for peer in peers:
            pl.semaphore_signal(
                levels.at[level], inc=1, device_id=(peer, d), device_id_type=MESH
            )

    loads[0].wait()
    for layer in range(4):
        ext[0, LAYER * (layer + 1) : LAYER * (layer + 2), :] = to_rows(
            vol[0, layer].astype(F32)
        ).astype(BF16)

    @pl.when(d == 0)
    def _():
        for k in range(2):
            ext[k, 0:LAYER, :] = jnp.zeros((LAYER, LANES), BF16)
        wide[0, 0 : 4 * LAYER, :] = jnp.zeros((4 * LAYER, LANES), BF16)

    @pl.when(d == 3)
    def _():
        for k in range(2):
            ext[k, 5 * LAYER : 6 * LAYER, :] = jnp.zeros((LAYER, LANES), BF16)
        wide[0, 8 * LAYER : 12 * LAYER, :] = jnp.zeros((4 * LAYER, LANES), BF16)


    sub = lax.broadcasted_iota(jnp.int32, (8, 128), 0)
    blk8 = lax.broadcasted_iota(jnp.int32, (8, 128), 1) // 32
    sub32 = lax.broadcasted_iota(jnp.int32, (32, 128), 0) % 4
    blk32 = lax.broadcasted_iota(jnp.int32, (32, 128), 1) // 32

    first_rows = (
        lax.broadcasted_iota(jnp.int32, (32, 128), 0) == lax.broadcasted_iota(jnp.int32, (32, 128), 1)
    ).astype(F32).astype(BF16)
    diagonal = [(sub32 == q) & (blk32 == q) for q in range(4)]

    def tap_tiles(l, a, c):
        taps = []
        for b in range(3):
            row = kf[l, pl.ds(9 * a + 3 * b + c, 1), :]
            tiles = []
            for r in range(4):
                low = jnp.broadcast_to(row[:, 256 * r : 256 * r + 128], (8, 128))
                high = jnp.broadcast_to(row[:, 256 * r + 128 : 256 * r + 256], (8, 128))
                z = jnp.where(blk8 == sub % 4, jnp.where(sub < 4, low, high), 0.0)
                z = z + pltpu.roll(z, 64, 1)
                tiles.append(z + pltpu.roll(z, 32, 1))
            taps.append(jnp.concatenate(tiles, axis=0))
        return taps

    def store_blocks(target, l, a, c, taps, step):
        row0 = pl.multiple_of(a * 256, 256)
        for hp in range(8):
            for j in range(2):
                block = jnp.zeros((32, 128), F32)
                for b in range(3):
                    h = hp + step * (b - 1)
                    if h // 4 == j and 0 <= h < 8:
                        block = jnp.where(blk32 == h % 4, taps[b], block)
                rows = pl.ds(pl.multiple_of(row0 + 32 * hp, 32), 32)
                target[l, c, rows, 128 * j : 128 * j + 128] = block.astype(BF16)

    def build(l, forward, backward):
        @pl.loop(0, 3)
        def _(a):
            for c in range(3):
                taps = tap_tiles(l, a, c)
                if forward:
                    store_blocks(fwd_w, l, a, c, taps, -1)
                if backward:
                    stacked = jnp.concatenate([tap for tap in taps for _ in range(4)], axis=0)
                    back = lax.dot_general(
                        first_rows, stacked.astype(BF16), NT, preferred_element_type=F32
                    )
                    store_blocks(
                        bwd_w, l, a, c, [back[:, 128 * b : 128 * b + 128] for b in range(3)], 1
                    )

    def at_rows(s, n):
        start = LAYER * s
        if not isinstance(s, int):
            start = pl.multiple_of(start, LAYER)
        return pl.ds(start, LAYER * n)

    def taps_of(lhs, l, forward):
        weights = fwd_w if forward else bwd_w
        outs = [jnp.dot(lhs, weights[l, c], preferred_element_type=F32) for c in range(3)]
        if forward:
            return outs[1] + from_left(outs[0]) + from_right(outs[2])
        return outs[1] + from_right(outs[0]) + from_left(outs[2])

    def conv(x, l, s, n, forward):
        shifts = (-1, 0, 1) if forward else (1, 0, -1)
        lhs = jnp.concatenate([x[at_rows(s + shift, n), :] for shift in shifts], axis=1)
        return taps_of(lhs, l, forward)

    def conv_ranges(x, l, ranges, forward):
        shifts = (-1, 0, 1) if forward else (1, 0, -1)
        lhs = [
            jnp.concatenate(
                [x[LAYER * (s + shift) : LAYER * (t + shift), :] for s, t in ranges], axis=0
            )
            for shift in shifts
        ]
        return taps_of(jnp.concatenate(lhs, axis=1), l, forward)

    def masked(values, s):
        parts = []
        n = values.shape[0] // LAYER
        for k in range(n):
            piece = values[LAYER * k : LAYER * (k + 1)]
            if s + k < 4:
                piece = jnp.where(d > 0, piece, 0.0)
            elif s + k >= 8:
                piece = jnp.where(d < 3, piece, 0.0)
            parts.append(piece)
        return jnp.concatenate(parts, axis=0)

    def halo_copies(x):
        low = pltpu.make_async_remote_copy(
            src_ref=ext.at[x, pl.ds(LAYER, LAYER), :],
            dst_ref=ext.at[x, pl.ds(5 * LAYER, LAYER), :],
            send_sem=halo_send.at[x, 0],
            recv_sem=halo_recv.at[x, 1],
            device_id=(me, lax.rem(d + 3, 4)),
            device_id_type=MESH,
        )
        high = pltpu.make_async_remote_copy(
            src_ref=ext.at[x, pl.ds(4 * LAYER, LAYER), :],
            dst_ref=ext.at[x, pl.ds(0, LAYER), :],
            send_sem=halo_send.at[x, 1],
            recv_sem=halo_recv.at[x, 0],
            device_id=(me, lax.rem(d + 1, 4)),
            device_id_type=MESH,
        )
        return low, high

    def halo_start(x):
        low, high = halo_copies(x)

        @pl.when(d > 0)
        def _():
            low.start()

        @pl.when(d < 3)
        def _():
            high.start()

    def halo_wait(x):
        low, high = halo_copies(x)

        @pl.when(d > 0)
        def _():
            low.wait_send()
            high.wait_recv()

        @pl.when(d < 3)
        def _():
            high.wait_send()
            low.wait_recv()

    def fill_pieces(slot, values, rows_from):
        n = values.shape[0] // 16
        at = rows_from // 16
        for j in range(2):
            pieces_out[slot, 16 * j + at : 16 * j + at + n] = (
                values[:, 128 * j : 128 * j + 128].astype(BF16).reshape(n, 16, 128)
            )

    def cot_copies():
        low = pltpu.make_async_remote_copy(
            src_ref=wide.at[4, pl.ds(4 * LAYER, 2 * LAYER), :],
            dst_ref=wide.at[4, pl.ds(8 * LAYER, 2 * LAYER), :],
            send_sem=cot_send.at[0],
            recv_sem=cot_recv.at[1],
            device_id=(me, lax.rem(d + 3, 4)),
            device_id_type=MESH,
        )
        high = pltpu.make_async_remote_copy(
            src_ref=wide.at[4, pl.ds(6 * LAYER, 2 * LAYER), :],
            dst_ref=wide.at[4, pl.ds(2 * LAYER, 2 * LAYER), :],
            send_sem=cot_send.at[1],
            recv_sem=cot_recv.at[0],
            device_id=(me, lax.rem(d + 1, 4)),
            device_id_type=MESH,
        )
        return low, high

    def first_copy(slot, source, target, to):
        return pltpu.make_async_remote_copy(
            src_ref=source,
            dst_ref=target,
            send_sem=a2a_send.at[slot, 0],
            recv_sem=a2a_recv.at[slot, 0],
            device_id=(to, d),
            device_id_type=MESH,
        )

    def scatter_start(slot):
        def send(peer):
            first_copy(slot, pieces_out.at[slot, peer - 16], pieces_in.at[slot, me], peer).start()

        peers_of(mid_order, send, True)

        @pl.when(mid)
        def _():
            pieces_in[slot, me] = pieces_out[slot, slot_here]

    def scatter_wait(slot):
        @pl.when(mid)
        def _():
            span = pieces_in.at[slot, pl.ds(0, 31)]
            first_copy(slot, pieces_out.at[slot, pl.ds(0, 31)], span, me).wait_send()
            span = pieces_in.at[slot, pl.ds(0, crops - 1)]
            first_copy(slot, span, span, me).wait_recv()

        @pl.when(jnp.logical_not(mid))
        def _():
            span = pieces_in.at[slot, pl.ds(0, 32)]
            first_copy(slot, pieces_out.at[slot], span, me).wait_send()

    def second_copy(slot, source, target, to):
        return pltpu.make_async_remote_copy(
            src_ref=source,
            dst_ref=target,
            send_sem=a2a_send.at[slot, 1],
            recv_sem=a2a_recv.at[slot, 1],
            device_id=(to, d),
            device_id_type=MESH,
        )

    def gather_start(slot):
        def send(peer):
            second_copy(
                slot, mixed_out.at[slot, peer], mixed_in.at[slot, slot_here], peer
            ).start()

        peers_of(all_order, send, True)
        mixed_in[slot, slot_here] = mixed_out[slot, me]

    def gather_wait(slot):
        @pl.when(mid)
        def _():
            span = mixed_out.at[slot, pl.ds(0, crops - 1)]
            second_copy(slot, span, span, me).wait_send()
            span = mixed_in.at[slot, pl.ds(0, 31)]
            second_copy(slot, span, span, me).wait_recv()

        @pl.when(jnp.logical_not(mid))
        def _():
            span = mixed_in.at[slot]
            second_copy(slot, span, span, me).wait_recv()

    def far_copy(source, target, to):
        return pltpu.make_async_remote_copy(
            src_ref=source,
            dst_ref=target,
            send_sem=far_sems.at[0],
            recv_sem=far_sems.at[1],
            device_id=(to, 3 - d),
            device_id_type=MESH,
        )

    def far_start():
        @pl.when(middle)
        def _():
            def send(peer):
                far_copy(mixed_out.at[0, peer], far_in.at[slot_here], peer).start()

            peers_of(far_order, send, False)

    def far_wait():
        @pl.when(middle)
        def _():
            @pl.when(mid)
            def _():
                far_copy(mixed_out.at[0], mixed_out.at[0], me).wait_send()

            far_copy(far_in, far_in, me).wait_recv()

    def near_copy():
        return pltpu.make_async_remote_copy(
            src_ref=mixed_in.at[0],
            dst_ref=near_in,
            send_sem=near_sems.at[0],
            recv_sem=near_sems.at[1],
            device_id=(me, mate),
            device_id_type=MESH,
        )

    def joined(pieces):
        return jnp.concatenate(
            [pieces[0:16].reshape(ROWS, 128), pieces[16:32].reshape(ROWS, 128)], axis=1
        )

    def kernel_grad(l, x, first, g):
        stacked = jnp.concatenate(
            [from_right(g).astype(BF16), g.astype(BF16), from_left(g).astype(BF16)], axis=1
        )
        totals = []
        for a in range(3):
            u = x[LAYER * (first + a) : LAYER * (first + a) + ROWS, :]
            for c in range(3):
                r = lax.dot_general(
                    u, stacked[:, 256 * c : 256 * c + 256], TN, preferred_element_type=F32
                )

                def at(hp, j):
                    return r[32 * hp : 32 * hp + 32, 128 * j : 128 * j + 128]

                g0 = at(1, 0) + at(5, 1)
                g1 = at(2, 0) + at(6, 1)
                g2 = jnp.where(blk32 >= 2, at(3, 0) + at(7, 1), at(3, 1))
                g3 = jnp.where(blk32 == 3, at(4, 0), at(4, 1) + jnp.where(blk32 < 2, at(0, 0), 0.0))
                total = (
                    g0 + pltpu.roll(g1, 96, 1) + pltpu.roll(g2, 64, 1) + pltpu.roll(g3, 32, 1)
                )
                totals.append(total)
        for k in range(6):
            extra = pltpu.roll(totals[6 + k // 3], 32 * (3 - k % 3), 1)
            packed = jnp.where(blk32 == 3, extra, totals[k])
            part[l, 0, k] = packed[0:16]
            part[l, 1, k] = packed[16:32]
        part[l, 0, 6] = totals[8][0:16]
        part[l, 1, 6] = totals[8][16:32]
        kg_send[l] = part[l, 1 - core].astype(BF16)

    def pair_copy(l):
        return pltpu.make_async_remote_copy(
            src_ref=kg_send.at[l],
            dst_ref=kg_recv.at[l],
            send_sem=pair_sems.at[l, 0],
            recv_sem=pair_sems.at[l, 1],
            device_id=(me, mate),
            device_id_type=MESH,
        )

    def all_copies(l):
        return [
            pltpu.make_async_remote_copy(
                src_ref=kg_pair.at[l],
                dst_ref=kg_all.at[l, k],
                send_sem=all_send.at[l, k],
                recv_sem=all_recv.at[l, k],
                device_id=(me, to),
                device_id_type=MESH,
            )
            for k, to in enumerate((mate, far, far_mate))
        ]

    def pair_sum(l):
        pair_copy(l).wait()
        kg_pair[l] = (part[l, core] + kg_recv[l].astype(F32)).astype(BF16)

    def reduce_pairs(l):
        pair_sum(l)
        for copy in all_copies(l):
            copy.start()

    def reduce_finish(l):
        for copy in all_copies(l):
            copy.wait()
        own = kg_pair[l].astype(F32) + kg_all[l, 1].astype(F32)
        other = kg_all[l, 0].astype(F32) + kg_all[l, 2].astype(F32)
        store_grads(l, own, other)

    def share_copy(l):
        return pltpu.make_async_remote_copy(
            src_ref=kg_sum.at[l - 1],
            dst_ref=kg_shared.at[l - 1],
            send_sem=share_sems.at[l - 1, 0],
            recv_sem=share_sems.at[l - 1, 1],
            device_id=(me, mate),
            device_id_type=MESH,
        )

    def reduce_share(l):
        all_copies(l)[1].wait()
        kg_sum[l - 1] = kg_pair[l].astype(F32) + kg_all[l, 1].astype(F32)
        share_copy(l).start()

    def share_finish(l):
        share_copy(l).wait()
        store_grads(l, kg_sum[l - 1], kg_shared[l - 1])

    def store_grads(l, own, other):
        tiles = [
            jnp.concatenate(
                [
                    jnp.where(core == 0, own[k], other[k]),
                    jnp.where(core == 0, other[k], own[k]),
                ],
                axis=0,
            )
            for k in range(7)
        ]
        terms = tiles[:6]
        for k in (0, 3):
            term = pltpu.roll(tiles[k], 32, 1)
            for m in (1, 2):
                term = jnp.where(blk32 == m, pltpu.roll(tiles[k + m], 32 * (m + 1), 1), term)
            terms.append(term)
        terms.append(tiles[6])
        for a in range(3):
            for c in range(3):
                x = terms[3 * a + c]
                turned = [x] + [pltpu.roll(x, 32 * m, 1) for m in (1, 2, 3)]
                for b in range(3):
                    z = jnp.zeros_like(x)
                    for q in range(4):
                        z = jnp.where(diagonal[q], turned[(q - 2 + b) % 4], z)
                    z = z.reshape(4, 8, 128)
                    z = z + pltpu.roll(z, 7, 1)
                    z = z + pltpu.roll(z, 6, 1)
                    t = 27 * l + 9 * a + 3 * b + c
                    for r in range(4):
                        kg[t, 2 * r : 2 * r + 1, :] = z[r, 0:1, :]
                        kg[t, 2 * r + 1 : 2 * r + 2, :] = z[r, 4:5, :]

    pl.semaphore_wait(barrier, 12)
    halo_start(0)
    tell(0, x_line)
    loads[1].wait()
    for l in range(3):
        kf[l] = kern[l].astype(F32)
    build(0, True, False)
    for load in loads[2:4]:
        load.wait()
    shape = (crops, crops)
    named = partner_row[...] == lax.broadcasted_iota(jnp.int32, shape, 0)
    found = jnp.where(named, lax.broadcasted_iota(jnp.int32, shape, 1), 0)
    inverse_rows[...] = jnp.broadcast_to(
        jnp.minimum(jnp.sum(found, axis=1, keepdims=True, dtype=jnp.int32), crops - 1),
        (crops, 128),
    )
    turn.start()

    xv, g1 = ext.at[0], ext.at[1]
    xb, xs, g3, g2, cotr = (wide.at[k] for k in range(5))


    def first_layer(ranges):
        v = conv_ranges(xv, 0, ranges, True)
        s = logistic(v)
        hidden = v * s
        slope = s * (1.0 + v * (1.0 - s))
        at = 0
        for first, last in ranges:
            n = LAYER * (last - first)
            slope1[LAYER * (first - 1) : LAYER * (last - 1), :] = slope[at : at + n]
            fill_pieces(0, hidden[at : at + n], LAYER * (first - 1))
            at += n

    first_layer(((2, 4),))
    loads[4].wait()
    for layer in range(4):
        cotr[LAYER * (layer + 4) : LAYER * (layer + 5), :] = to_rows(
            cot[0, layer].astype(F32)
        ).astype(BF16)
    cot_low, cot_high = cot_copies()

    @pl.when(d > 0)
    def _():
        cot_low.start()

    @pl.when(d < 3)
    def _():
        cot_high.start()

    pl.semaphore_wait(levels.at[0], 3)
    tell(1, z_line)
    build(1, True, False)
    halo_wait(0)
    first_layer(((1, 2), (4, 5)))

    pl.semaphore_wait(levels.at[1], 3)
    scatter_start(0)
    build(2, True, True)
    scatter_wait(0)

    def mix(slot, other_of):
        def step(n, carry):
            own = pieces_in[slot, n].astype(F32)
            other = pieces_in[slot, other_of(n)].astype(F32)
            mixed_out[slot, n] = (OWN_SHARE * own + PARTNER_SHARE * other).astype(BF16)
            return carry

        lax.fori_loop(0, crops, step, 0, unroll=8)

    @pl.when(mid)
    def _():
        mix(0, lambda n: partner[0, n])
        far_start()
        gather_start(0)

    build(1, False, True)
    build(0, False, True)
    gather_wait(0)
    near_copy().start()
    xb[4 * LAYER : 8 * LAYER, :] = joined(mixed_in[0])

    upper = d // 2

    def near_store():
        near_copy().wait()
        xb[pl.ds(pl.multiple_of(512 * (1 - core), 512), 256), :] = joined(near_in[...])

    def far_masked(values):
        parts = []
        for k in range(4):
            piece = values[LAYER * k : LAYER * (k + 1)]
            if k == 0:
                keep = middle | (upper == 1)
            elif k == 3:
                keep = middle | (upper == 0)
            else:
                keep = middle
            parts.append(jnp.where(keep, piece, 0.0))
        return jnp.concatenate(parts, axis=0)

    def second_layer(s, n, mask):
        v = conv(xb, 1, s, n, True)
        gate = logistic(v)
        second = v * gate
        rows = at_rows(s, n)
        xs[rows, :] = (far_masked(second) if mask else second).astype(BF16)
        slope2[rows, :] = gate * (1.0 + v * (1.0 - gate))

    second_layer(5, 2, False)

    @pl.when(middle)
    def _():
        near_store()

    second_layer(1 + 6 * upper, 4, True)

    @pl.when(d > 0)
    def _():
        cot_low.wait_send()
        cot_high.wait_recv()

    @pl.when(d < 3)
    def _():
        cot_high.wait_send()
        cot_low.wait_recv()

    def third_layer(s, far_side):
        v = conv(xs, 2, s, 4, True)
        gate = logistic(v)
        slope = gate * (1.0 + v * (1.0 - gate))
        rows = at_rows(s, 4)
        values = cotr[rows, :].astype(F32) * slope
        if far_side:
            parts = []
            for k in range(4):
                piece = values[LAYER * k : LAYER * (k + 1)]
                keep = middle | ((upper == 1) if k < 2 else (upper == 0))
                parts.append(jnp.where(keep, piece, 0.0))
            values = jnp.concatenate(parts, axis=0)
        g3[rows, :] = values.astype(BF16)

    third_layer(2 + 4 * upper, True)
    far_wait()

    @pl.when(middle)
    def _():
        xb[pl.ds(pl.multiple_of(512 * core, 512), 256), :] = joined(far_in[...])

    @pl.when(jnp.logical_not(middle))
    def _():
        near_store()

    second_layer(7 - 6 * upper, 4, False)
    third_layer(6 - 4 * upper, False)

    def back_three(s, n):
        g = conv(g3, 2, s, n, False) * slope2[LAYER * s : LAYER * (s + n), :]
        g2[LAYER * s : LAYER * (s + n), :] = masked(g, s).astype(BF16)

    back_three(3, 3)
    back_three(6, 3)
    fill_pieces(1, conv(g2, 1, 4, 4, False), 0)
    scatter_start(1)
    kernel_grad(2, xs, 3, g3[4 * LAYER : 8 * LAYER, :].astype(F32))
    pair_copy(2).start()
    kernel_grad(1, xb, 3, g2[4 * LAYER : 8 * LAYER, :].astype(F32))
    pair_copy(1).start()
    turn.wait()
    scatter_wait(1)

    @pl.when(mid)
    def _():
        mix(1, lambda n: inverse[n, 0])
        gather_start(1)

    pair_sum(2)
    all_copies(2)[1].start()
    pair_sum(1)
    all_copies(1)[1].start()
    gather_wait(1)

    g_one = (joined(mixed_in[1]).astype(F32) * slope1[...]).astype(BF16)
    g1[LAYER : 5 * LAYER, :] = g_one
    halo_start(1)
    kernel_grad(0, xv, 0, g_one.astype(F32))
    pair_copy(0).start()
    reduce_share(2)
    reduce_share(1)
    g = conv(g1, 0, 2, 2, False)
    gvol[0, 1] = from_rows(g[0:LAYER]).astype(BF16)
    gvol[0, 2] = from_rows(g[LAYER:]).astype(BF16)
    reduce_pairs(0)
    halo_wait(1)
    g = conv_ranges(g1, 0, ((1, 2), (4, 5)), False)
    gvol[0, 0] = from_rows(g[0:LAYER]).astype(BF16)
    gvol[0, 3] = from_rows(g[LAYER:]).astype(BF16)
    share_finish(2)
    share_finish(1)
    reduce_finish(0)


def write_out(gvol, kg, gvol_out, kg_out, sems):
    copies = (
        pltpu.make_async_copy(gvol, gvol_out, sems.at[0]),
        pltpu.make_async_copy(kg, kg_out, sems.at[1]),
    )
    for copy in copies:
        copy.start()
    for copy in copies:
        copy.wait()


def per_device(crops, volume, kernels, partner, cotangent):
    vmem = pl.BlockSpec(memory_space=pltpu.VMEM)
    hbm = pl.BlockSpec(memory_space=pltpu.HBM)
    dma = pltpu.SemaphoreType.DMA
    grad_volume, kg = pl.pallas_call(
        functools.partial(kernel, crops),
        out_shape=(
            jax.ShapeDtypeStruct((1, 4, 8, 2048), BF16),
            jax.ShapeDtypeStruct((81, 8, 128), F32),
        ),
        in_specs=[hbm] * 4,
        out_specs=(vmem, vmem),
        scratch_shapes=[
            pltpu.SMEM((1, crops), jnp.int32),
            pltpu.VMEM((1, crops), jnp.int32),
            pltpu.VMEM((crops, 128), jnp.int32),
            pltpu.SMEM((crops, 128), jnp.int32),
            pltpu.VMEM((1, 4, 8, 2048), BF16),
            pltpu.VMEM((1, 4, 8, 2048), BF16),
            pltpu.VMEM((3, 27, 1024), BF16),
            pltpu.VMEM((3, 27, 1024), F32),
            pltpu.VMEM((3, 3, 768, 256), BF16),
            pltpu.VMEM((3, 3, 768, 256), BF16),
            pltpu.VMEM((2, 384, 256), BF16),
            pltpu.VMEM((5, 768, 256), BF16),
            pltpu.VMEM((256, 256), F32),
            pltpu.VMEM((768, 256), F32),
            pltpu.VMEM((3, 2, 7, 16, 128), F32),
            pltpu.VMEM((2, 32, 16, 128), BF16),
            pltpu.VMEM((2, crops, 16, 128), BF16),
            pltpu.VMEM((2, crops, 16, 128), BF16),
            pltpu.VMEM((2, 32, 16, 128), BF16),
            pltpu.VMEM((32, 16, 128), BF16),
            pltpu.VMEM((32, 16, 128), BF16),
            pltpu.VMEM((3, 7, 16, 128), BF16),
            pltpu.VMEM((3, 7, 16, 128), BF16),
            pltpu.VMEM((3, 7, 16, 128), BF16),
            pltpu.VMEM((3, 3, 7, 16, 128), BF16),
            pltpu.VMEM((2, 7, 16, 128), F32),
            pltpu.VMEM((2, 7, 16, 128), F32),
            dma((2, 2)),
            dma((2, 2)),
            dma((2,)),
            dma((2,)),
            dma((2,)),
            dma((2,)),
            dma((2, 2)),
            dma((2, 2)),
            dma((3, 2)),
            dma((3, 3)),
            dma((3, 3)),
            dma((2, 2)),
            dma((6,)),
            pltpu.SemaphoreType.REGULAR((2,)),
        ],
        compiler_params=pltpu.CompilerParams(
            collective_id=0, has_side_effects=True, vmem_limit_bytes=48 * 1024 * 1024
        ),
    )(*(pltpu.with_memory_space_constraint(x, pltpu.HBM) for x in (partner[None, :], volume, cotangent, kernels)))
    grad_volume, kg = pl.pallas_call(
        write_out,
        out_shape=(
            jax.ShapeDtypeStruct((1, 4, 8, 2048), BF16),
            jax.ShapeDtypeStruct((81, 8, 128), F32),
        ),
        in_specs=[vmem, vmem],
        out_specs=(hbm, hbm),
        scratch_shapes=[dma((2,))],
        compiler_params=pltpu.CompilerParams(vmem_limit_bytes=1024 * 1024),
    )(grad_volume, kg)
    return grad_volume, kg.reshape(1, 3, 27, CH * CH)


def solution(mesh):
    crops = mesh.shape["sample"]
    in_specs = (P("sample", "depth", None, None), P(), P(), P("sample", "depth", None, None))
    out_specs = (P("sample", "depth", None, None), P("sample", None, None, None))
    return jax.shard_map(
        functools.partial(per_device, crops),
        mesh=mesh,
        in_specs=in_specs,
        out_specs=out_specs,
        check_vma=False,
    )
```

```python
import functools

import jax
import jax.numpy as jnp
from jax import lax
from jax.experimental import pallas as pl
from jax.experimental.pallas import tpu as pltpu
from jax.sharding import PartitionSpec as P

CH = 32
OWN_SHARE = 0.6
PARTNER_SHARE = 0.4
MESH = pl.DeviceIdType.MESH
F32 = jnp.float32
BF16 = jnp.bfloat16
ROWS = 256
LANES = 256
LAYER = 64
NT = (((1,), (1,)), ((), ()))
TN = (((0,), (0,)), ((), ()))


def logistic(v):
    return 0.5 * jnp.tanh(0.5 * v) + 0.5


def block_transpose(y):
    sub = lax.broadcasted_iota(jnp.int32, y.shape, 1) % 4
    blk = lax.broadcasted_iota(jnp.int32, y.shape, 2) // 32
    delta = sub - blk
    turned = [y] + [pltpu.roll(y, 128 - 32 * m, 2) for m in (1, 2, 3)]
    out = y
    for m in (1, 2, 3):
        out = jnp.where(delta == m, pltpu.roll(turned[m], m, 1), out)
        out = jnp.where(delta == m - 4, pltpu.roll(turned[m], m + 4, 1), out)
    return out


def to_rows(v):
    even = jnp.stack([v[:, 256 * t : 256 * t + 128] for t in range(8)])
    odd = jnp.stack([v[:, 256 * t + 128 : 256 * t + 256] for t in range(8)])
    first = lax.broadcasted_iota(jnp.int32, even.shape, 1) < 4
    y0 = jnp.where(first, even, pltpu.roll(odd, 4, 1))
    y1 = jnp.where(first, pltpu.roll(even, 4, 1), odd)
    return jnp.concatenate(
        [block_transpose(y0).reshape(64, 128), block_transpose(y1).reshape(64, 128)], axis=1
    )


def from_rows(r):
    y0 = block_transpose(r[:, :128].reshape(8, 8, 128))
    y1 = block_transpose(r[:, 128:].reshape(8, 8, 128))
    first = lax.broadcasted_iota(jnp.int32, y0.shape, 1) < 4
    even = jnp.where(first, y0, pltpu.roll(y1, 4, 1))
    odd = jnp.where(first, pltpu.roll(y0, 4, 1), y1)
    return jnp.concatenate([part[t] for t in range(8) for part in (even, odd)], axis=1)


def width_index(shape):
    return lax.broadcasted_iota(jnp.int32, shape, 0) % LAYER


def from_left(x):
    return jnp.where(width_index(x.shape) == 0, 0.0, pltpu.roll(x, 1, 0))


def from_right(x):
    return jnp.where(width_index(x.shape) == LAYER - 1, 0.0, pltpu.roll(x, x.shape[0] - 1, 0))


def kernel(
    crops,
    partner_hbm,
    vol_hbm,
    cot_hbm,
    kern_hbm,
    gvol,
    kg,
    partner,
    partner_row,
    inverse_rows,
    inverse,
    vol,
    cot,
    kern,
    kf,
    fwd_w,
    bwd_w,
    ext,
    wide,
    slope1,
    slope2,
    part,
    pieces_out,
    pieces_in,
    mixed_out,
    mixed_in,
    far_in,
    near_in,
    kg_send,
    kg_recv,
    kg_pair,
    kg_all,
    kg_sum,
    kg_shared,
    halo_send,
    halo_recv,
    cot_send,
    cot_recv,
    far_sems,
    near_sems,
    a2a_send,
    a2a_recv,
    pair_sems,
    all_send,
    all_recv,
    share_sems,
    load_sems,
    levels,
):
    loads = [
        pltpu.make_async_copy(source, target, load_sems.at[k])
        for k, (source, target) in enumerate(
            (
                (vol_hbm, vol),
                (kern_hbm, kern),
                (partner_hbm, partner_row),
                (partner_hbm, partner),
                (cot_hbm, cot),
            )
        )
    ]
    turn = pltpu.make_async_copy(inverse_rows, inverse, load_sems.at[5])
    for load in loads:
        load.start()
    me = lax.axis_index("sample")
    d = lax.axis_index("depth")
    core = lax.rem(d, 2)
    mate = d + 1 - 2 * core
    far = lax.rem(d + 2, 4)
    far_mate = lax.rem(mate + 2, 4)

    z = me // 16
    mid = (z == 1) | (z == 2)
    middle = (d == 1) | (d == 2)
    mid_count = lax.rem((z + 1) // 2, 2)
    slot_here = me - 16
    ys = [lax.rem(me + 2 + k, 4) for k in range(4)]
    xs_far = me // 4 + 2

    def peers_of(zts, send, skip_own):
        @pl.loop(0, 4)
        def _(k):
            row = 4 * lax.rem(xs_far + k, 4)
            for at, y in enumerate(ys):
                for zt in zts:
                    if skip_own and at == 2:

                        @pl.when((k != 2) | (zt != z))
                        def _():
                            send(16 * zt + row + y)
                    else:
                        send(16 * zt + row + y)

    mids_first = 1 + mid_count * (2 - z) + (1 - mid_count) * (1 - z // 3)
    mid_order = (mids_first, 3 - mids_first)
    edge = 3 * (2 - z)
    all_order = (edge, 3 - edge, 3 - z, z)
    far_order = (z, 3 - z, 3 - edge, edge)

    barrier = pltpu.get_barrier_semaphore()

    x_line = [16 * z + 4 * lax.rem(me // 4 + k, 4) + lax.rem(me, 4) for k in (1, 2, 3)]
    y_line = [4 * (me // 4) + lax.rem(me + k, 4) for k in (1, 2, 3)]
    z_line = [16 * lax.rem(z + k, 4) + lax.rem(me, 16) for k in (2, 1, 3)]
    for k in (2, 3, 1):
        pl.semaphore_signal(
            barrier, inc=1, device_id=(me, lax.rem(d + k, 4)), device_id_type=MESH
        )
    for peer in z_line + x_line + y_line:
        pl.semaphore_signal(barrier, inc=1, device_id=(peer, d), device_id_type=MESH)

    def tell(level, peers):
        for peer in peers:
            pl.semaphore_signal(
                levels.at[level], inc=1, device_id=(peer, d), device_id_type=MESH
            )

    loads[0].wait()
    for layer in range(4):
        ext[0, LAYER * (layer + 1) : LAYER * (layer + 2), :] = to_rows(
            vol[0, layer].astype(F32)
        ).astype(BF16)

    @pl.when(d == 0)
    def _():
        for k in range(2):
            ext[k, 0:LAYER, :] = jnp.zeros((LAYER, LANES), BF16)
        wide[0, 0 : 4 * LAYER, :] = jnp.zeros((4 * LAYER, LANES), BF16)

    @pl.when(d == 3)
    def _():
        for k in range(2):
            ext[k, 5 * LAYER : 6 * LAYER, :] = jnp.zeros((LAYER, LANES), BF16)
        wide[0, 8 * LAYER : 12 * LAYER, :] = jnp.zeros((4 * LAYER, LANES), BF16)


    sub = lax.broadcasted_iota(jnp.int32, (8, 128), 0)
    blk8 = lax.broadcasted_iota(jnp.int32, (8, 128), 1) // 32
    sub32 = lax.broadcasted_iota(jnp.int32, (32, 128), 0) % 4
    blk32 = lax.broadcasted_iota(jnp.int32, (32, 128), 1) // 32

    first_rows = (
        lax.broadcasted_iota(jnp.int32, (32, 128), 0) == lax.broadcasted_iota(jnp.int32, (32, 128), 1)
    ).astype(F32).astype(BF16)
    diagonal = [(sub32 == q) & (blk32 == q) for q in range(4)]

    def tap_tiles(l, a, c):
        taps = []
        for b in range(3):
            row = kf[l, pl.ds(9 * a + 3 * b + c, 1), :]
            tiles = []
            for r in range(4):
                low = jnp.broadcast_to(row[:, 256 * r : 256 * r + 128], (8, 128))
                high = jnp.broadcast_to(row[:, 256 * r + 128 : 256 * r + 256], (8, 128))
                z = jnp.where(blk8 == sub % 4, jnp.where(sub < 4, low, high), 0.0)
                z = z + pltpu.roll(z, 64, 1)
                tiles.append(z + pltpu.roll(z, 32, 1))
            taps.append(jnp.concatenate(tiles, axis=0))
        return taps

    def store_blocks(target, l, a, c, taps, step):
        row0 = pl.multiple_of(a * 256, 256)
        for hp in range(8):
            for j in range(2):
                block = jnp.zeros((32, 128), F32)
                for b in range(3):
                    h = hp + step * (b - 1)
                    if h // 4 == j and 0 <= h < 8:
                        block = jnp.where(blk32 == h % 4, taps[b], block)
                rows = pl.ds(pl.multiple_of(row0 + 32 * hp, 32), 32)
                target[l, c, rows, 128 * j : 128 * j + 128] = block.astype(BF16)

    def build(l, forward, backward):
        @pl.loop(0, 3)
        def _(a):
            for c in range(3):
                taps = tap_tiles(l, a, c)
                if forward:
                    store_blocks(fwd_w, l, a, c, taps, -1)
                if backward:
                    stacked = jnp.concatenate([tap for tap in taps for _ in range(4)], axis=0)
                    back = lax.dot_general(
                        first_rows, stacked.astype(BF16), NT, preferred_element_type=F32
                    )
                    store_blocks(
                        bwd_w, l, a, c, [back[:, 128 * b : 128 * b + 128] for b in range(3)], 1
                    )

    def at_rows(s, n):
        start = LAYER * s
        if not isinstance(s, int):
            start = pl.multiple_of(start, LAYER)
        return pl.ds(start, LAYER * n)

    def taps_of(lhs, l, forward):
        weights = fwd_w if forward else bwd_w
        outs = [jnp.dot(lhs, weights[l, c], preferred_element_type=F32) for c in range(3)]
        if forward:
            return outs[1] + from_left(outs[0]) + from_right(outs[2])
        return outs[1] + from_right(outs[0]) + from_left(outs[2])

    def conv(x, l, s, n, forward):
        shifts = (-1, 0, 1) if forward else (1, 0, -1)
        lhs = jnp.concatenate([x[at_rows(s + shift, n), :] for shift in shifts], axis=1)
        return taps_of(lhs, l, forward)

    def conv_ranges(x, l, ranges, forward):
        shifts = (-1, 0, 1) if forward else (1, 0, -1)
        lhs = [
            jnp.concatenate(
                [x[LAYER * (s + shift) : LAYER * (t + shift), :] for s, t in ranges], axis=0
            )
            for shift in shifts
        ]
        return taps_of(jnp.concatenate(lhs, axis=1), l, forward)

    def masked(values, s):
        parts = []
        n = values.shape[0] // LAYER
        for k in range(n):
            piece = values[LAYER * k : LAYER * (k + 1)]
            if s + k < 4:
                piece = jnp.where(d > 0, piece, 0.0)
            elif s + k >= 8:
                piece = jnp.where(d < 3, piece, 0.0)
            parts.append(piece)
        return jnp.concatenate(parts, axis=0)

    def halo_copies(x):
        low = pltpu.make_async_remote_copy(
            src_ref=ext.at[x, pl.ds(LAYER, LAYER), :],
            dst_ref=ext.at[x, pl.ds(5 * LAYER, LAYER), :],
            send_sem=halo_send.at[x, 0],
            recv_sem=halo_recv.at[x, 1],
            device_id=(me, lax.rem(d + 3, 4)),
            device_id_type=MESH,
        )
        high = pltpu.make_async_remote_copy(
            src_ref=ext.at[x, pl.ds(4 * LAYER, LAYER), :],
            dst_ref=ext.at[x, pl.ds(0, LAYER), :],
            send_sem=halo_send.at[x, 1],
            recv_sem=halo_recv.at[x, 0],
            device_id=(me, lax.rem(d + 1, 4)),
            device_id_type=MESH,
        )
        return low, high

    def halo_start(x):
        low, high = halo_copies(x)

        @pl.when(d > 0)
        def _():
            low.start()

        @pl.when(d < 3)
        def _():
            high.start()

    def halo_wait(x):
        low, high = halo_copies(x)

        @pl.when(d > 0)
        def _():
            low.wait_send()
            high.wait_recv()

        @pl.when(d < 3)
        def _():
            high.wait_send()
            low.wait_recv()

    def fill_pieces(slot, values, rows_from):
        n = values.shape[0] // 16
        at = rows_from // 16
        for j in range(2):
            pieces_out[slot, 16 * j + at : 16 * j + at + n] = (
                values[:, 128 * j : 128 * j + 128].astype(BF16).reshape(n, 16, 128)
            )

    def cot_copies():
        low = pltpu.make_async_remote_copy(
            src_ref=wide.at[4, pl.ds(4 * LAYER, 2 * LAYER), :],
            dst_ref=wide.at[4, pl.ds(8 * LAYER, 2 * LAYER), :],
            send_sem=cot_send.at[0],
            recv_sem=cot_recv.at[1],
            device_id=(me, lax.rem(d + 3, 4)),
            device_id_type=MESH,
        )
        high = pltpu.make_async_remote_copy(
            src_ref=wide.at[4, pl.ds(6 * LAYER, 2 * LAYER), :],
            dst_ref=wide.at[4, pl.ds(2 * LAYER, 2 * LAYER), :],
            send_sem=cot_send.at[1],
            recv_sem=cot_recv.at[0],
            device_id=(me, lax.rem(d + 1, 4)),
            device_id_type=MESH,
        )
        return low, high

    def first_copy(slot, source, target, to):
        return pltpu.make_async_remote_copy(
            src_ref=source,
            dst_ref=target,
            send_sem=a2a_send.at[slot, 0],
            recv_sem=a2a_recv.at[slot, 0],
            device_id=(to, d),
            device_id_type=MESH,
        )

    def scatter_start(slot):
        def send(peer):
            first_copy(slot, pieces_out.at[slot, peer - 16], pieces_in.at[slot, me], peer).start()

        peers_of(mid_order, send, True)

        @pl.when(mid)
        def _():
            pieces_in[slot, me] = pieces_out[slot, slot_here]

    def scatter_wait(slot):
        @pl.when(mid)
        def _():
            span = pieces_in.at[slot, pl.ds(0, 31)]
            first_copy(slot, pieces_out.at[slot, pl.ds(0, 31)], span, me).wait_send()
            span = pieces_in.at[slot, pl.ds(0, crops - 1)]
            first_copy(slot, span, span, me).wait_recv()

        @pl.when(jnp.logical_not(mid))
        def _():
            span = pieces_in.at[slot, pl.ds(0, 32)]
            first_copy(slot, pieces_out.at[slot], span, me).wait_send()

    def second_copy(slot, source, target, to):
        return pltpu.make_async_remote_copy(
            src_ref=source,
            dst_ref=target,
            send_sem=a2a_send.at[slot, 1],
            recv_sem=a2a_recv.at[slot, 1],
            device_id=(to, d),
            device_id_type=MESH,
        )

    def gather_start(slot):
        def send(peer):
            second_copy(
                slot, mixed_out.at[slot, peer], mixed_in.at[slot, slot_here], peer
            ).start()

        peers_of(all_order, send, True)
        mixed_in[slot, slot_here] = mixed_out[slot, me]

    def gather_wait(slot):
        @pl.when(mid)
        def _():
            span = mixed_out.at[slot, pl.ds(0, crops - 1)]
            second_copy(slot, span, span, me).wait_send()
            span = mixed_in.at[slot, pl.ds(0, 31)]
            second_copy(slot, span, span, me).wait_recv()

        @pl.when(jnp.logical_not(mid))
        def _():
            span = mixed_in.at[slot]
            second_copy(slot, span, span, me).wait_recv()

    def far_copy(source, target, to):
        return pltpu.make_async_remote_copy(
            src_ref=source,
            dst_ref=target,
            send_sem=far_sems.at[0],
            recv_sem=far_sems.at[1],
            device_id=(to, 3 - d),
            device_id_type=MESH,
        )

    def far_start():
        @pl.when(middle)
        def _():
            def send(peer):
                far_copy(mixed_out.at[0, peer], far_in.at[slot_here], peer).start()

            peers_of(far_order, send, False)

    def far_wait():
        @pl.when(middle)
        def _():
            @pl.when(mid)
            def _():
                far_copy(mixed_out.at[0], mixed_out.at[0], me).wait_send()

            far_copy(far_in, far_in, me).wait_recv()

    def near_copy():
        return pltpu.make_async_remote_copy(
            src_ref=mixed_in.at[0],
            dst_ref=near_in,
            send_sem=near_sems.at[0],
            recv_sem=near_sems.at[1],
            device_id=(me, mate),
            device_id_type=MESH,
        )

    def joined(pieces):
        return jnp.concatenate(
            [pieces[0:16].reshape(ROWS, 128), pieces[16:32].reshape(ROWS, 128)], axis=1
        )

    def kernel_grad(l, x, first, g):
        stacked = jnp.concatenate(
            [from_right(g).astype(BF16), g.astype(BF16), from_left(g).astype(BF16)], axis=1
        )
        totals = []
        for a in range(3):
            u = x[LAYER * (first + a) : LAYER * (first + a) + ROWS, :]
            for c in range(3):
                r = lax.dot_general(
                    u, stacked[:, 256 * c : 256 * c + 256], TN, preferred_element_type=F32
                )

                def at(hp, j):
                    return r[32 * hp : 32 * hp + 32, 128 * j : 128 * j + 128]

                g0 = at(1, 0) + at(5, 1)
                g1 = at(2, 0) + at(6, 1)
                g2 = jnp.where(blk32 >= 2, at(3, 0) + at(7, 1), at(3, 1))
                g3 = jnp.where(blk32 == 3, at(4, 0), at(4, 1) + jnp.where(blk32 < 2, at(0, 0), 0.0))
                total = (
                    g0 + pltpu.roll(g1, 96, 1) + pltpu.roll(g2, 64, 1) + pltpu.roll(g3, 32, 1)
                )
                totals.append(total)
        for k in range(6):
            extra = pltpu.roll(totals[6 + k // 3], 32 * (3 - k % 3), 1)
            packed = jnp.where(blk32 == 3, extra, totals[k])
            part[l, 0, k] = packed[0:16]
            part[l, 1, k] = packed[16:32]
        part[l, 0, 6] = totals[8][0:16]
        part[l, 1, 6] = totals[8][16:32]
        kg_send[l] = part[l, 1 - core].astype(BF16)

    def pair_copy(l):
        return pltpu.make_async_remote_copy(
            src_ref=kg_send.at[l],
            dst_ref=kg_recv.at[l],
            send_sem=pair_sems.at[l, 0],
            recv_sem=pair_sems.at[l, 1],
            device_id=(me, mate),
            device_id_type=MESH,
        )

    def all_copies(l):
        return [
            pltpu.make_async_remote_copy(
                src_ref=kg_pair.at[l],
                dst_ref=kg_all.at[l, k],
                send_sem=all_send.at[l, k],
                recv_sem=all_recv.at[l, k],
                device_id=(me, to),
                device_id_type=MESH,
            )
            for k, to in enumerate((mate, far, far_mate))
        ]

    def pair_sum(l):
        pair_copy(l).wait()
        kg_pair[l] = (part[l, core] + kg_recv[l].astype(F32)).astype(BF16)

    def reduce_pairs(l):
        pair_sum(l)
        for copy in all_copies(l):
            copy.start()

    def reduce_finish(l):
        for copy in all_copies(l):
            copy.wait()
        own = kg_pair[l].astype(F32) + kg_all[l, 1].astype(F32)
        other = kg_all[l, 0].astype(F32) + kg_all[l, 2].astype(F32)
        store_grads(l, own, other)

    def share_copy(l):
        return pltpu.make_async_remote_copy(
            src_ref=kg_sum.at[l - 1],
            dst_ref=kg_shared.at[l - 1],
            send_sem=share_sems.at[l - 1, 0],
            recv_sem=share_sems.at[l - 1, 1],
            device_id=(me, mate),
            device_id_type=MESH,
        )

    def reduce_share(l):
        all_copies(l)[1].wait()
        kg_sum[l - 1] = kg_pair[l].astype(F32) + kg_all[l, 1].astype(F32)
        share_copy(l).start()

    def share_finish(l):
        share_copy(l).wait()
        store_grads(l, kg_sum[l - 1], kg_shared[l - 1])

    def store_grads(l, own, other):
        tiles = [
            jnp.concatenate(
                [
                    jnp.where(core == 0, own[k], other[k]),
                    jnp.where(core == 0, other[k], own[k]),
                ],
                axis=0,
            )
            for k in range(7)
        ]
        terms = tiles[:6]
        for k in (0, 3):
            term = pltpu.roll(tiles[k], 32, 1)
            for m in (1, 2):
                term = jnp.where(blk32 == m, pltpu.roll(tiles[k + m], 32 * (m + 1), 1), term)
            terms.append(term)
        terms.append(tiles[6])
        for a in range(3):
            for c in range(3):
                x = terms[3 * a + c]
                turned = [x] + [pltpu.roll(x, 32 * m, 1) for m in (1, 2, 3)]
                for b in range(3):
                    z = jnp.zeros_like(x)
                    for q in range(4):
                        z = jnp.where(diagonal[q], turned[(q - 2 + b) % 4], z)
                    z = z.reshape(4, 8, 128)
                    z = z + pltpu.roll(z, 7, 1)
                    z = z + pltpu.roll(z, 6, 1)
                    t = 27 * l + 9 * a + 3 * b + c
                    for r in range(4):
                        kg[t, 2 * r : 2 * r + 1, :] = z[r, 0:1, :]
                        kg[t, 2 * r + 1 : 2 * r + 2, :] = z[r, 4:5, :]

    pl.semaphore_wait(barrier, 12)
    halo_start(0)
    tell(0, x_line)
    loads[1].wait()
    for l in range(3):
        kf[l] = kern[l].astype(F32)
    build(0, True, False)
    for load in loads[2:4]:
        load.wait()
    shape = (crops, crops)
    named = partner_row[...] == lax.broadcasted_iota(jnp.int32, shape, 0)
    found = jnp.where(named, lax.broadcasted_iota(jnp.int32, shape, 1), 0)
    inverse_rows[...] = jnp.broadcast_to(
        jnp.minimum(jnp.sum(found, axis=1, keepdims=True, dtype=jnp.int32), crops - 1),
        (crops, 128),
    )
    turn.start()

    xv, g1 = ext.at[0], ext.at[1]
    xb, xs, g3, g2, cotr = (wide.at[k] for k in range(5))


    def first_layer(ranges):
        v = conv_ranges(xv, 0, ranges, True)
        s = logistic(v)
        hidden = v * s
        slope = s * (1.0 + v * (1.0 - s))
        at = 0
        for first, last in ranges:
            n = LAYER * (last - first)
            slope1[LAYER * (first - 1) : LAYER * (last - 1), :] = slope[at : at + n]
            fill_pieces(0, hidden[at : at + n], LAYER * (first - 1))
            at += n

    first_layer(((2, 4),))
    loads[4].wait()
    for layer in range(4):
        cotr[LAYER * (layer + 4) : LAYER * (layer + 5), :] = to_rows(
            cot[0, layer].astype(F32)
        ).astype(BF16)
    cot_low, cot_high = cot_copies()

    @pl.when(d > 0)
    def _():
        cot_low.start()

    @pl.when(d < 3)
    def _():
        cot_high.start()

    pl.semaphore_wait(levels.at[0], 3)
    tell(1, z_line)
    build(1, True, False)
    halo_wait(0)
    first_layer(((1, 2), (4, 5)))

    pl.semaphore_wait(levels.at[1], 3)
    scatter_start(0)
    build(2, True, True)
    scatter_wait(0)

    def mix(slot, other_of):
        def step(n, carry):
            own = pieces_in[slot, n].astype(F32)
            other = pieces_in[slot, other_of(n)].astype(F32)
            mixed_out[slot, n] = (OWN_SHARE * own + PARTNER_SHARE * other).astype(BF16)
            return carry

        lax.fori_loop(0, crops, step, 0, unroll=8)

    @pl.when(mid)
    def _():
        mix(0, lambda n: partner[0, n])
        gather_start(0)
        far_start()

    build(1, False, True)
    build(0, False, True)
    gather_wait(0)
    near_copy().start()
    xb[4 * LAYER : 8 * LAYER, :] = joined(mixed_in[0])

    upper = d // 2

    def near_store():
        near_copy().wait()
        xb[pl.ds(pl.multiple_of(512 * (1 - core), 512), 256), :] = joined(near_in[...])

    def far_masked(values):
        parts = []
        for k in range(4):
            piece = values[LAYER * k : LAYER * (k + 1)]
            if k == 0:
                keep = middle | (upper == 1)
            elif k == 3:
                keep = middle | (upper == 0)
            else:
                keep = middle
            parts.append(jnp.where(keep, piece, 0.0))
        return jnp.concatenate(parts, axis=0)

    def second_layer(s, n, mask):
        v = conv(xb, 1, s, n, True)
        gate = logistic(v)
        second = v * gate
        rows = at_rows(s, n)
        xs[rows, :] = (far_masked(second) if mask else second).astype(BF16)
        slope2[rows, :] = gate * (1.0 + v * (1.0 - gate))

    second_layer(5, 2, False)

    @pl.when(middle)
    def _():
        near_store()

    second_layer(1 + 6 * upper, 4, True)

    @pl.when(d > 0)
    def _():
        cot_low.wait_send()
        cot_high.wait_recv()

    @pl.when(d < 3)
    def _():
        cot_high.wait_send()
        cot_low.wait_recv()

    def third_layer(s, far_side):
        v = conv(xs, 2, s, 4, True)
        gate = logistic(v)
        slope = gate * (1.0 + v * (1.0 - gate))
        rows = at_rows(s, 4)
        values = cotr[rows, :].astype(F32) * slope
        if far_side:
            parts = []
            for k in range(4):
                piece = values[LAYER * k : LAYER * (k + 1)]
                keep = middle | ((upper == 1) if k < 2 else (upper == 0))
                parts.append(jnp.where(keep, piece, 0.0))
            values = jnp.concatenate(parts, axis=0)
        g3[rows, :] = values.astype(BF16)

    third_layer(2 + 4 * upper, True)
    far_wait()

    @pl.when(middle)
    def _():
        xb[pl.ds(pl.multiple_of(512 * core, 512), 256), :] = joined(far_in[...])

    @pl.when(jnp.logical_not(middle))
    def _():
        near_store()

    second_layer(7 - 6 * upper, 4, False)
    third_layer(6 - 4 * upper, False)

    def back_three(s, n):
        g = conv(g3, 2, s, n, False) * slope2[LAYER * s : LAYER * (s + n), :]
        g2[LAYER * s : LAYER * (s + n), :] = masked(g, s).astype(BF16)

    back_three(3, 3)
    back_three(6, 3)
    fill_pieces(1, conv(g2, 1, 4, 4, False), 0)
    scatter_start(1)
    kernel_grad(2, xs, 3, g3[4 * LAYER : 8 * LAYER, :].astype(F32))
    pair_copy(2).start()
    kernel_grad(1, xb, 3, g2[4 * LAYER : 8 * LAYER, :].astype(F32))
    pair_copy(1).start()
    turn.wait()
    scatter_wait(1)

    @pl.when(mid)
    def _():
        mix(1, lambda n: inverse[n, 0])
        gather_start(1)

    pair_sum(2)
    all_copies(2)[1].start()
    pair_sum(1)
    all_copies(1)[1].start()
    gather_wait(1)

    g_one = (joined(mixed_in[1]).astype(F32) * slope1[...]).astype(BF16)
    g1[LAYER : 5 * LAYER, :] = g_one
    halo_start(1)
    kernel_grad(0, xv, 0, g_one.astype(F32))
    pair_copy(0).start()
    reduce_share(2)
    reduce_share(1)
    g = conv(g1, 0, 2, 2, False)
    gvol[0, 1] = from_rows(g[0:LAYER]).astype(BF16)
    gvol[0, 2] = from_rows(g[LAYER:]).astype(BF16)
    reduce_pairs(0)
    halo_wait(1)
    g = conv_ranges(g1, 0, ((1, 2), (4, 5)), False)
    gvol[0, 0] = from_rows(g[0:LAYER]).astype(BF16)
    gvol[0, 3] = from_rows(g[LAYER:]).astype(BF16)
    share_finish(2)
    share_finish(1)
    reduce_finish(0)


def write_out(gvol, kg, gvol_out, kg_out, sems):
    copies = (
        pltpu.make_async_copy(gvol, gvol_out, sems.at[0]),
        pltpu.make_async_copy(kg, kg_out, sems.at[1]),
    )
    for copy in copies:
        copy.start()
    for copy in copies:
        copy.wait()


def per_device(crops, volume, kernels, partner, cotangent):
    vmem = pl.BlockSpec(memory_space=pltpu.VMEM)
    hbm = pl.BlockSpec(memory_space=pltpu.HBM)
    dma = pltpu.SemaphoreType.DMA
    grad_volume, kg = pl.pallas_call(
        functools.partial(kernel, crops),
        out_shape=(
            jax.ShapeDtypeStruct((1, 4, 8, 2048), BF16),
            jax.ShapeDtypeStruct((81, 8, 128), F32),
        ),
        in_specs=[hbm] * 4,
        out_specs=(vmem, vmem),
        scratch_shapes=[
            pltpu.SMEM((1, crops), jnp.int32),
            pltpu.VMEM((1, crops), jnp.int32),
            pltpu.VMEM((crops, 128), jnp.int32),
            pltpu.SMEM((crops, 128), jnp.int32),
            pltpu.VMEM((1, 4, 8, 2048), BF16),
            pltpu.VMEM((1, 4, 8, 2048), BF16),
            pltpu.VMEM((3, 27, 1024), BF16),
            pltpu.VMEM((3, 27, 1024), F32),
            pltpu.VMEM((3, 3, 768, 256), BF16),
            pltpu.VMEM((3, 3, 768, 256), BF16),
            pltpu.VMEM((2, 384, 256), BF16),
            pltpu.VMEM((5, 768, 256), BF16),
            pltpu.VMEM((256, 256), F32),
            pltpu.VMEM((768, 256), F32),
            pltpu.VMEM((3, 2, 7, 16, 128), F32),
            pltpu.VMEM((2, 32, 16, 128), BF16),
            pltpu.VMEM((2, crops, 16, 128), BF16),
            pltpu.VMEM((2, crops, 16, 128), BF16),
            pltpu.VMEM((2, 32, 16, 128), BF16),
            pltpu.VMEM((32, 16, 128), BF16),
            pltpu.VMEM((32, 16, 128), BF16),
            pltpu.VMEM((3, 7, 16, 128), BF16),
            pltpu.VMEM((3, 7, 16, 128), BF16),
            pltpu.VMEM((3, 7, 16, 128), BF16),
            pltpu.VMEM((3, 3, 7, 16, 128), BF16),
            pltpu.VMEM((2, 7, 16, 128), F32),
            pltpu.VMEM((2, 7, 16, 128), F32),
            dma((2, 2)),
            dma((2, 2)),
            dma((2,)),
            dma((2,)),
            dma((2,)),
            dma((2,)),
            dma((2, 2)),
            dma((2, 2)),
            dma((3, 2)),
            dma((3, 3)),
            dma((3, 3)),
            dma((2, 2)),
            dma((6,)),
            pltpu.SemaphoreType.REGULAR((2,)),
        ],
        compiler_params=pltpu.CompilerParams(
            collective_id=0, has_side_effects=True, vmem_limit_bytes=48 * 1024 * 1024
        ),
    )(*(pltpu.with_memory_space_constraint(x, pltpu.HBM) for x in (partner[None, :], volume, cotangent, kernels)))
    grad_volume, kg = pl.pallas_call(
        write_out,
        out_shape=(
            jax.ShapeDtypeStruct((1, 4, 8, 2048), BF16),
            jax.ShapeDtypeStruct((81, 8, 128), F32),
        ),
        in_specs=[vmem, vmem],
        out_specs=(hbm, hbm),
        scratch_shapes=[dma((2,))],
        compiler_params=pltpu.CompilerParams(vmem_limit_bytes=1024 * 1024),
    )(grad_volume, kg)
    return grad_volume, kg.reshape(1, 3, 27, CH * CH)


def solution(mesh):
    crops = mesh.shape["sample"]
    in_specs = (P("sample", "depth", None, None), P(), P(), P("sample", "depth", None, None))
    out_specs = (P("sample", "depth", None, None), P("sample", None, None, None))
    return jax.shard_map(
        functools.partial(per_device, crops),
        mesh=mesh,
        in_specs=in_specs,
        out_specs=out_specs,
        check_vma=False,
    )
```

```python
import functools

import jax
import jax.numpy as jnp
from jax import lax
from jax.experimental import pallas as pl
from jax.experimental.pallas import tpu as pltpu
from jax.sharding import PartitionSpec as P

CH = 32
OWN_SHARE = 0.6
PARTNER_SHARE = 0.4
MESH = pl.DeviceIdType.MESH
F32 = jnp.float32
BF16 = jnp.bfloat16
ROWS = 256
LANES = 256
LAYER = 64
NT = (((1,), (1,)), ((), ()))
TN = (((0,), (0,)), ((), ()))


def logistic(v):
    return 0.5 * jnp.tanh(0.5 * v) + 0.5


def block_transpose(y):
    sub = lax.broadcasted_iota(jnp.int32, y.shape, 1) % 4
    blk = lax.broadcasted_iota(jnp.int32, y.shape, 2) // 32
    delta = sub - blk
    turned = [y] + [pltpu.roll(y, 128 - 32 * m, 2) for m in (1, 2, 3)]
    out = y
    for m in (1, 2, 3):
        out = jnp.where(delta == m, pltpu.roll(turned[m], m, 1), out)
        out = jnp.where(delta == m - 4, pltpu.roll(turned[m], m + 4, 1), out)
    return out


def to_rows(v):
    even = jnp.stack([v[:, 256 * t : 256 * t + 128] for t in range(8)])
    odd = jnp.stack([v[:, 256 * t + 128 : 256 * t + 256] for t in range(8)])
    first = lax.broadcasted_iota(jnp.int32, even.shape, 1) < 4
    y0 = jnp.where(first, even, pltpu.roll(odd, 4, 1))
    y1 = jnp.where(first, pltpu.roll(even, 4, 1), odd)
    return jnp.concatenate(
        [block_transpose(y0).reshape(64, 128), block_transpose(y1).reshape(64, 128)], axis=1
    )


def from_rows(r):
    y0 = block_transpose(r[:, :128].reshape(8, 8, 128))
    y1 = block_transpose(r[:, 128:].reshape(8, 8, 128))
    first = lax.broadcasted_iota(jnp.int32, y0.shape, 1) < 4
    even = jnp.where(first, y0, pltpu.roll(y1, 4, 1))
    odd = jnp.where(first, pltpu.roll(y0, 4, 1), y1)
    return jnp.concatenate([part[t] for t in range(8) for part in (even, odd)], axis=1)


def width_index(shape):
    return lax.broadcasted_iota(jnp.int32, shape, 0) % LAYER


def from_left(x):
    return jnp.where(width_index(x.shape) == 0, 0.0, pltpu.roll(x, 1, 0))


def from_right(x):
    return jnp.where(width_index(x.shape) == LAYER - 1, 0.0, pltpu.roll(x, x.shape[0] - 1, 0))


def kernel(
    crops,
    partner_hbm,
    vol_hbm,
    cot_hbm,
    kern_hbm,
    gvol,
    kg,
    partner,
    partner_row,
    inverse_rows,
    inverse,
    vol,
    cot,
    kern,
    kf,
    fwd_w,
    bwd_w,
    ext,
    wide,
    slope1,
    slope2,
    part,
    pieces_out,
    pieces_in,
    mixed_out,
    mixed_in,
    far_in,
    near_in,
    kg_send,
    kg_recv,
    kg_pair,
    kg_all,
    kg_sum,
    kg_shared,
    halo_send,
    halo_recv,
    cot_send,
    cot_recv,
    far_sems,
    near_sems,
    a2a_send,
    a2a_recv,
    pair_sems,
    all_send,
    all_recv,
    share_sems,
    load_sems,
    levels,
    turned_xv,
):
    loads = [
        pltpu.make_async_copy(source, target, load_sems.at[k])
        for k, (source, target) in enumerate(
            (
                (vol_hbm, vol),
                (kern_hbm, kern),
                (partner_hbm, partner_row),
                (partner_hbm, partner),
                (cot_hbm, cot),
            )
        )
    ]
    turn = pltpu.make_async_copy(inverse_rows, inverse, load_sems.at[5])
    for load in loads:
        load.start()
    me = lax.axis_index("sample")
    d = lax.axis_index("depth")
    core = lax.rem(d, 2)
    mate = d + 1 - 2 * core
    far = lax.rem(d + 2, 4)
    far_mate = lax.rem(mate + 2, 4)

    z = me // 16
    mid = (z == 1) | (z == 2)
    middle = (d == 1) | (d == 2)
    mid_count = lax.rem((z + 1) // 2, 2)
    slot_here = me - 16
    ys = [lax.rem(me + 2 + k, 4) for k in range(4)]
    xs_far = me // 4 + 2

    def peers_of(zts, send, skip_own):
        @pl.loop(0, 4)
        def _(k):
            row = 4 * lax.rem(xs_far + k, 4)
            for at, y in enumerate(ys):
                for zt in zts:
                    if skip_own and at == 2:

                        @pl.when((k != 2) | (zt != z))
                        def _():
                            send(16 * zt + row + y)
                    else:
                        send(16 * zt + row + y)

    mids_first = 1 + mid_count * (2 - z) + (1 - mid_count) * (1 - z // 3)
    mid_order = (mids_first, 3 - mids_first)
    edge = 3 * (2 - z)
    all_order = (edge, 3 - edge, 3 - z, z)
    far_order = (z, 3 - z, 3 - edge, edge)

    barrier = pltpu.get_barrier_semaphore()

    x_line = [16 * z + 4 * lax.rem(me // 4 + k, 4) + lax.rem(me, 4) for k in (1, 2, 3)]
    y_line = [4 * (me // 4) + lax.rem(me + k, 4) for k in (1, 2, 3)]
    z_line = [16 * lax.rem(z + k, 4) + lax.rem(me, 16) for k in (2, 1, 3)]
    for k in (2, 3, 1):
        pl.semaphore_signal(
            barrier, inc=1, device_id=(me, lax.rem(d + k, 4)), device_id_type=MESH
        )
    for peer in z_line + x_line + y_line:
        pl.semaphore_signal(barrier, inc=1, device_id=(peer, d), device_id_type=MESH)

    def tell(level, peers):
        for peer in peers:
            pl.semaphore_signal(
                levels.at[level], inc=1, device_id=(peer, d), device_id_type=MESH
            )

    loads[0].wait()
    for layer in range(4):
        ext[0, LAYER * (layer + 1) : LAYER * (layer + 2), :] = to_rows(
            vol[0, layer].astype(F32)
        ).astype(BF16)

    @pl.when(d == 0)
    def _():
        for k in range(2):
            ext[k, 0:LAYER, :] = jnp.zeros((LAYER, LANES), BF16)
        wide[0, 0 : 4 * LAYER, :] = jnp.zeros((4 * LAYER, LANES), BF16)

    @pl.when(d == 3)
    def _():
        for k in range(2):
            ext[k, 5 * LAYER : 6 * LAYER, :] = jnp.zeros((LAYER, LANES), BF16)
        wide[0, 8 * LAYER : 12 * LAYER, :] = jnp.zeros((4 * LAYER, LANES), BF16)


    sub = lax.broadcasted_iota(jnp.int32, (8, 128), 0)
    blk8 = lax.broadcasted_iota(jnp.int32, (8, 128), 1) // 32
    sub32 = lax.broadcasted_iota(jnp.int32, (32, 128), 0) % 4
    blk32 = lax.broadcasted_iota(jnp.int32, (32, 128), 1) // 32

    first_rows = (
        lax.broadcasted_iota(jnp.int32, (32, 128), 0) == lax.broadcasted_iota(jnp.int32, (32, 128), 1)
    ).astype(F32).astype(BF16)
    diagonal = [(sub32 == q) & (blk32 == q) for q in range(4)]

    def tap_tiles(l, a, c):
        taps = []
        for b in range(3):
            row = kf[l, pl.ds(9 * a + 3 * b + c, 1), :]
            tiles = []
            for r in range(4):
                low = jnp.broadcast_to(row[:, 256 * r : 256 * r + 128], (8, 128))
                high = jnp.broadcast_to(row[:, 256 * r + 128 : 256 * r + 256], (8, 128))
                z = jnp.where(blk8 == sub % 4, jnp.where(sub < 4, low, high), 0.0)
                z = z + pltpu.roll(z, 64, 1)
                tiles.append(z + pltpu.roll(z, 32, 1))
            taps.append(jnp.concatenate(tiles, axis=0))
        return taps

    def store_blocks(target, l, a, c, taps, step):
        row0 = pl.multiple_of(a * 256, 256)
        for hp in range(8):
            for j in range(2):
                block = jnp.zeros((32, 128), F32)
                for b in range(3):
                    h = hp + step * (b - 1)
                    if h // 4 == j and 0 <= h < 8:
                        block = jnp.where(blk32 == h % 4, taps[b], block)
                rows = pl.ds(pl.multiple_of(row0 + 32 * hp, 32), 32)
                target[l, c, rows, 128 * j : 128 * j + 128] = block.astype(BF16)

    def build(l, forward, backward):
        @pl.loop(0, 3)
        def _(a):
            for c in range(3):
                taps = tap_tiles(l, a, c)
                if forward:
                    store_blocks(fwd_w, l, a, c, taps, -1)
                if backward:
                    stacked = jnp.concatenate([tap for tap in taps for _ in range(4)], axis=0)
                    back = lax.dot_general(
                        first_rows, stacked.astype(BF16), NT, preferred_element_type=F32
                    )
                    store_blocks(
                        bwd_w, l, a, c, [back[:, 128 * b : 128 * b + 128] for b in range(3)], 1
                    )

    def at_rows(s, n):
        start = LAYER * s
        if not isinstance(s, int):
            start = pl.multiple_of(start, LAYER)
        return pl.ds(start, LAYER * n)

    def taps_of(lhs, l, forward):
        weights = fwd_w if forward else bwd_w
        outs = [jnp.dot(lhs, weights[l, c], preferred_element_type=F32) for c in range(3)]
        if forward:
            return outs[1] + from_left(outs[0]) + from_right(outs[2])
        return outs[1] + from_right(outs[0]) + from_left(outs[2])

    def conv(x, l, s, n, forward):
        shifts = (-1, 0, 1) if forward else (1, 0, -1)
        lhs = jnp.concatenate([x[at_rows(s + shift, n), :] for shift in shifts], axis=1)
        return taps_of(lhs, l, forward)

    def conv_ranges(x, l, ranges, forward):
        shifts = (-1, 0, 1) if forward else (1, 0, -1)
        lhs = [
            jnp.concatenate(
                [x[LAYER * (s + shift) : LAYER * (t + shift), :] for s, t in ranges], axis=0
            )
            for shift in shifts
        ]
        return taps_of(jnp.concatenate(lhs, axis=1), l, forward)

    def masked(values, s):
        parts = []
        n = values.shape[0] // LAYER
        for k in range(n):
            piece = values[LAYER * k : LAYER * (k + 1)]
            if s + k < 4:
                piece = jnp.where(d > 0, piece, 0.0)
            elif s + k >= 8:
                piece = jnp.where(d < 3, piece, 0.0)
            parts.append(piece)
        return jnp.concatenate(parts, axis=0)

    def halo_copies(x):
        low = pltpu.make_async_remote_copy(
            src_ref=ext.at[x, pl.ds(LAYER, LAYER), :],
            dst_ref=ext.at[x, pl.ds(5 * LAYER, LAYER), :],
            send_sem=halo_send.at[x, 0],
            recv_sem=halo_recv.at[x, 1],
            device_id=(me, lax.rem(d + 3, 4)),
            device_id_type=MESH,
        )
        high = pltpu.make_async_remote_copy(
            src_ref=ext.at[x, pl.ds(4 * LAYER, LAYER), :],
            dst_ref=ext.at[x, pl.ds(0, LAYER), :],
            send_sem=halo_send.at[x, 1],
            recv_sem=halo_recv.at[x, 0],
            device_id=(me, lax.rem(d + 1, 4)),
            device_id_type=MESH,
        )
        return low, high

    def halo_start(x):
        low, high = halo_copies(x)

        @pl.when(d > 0)
        def _():
            low.start()

        @pl.when(d < 3)
        def _():
            high.start()

    def halo_wait(x):
        low, high = halo_copies(x)

        @pl.when(d > 0)
        def _():
            low.wait_send()
            high.wait_recv()

        @pl.when(d < 3)
        def _():
            high.wait_send()
            low.wait_recv()

    def fill_pieces(slot, values, rows_from):
        n = values.shape[0] // 16
        at = rows_from // 16
        for j in range(2):
            pieces_out[slot, 16 * j + at : 16 * j + at + n] = (
                values[:, 128 * j : 128 * j + 128].astype(BF16).reshape(n, 16, 128)
            )

    def cot_copies():
        low = pltpu.make_async_remote_copy(
            src_ref=wide.at[4, pl.ds(4 * LAYER, 2 * LAYER), :],
            dst_ref=wide.at[4, pl.ds(8 * LAYER, 2 * LAYER), :],
            send_sem=cot_send.at[0],
            recv_sem=cot_recv.at[1],
            device_id=(me, lax.rem(d + 3, 4)),
            device_id_type=MESH,
        )
        high = pltpu.make_async_remote_copy(
            src_ref=wide.at[4, pl.ds(6 * LAYER, 2 * LAYER), :],
            dst_ref=wide.at[4, pl.ds(2 * LAYER, 2 * LAYER), :],
            send_sem=cot_send.at[1],
            recv_sem=cot_recv.at[0],
            device_id=(me, lax.rem(d + 1, 4)),
            device_id_type=MESH,
        )
        return low, high

    def first_copy(slot, source, target, to):
        return pltpu.make_async_remote_copy(
            src_ref=source,
            dst_ref=target,
            send_sem=a2a_send.at[slot, 0],
            recv_sem=a2a_recv.at[slot, 0],
            device_id=(to, d),
            device_id_type=MESH,
        )

    def scatter_start(slot):
        def send(peer):
            first_copy(slot, pieces_out.at[slot, peer - 16], pieces_in.at[slot, me], peer).start()

        peers_of(mid_order, send, True)

        @pl.when(mid)
        def _():
            pieces_in[slot, me] = pieces_out[slot, slot_here]

    def scatter_wait(slot):
        @pl.when(mid)
        def _():
            span = pieces_in.at[slot, pl.ds(0, 31)]
            first_copy(slot, pieces_out.at[slot, pl.ds(0, 31)], span, me).wait_send()
            span = pieces_in.at[slot, pl.ds(0, crops - 1)]
            first_copy(slot, span, span, me).wait_recv()

        @pl.when(jnp.logical_not(mid))
        def _():
            span = pieces_in.at[slot, pl.ds(0, 32)]
            first_copy(slot, pieces_out.at[slot], span, me).wait_send()

    def second_copy(slot, source, target, to):
        return pltpu.make_async_remote_copy(
            src_ref=source,
            dst_ref=target,
            send_sem=a2a_send.at[slot, 1],
            recv_sem=a2a_recv.at[slot, 1],
            device_id=(to, d),
            device_id_type=MESH,
        )

    def gather_start(slot):
        def send(peer):
            second_copy(
                slot, mixed_out.at[slot, peer], mixed_in.at[slot, slot_here], peer
            ).start()

        peers_of(all_order, send, True)
        mixed_in[slot, slot_here] = mixed_out[slot, me]

    def gather_wait(slot):
        @pl.when(mid)
        def _():
            span = mixed_out.at[slot, pl.ds(0, crops - 1)]
            second_copy(slot, span, span, me).wait_send()
            span = mixed_in.at[slot, pl.ds(0, 31)]
            second_copy(slot, span, span, me).wait_recv()

        @pl.when(jnp.logical_not(mid))
        def _():
            span = mixed_in.at[slot]
            second_copy(slot, span, span, me).wait_recv()

    def far_copy(source, target, to):
        return pltpu.make_async_remote_copy(
            src_ref=source,
            dst_ref=target,
            send_sem=far_sems.at[0],
            recv_sem=far_sems.at[1],
            device_id=(to, 3 - d),
            device_id_type=MESH,
        )

    def far_start():
        @pl.when(middle)
        def _():
            def send(peer):
                far_copy(mixed_out.at[0, peer], far_in.at[slot_here], peer).start()

            peers_of(far_order, send, False)

    def far_wait():
        @pl.when(middle)
        def _():
            @pl.when(mid)
            def _():
                far_copy(mixed_out.at[0], mixed_out.at[0], me).wait_send()

            far_copy(far_in, far_in, me).wait_recv()

    def near_copy():
        return pltpu.make_async_remote_copy(
            src_ref=mixed_in.at[0],
            dst_ref=near_in,
            send_sem=near_sems.at[0],
            recv_sem=near_sems.at[1],
            device_id=(me, mate),
            device_id_type=MESH,
        )

    def joined(pieces):
        return jnp.concatenate(
            [pieces[0:16].reshape(ROWS, 128), pieces[16:32].reshape(ROWS, 128)], axis=1
        )

    def kernel_grad(l, x, first, g):
        stacked = jnp.concatenate(
            [from_right(g).astype(BF16), g.astype(BF16), from_left(g).astype(BF16)], axis=1
        )
        totals = []
        for a in range(3):
            u = x[LAYER * (first + a) : LAYER * (first + a) + ROWS, :]
            for c in range(3):
                g_c = stacked[:, 256 * c : 256 * c + 256]
                if l == 0:
                    r = jnp.dot(turned_xv[a], g_c, preferred_element_type=F32)
                else:
                    r = lax.dot_general(u, g_c, TN, preferred_element_type=F32)

                def at(hp, j):
                    return r[32 * hp : 32 * hp + 32, 128 * j : 128 * j + 128]

                g0 = at(1, 0) + at(5, 1)
                g1 = at(2, 0) + at(6, 1)
                g2 = jnp.where(blk32 >= 2, at(3, 0) + at(7, 1), at(3, 1))
                g3 = jnp.where(blk32 == 3, at(4, 0), at(4, 1) + jnp.where(blk32 < 2, at(0, 0), 0.0))
                total = (
                    g0 + pltpu.roll(g1, 96, 1) + pltpu.roll(g2, 64, 1) + pltpu.roll(g3, 32, 1)
                )
                totals.append(total)
        for k in range(6):
            extra = pltpu.roll(totals[6 + k // 3], 32 * (3 - k % 3), 1)
            packed = jnp.where(blk32 == 3, extra, totals[k])
            part[l, 0, k] = packed[0:16]
            part[l, 1, k] = packed[16:32]
        part[l, 0, 6] = totals[8][0:16]
        part[l, 1, 6] = totals[8][16:32]
        kg_send[l] = part[l, 1 - core].astype(BF16)

    def pair_copy(l):
        return pltpu.make_async_remote_copy(
            src_ref=kg_send.at[l],
            dst_ref=kg_recv.at[l],
            send_sem=pair_sems.at[l, 0],
            recv_sem=pair_sems.at[l, 1],
            device_id=(me, mate),
            device_id_type=MESH,
        )

    def all_copies(l):
        return [
            pltpu.make_async_remote_copy(
                src_ref=kg_pair.at[l],
                dst_ref=kg_all.at[l, k],
                send_sem=all_send.at[l, k],
                recv_sem=all_recv.at[l, k],
                device_id=(me, to),
                device_id_type=MESH,
            )
            for k, to in enumerate((mate, far, far_mate))
        ]

    def pair_sum(l):
        pair_copy(l).wait()
        kg_pair[l] = (part[l, core] + kg_recv[l].astype(F32)).astype(BF16)

    def reduce_pairs(l):
        pair_sum(l)
        for copy in all_copies(l):
            copy.start()

    def reduce_finish(l):
        for copy in all_copies(l):
            copy.wait()
        own = kg_pair[l].astype(F32) + kg_all[l, 1].astype(F32)
        other = kg_all[l, 0].astype(F32) + kg_all[l, 2].astype(F32)
        store_grads(l, own, other)

    def share_copy(l):
        return pltpu.make_async_remote_copy(
            src_ref=kg_sum.at[l - 1],
            dst_ref=kg_shared.at[l - 1],
            send_sem=share_sems.at[l - 1, 0],
            recv_sem=share_sems.at[l - 1, 1],
            device_id=(me, mate),
            device_id_type=MESH,
        )

    def reduce_share(l):
        all_copies(l)[1].wait()
        kg_sum[l - 1] = kg_pair[l].astype(F32) + kg_all[l, 1].astype(F32)
        share_copy(l).start()

    def share_finish(l):
        share_copy(l).wait()
        store_grads(l, kg_sum[l - 1], kg_shared[l - 1])

    def store_grads(l, own, other):
        tiles = [
            jnp.concatenate(
                [
                    jnp.where(core == 0, own[k], other[k]),
                    jnp.where(core == 0, other[k], own[k]),
                ],
                axis=0,
            )
            for k in range(7)
        ]
        terms = tiles[:6]
        for k in (0, 3):
            term = pltpu.roll(tiles[k], 32, 1)
            for m in (1, 2):
                term = jnp.where(blk32 == m, pltpu.roll(tiles[k + m], 32 * (m + 1), 1), term)
            terms.append(term)
        terms.append(tiles[6])
        for a in range(3):
            for c in range(3):
                x = terms[3 * a + c]
                turned = [x] + [pltpu.roll(x, 32 * m, 1) for m in (1, 2, 3)]
                for b in range(3):
                    z = jnp.zeros_like(x)
                    for q in range(4):
                        z = jnp.where(diagonal[q], turned[(q - 2 + b) % 4], z)
                    z = z.reshape(4, 8, 128)
                    z = z + pltpu.roll(z, 7, 1)
                    z = z + pltpu.roll(z, 6, 1)
                    t = 27 * l + 9 * a + 3 * b + c
                    for r in range(4):
                        kg[t, 2 * r : 2 * r + 1, :] = z[r, 0:1, :]
                        kg[t, 2 * r + 1 : 2 * r + 2, :] = z[r, 4:5, :]

    pl.semaphore_wait(barrier, 12)
    halo_start(0)
    tell(0, x_line)
    loads[1].wait()
    for l in range(3):
        kf[l] = kern[l].astype(F32)
    build(0, True, False)
    for load in loads[2:4]:
        load.wait()
    shape = (crops, crops)
    named = partner_row[...] == lax.broadcasted_iota(jnp.int32, shape, 0)
    found = jnp.where(named, lax.broadcasted_iota(jnp.int32, shape, 1), 0)
    inverse_rows[...] = jnp.broadcast_to(
        jnp.minimum(jnp.sum(found, axis=1, keepdims=True, dtype=jnp.int32), crops - 1),
        (crops, 128),
    )
    turn.start()

    xv, g1 = ext.at[0], ext.at[1]
    xb, xs, g3, g2, cotr = (wide.at[k] for k in range(5))


    def first_layer(ranges):
        v = conv_ranges(xv, 0, ranges, True)
        s = logistic(v)
        hidden = v * s
        slope = s * (1.0 + v * (1.0 - s))
        at = 0
        for first, last in ranges:
            n = LAYER * (last - first)
            slope1[LAYER * (first - 1) : LAYER * (last - 1), :] = slope[at : at + n]
            fill_pieces(0, hidden[at : at + n], LAYER * (first - 1))
            at += n

    first_layer(((2, 4),))
    loads[4].wait()
    for layer in range(4):
        cotr[LAYER * (layer + 4) : LAYER * (layer + 5), :] = to_rows(
            cot[0, layer].astype(F32)
        ).astype(BF16)
    cot_low, cot_high = cot_copies()

    @pl.when(d > 0)
    def _():
        cot_low.start()

    @pl.when(d < 3)
    def _():
        cot_high.start()

    pl.semaphore_wait(levels.at[0], 3)
    tell(1, z_line)
    build(1, True, False)
    halo_wait(0)
    first_layer(((1, 2), (4, 5)))

    pl.semaphore_wait(levels.at[1], 3)
    scatter_start(0)
    build(2, True, True)
    scatter_wait(0)

    def mix(slot, other_of):
        def step(n, carry):
            own = pieces_in[slot, n].astype(F32)
            other = pieces_in[slot, other_of(n)].astype(F32)
            mixed_out[slot, n] = (OWN_SHARE * own + PARTNER_SHARE * other).astype(BF16)
            return carry

        lax.fori_loop(0, crops, step, 0, unroll=8)

    @pl.when(mid)
    def _():
        mix(0, lambda n: partner[0, n])
        gather_start(0)
        far_start()

    build(1, False, True)
    build(0, False, True)
    for a in range(3):
        turned_xv[a] = xv[LAYER * a : LAYER * a + ROWS, :].astype(F32).T.astype(BF16)
    gather_wait(0)
    near_copy().start()
    xb[4 * LAYER : 8 * LAYER, :] = joined(mixed_in[0])

    upper = d // 2

    def near_store():
        near_copy().wait()
        xb[pl.ds(pl.multiple_of(512 * (1 - core), 512), 256), :] = joined(near_in[...])

    def far_masked(values):
        parts = []
        for k in range(4):
            piece = values[LAYER * k : LAYER * (k + 1)]
            if k == 0:
                keep = middle | (upper == 1)
            elif k == 3:
                keep = middle | (upper == 0)
            else:
                keep = middle
            parts.append(jnp.where(keep, piece, 0.0))
        return jnp.concatenate(parts, axis=0)

    def second_layer(s, n, mask):
        v = conv(xb, 1, s, n, True)
        gate = logistic(v)
        second = v * gate
        rows = at_rows(s, n)
        xs[rows, :] = (far_masked(second) if mask else second).astype(BF16)
        slope2[rows, :] = gate * (1.0 + v * (1.0 - gate))

    second_layer(5, 2, False)

    @pl.when(middle)
    def _():
        near_store()

    second_layer(1 + 6 * upper, 4, True)

    @pl.when(d > 0)
    def _():
        cot_low.wait_send()
        cot_high.wait_recv()

    @pl.when(d < 3)
    def _():
        cot_high.wait_send()
        cot_low.wait_recv()

    def third_layer(s, far_side):
        v = conv(xs, 2, s, 4, True)
        gate = logistic(v)
        slope = gate * (1.0 + v * (1.0 - gate))
        rows = at_rows(s, 4)
        values = cotr[rows, :].astype(F32) * slope
        if far_side:
            parts = []
            for k in range(4):
                piece = values[LAYER * k : LAYER * (k + 1)]
                keep = middle | ((upper == 1) if k < 2 else (upper == 0))
                parts.append(jnp.where(keep, piece, 0.0))
            values = jnp.concatenate(parts, axis=0)
        g3[rows, :] = values.astype(BF16)

    third_layer(2 + 4 * upper, True)
    far_wait()

    @pl.when(middle)
    def _():
        xb[pl.ds(pl.multiple_of(512 * core, 512), 256), :] = joined(far_in[...])

    @pl.when(jnp.logical_not(middle))
    def _():
        near_store()

    second_layer(7 - 6 * upper, 4, False)
    third_layer(6 - 4 * upper, False)

    def back_three(s, n):
        g = conv(g3, 2, s, n, False) * slope2[LAYER * s : LAYER * (s + n), :]
        g2[LAYER * s : LAYER * (s + n), :] = masked(g, s).astype(BF16)

    back_three(3, 3)
    back_three(6, 3)
    fill_pieces(1, conv(g2, 1, 4, 4, False), 0)
    scatter_start(1)
    kernel_grad(2, xs, 3, g3[4 * LAYER : 8 * LAYER, :].astype(F32))
    pair_copy(2).start()
    kernel_grad(1, xb, 3, g2[4 * LAYER : 8 * LAYER, :].astype(F32))
    pair_copy(1).start()
    turn.wait()
    scatter_wait(1)

    @pl.when(mid)
    def _():
        mix(1, lambda n: inverse[n, 0])
        gather_start(1)

    pair_sum(2)
    all_copies(2)[1].start()
    pair_sum(1)
    all_copies(1)[1].start()
    gather_wait(1)

    g_one = (joined(mixed_in[1]).astype(F32) * slope1[...]).astype(BF16)
    g1[LAYER : 5 * LAYER, :] = g_one
    halo_start(1)
    kernel_grad(0, xv, 0, g_one.astype(F32))
    pair_copy(0).start()
    reduce_share(2)
    reduce_share(1)
    g = conv(g1, 0, 2, 2, False)
    gvol[0, 1] = from_rows(g[0:LAYER]).astype(BF16)
    gvol[0, 2] = from_rows(g[LAYER:]).astype(BF16)
    reduce_pairs(0)
    halo_wait(1)
    g = conv_ranges(g1, 0, ((1, 2), (4, 5)), False)
    gvol[0, 0] = from_rows(g[0:LAYER]).astype(BF16)
    gvol[0, 3] = from_rows(g[LAYER:]).astype(BF16)
    share_finish(2)
    share_finish(1)
    reduce_finish(0)


def write_out(gvol, kg, gvol_out, kg_out, sems):
    copies = (
        pltpu.make_async_copy(gvol, gvol_out, sems.at[0]),
        pltpu.make_async_copy(kg, kg_out, sems.at[1]),
    )
    for copy in copies:
        copy.start()
    for copy in copies:
        copy.wait()


def per_device(crops, volume, kernels, partner, cotangent):
    vmem = pl.BlockSpec(memory_space=pltpu.VMEM)
    hbm = pl.BlockSpec(memory_space=pltpu.HBM)
    dma = pltpu.SemaphoreType.DMA
    grad_volume, kg = pl.pallas_call(
        functools.partial(kernel, crops),
        out_shape=(
            jax.ShapeDtypeStruct((1, 4, 8, 2048), BF16),
            jax.ShapeDtypeStruct((81, 8, 128), F32),
        ),
        in_specs=[hbm] * 4,
        out_specs=(vmem, vmem),
        scratch_shapes=[
            pltpu.SMEM((1, crops), jnp.int32),
            pltpu.VMEM((1, crops), jnp.int32),
            pltpu.VMEM((crops, 128), jnp.int32),
            pltpu.SMEM((crops, 128), jnp.int32),
            pltpu.VMEM((1, 4, 8, 2048), BF16),
            pltpu.VMEM((1, 4, 8, 2048), BF16),
            pltpu.VMEM((3, 27, 1024), BF16),
            pltpu.VMEM((3, 27, 1024), F32),
            pltpu.VMEM((3, 3, 768, 256), BF16),
            pltpu.VMEM((3, 3, 768, 256), BF16),
            pltpu.VMEM((2, 384, 256), BF16),
            pltpu.VMEM((5, 768, 256), BF16),
            pltpu.VMEM((256, 256), F32),
            pltpu.VMEM((768, 256), F32),
            pltpu.VMEM((3, 2, 7, 16, 128), F32),
            pltpu.VMEM((2, 32, 16, 128), BF16),
            pltpu.VMEM((2, crops, 16, 128), BF16),
            pltpu.VMEM((2, crops, 16, 128), BF16),
            pltpu.VMEM((2, 32, 16, 128), BF16),
            pltpu.VMEM((32, 16, 128), BF16),
            pltpu.VMEM((32, 16, 128), BF16),
            pltpu.VMEM((3, 7, 16, 128), BF16),
            pltpu.VMEM((3, 7, 16, 128), BF16),
            pltpu.VMEM((3, 7, 16, 128), BF16),
            pltpu.VMEM((3, 3, 7, 16, 128), BF16),
            pltpu.VMEM((2, 7, 16, 128), F32),
            pltpu.VMEM((2, 7, 16, 128), F32),
            dma((2, 2)),
            dma((2, 2)),
            dma((2,)),
            dma((2,)),
            dma((2,)),
            dma((2,)),
            dma((2, 2)),
            dma((2, 2)),
            dma((3, 2)),
            dma((3, 3)),
            dma((3, 3)),
            dma((2, 2)),
            dma((6,)),
            pltpu.SemaphoreType.REGULAR((2,)),
            pltpu.VMEM((3, 256, 256), BF16),
        ],
        compiler_params=pltpu.CompilerParams(
            collective_id=0, has_side_effects=True, vmem_limit_bytes=48 * 1024 * 1024
        ),
    )(*(pltpu.with_memory_space_constraint(x, pltpu.HBM) for x in (partner[None, :], volume, cotangent, kernels)))
    grad_volume, kg = pl.pallas_call(
        write_out,
        out_shape=(
            jax.ShapeDtypeStruct((1, 4, 8, 2048), BF16),
            jax.ShapeDtypeStruct((81, 8, 128), F32),
        ),
        in_specs=[vmem, vmem],
        out_specs=(hbm, hbm),
        scratch_shapes=[dma((2,))],
        compiler_params=pltpu.CompilerParams(vmem_limit_bytes=1024 * 1024),
    )(grad_volume, kg)
    return grad_volume, kg.reshape(1, 3, 27, CH * CH)


def solution(mesh):
    crops = mesh.shape["sample"]
    in_specs = (P("sample", "depth", None, None), P(), P(), P("sample", "depth", None, None))
    out_specs = (P("sample", "depth", None, None), P("sample", None, None, None))
    return jax.shard_map(
        functools.partial(per_device, crops),
        mesh=mesh,
        in_specs=in_specs,
        out_specs=out_specs,
        check_vma=False,
    )
```
